32 devices in a mesh: grp: 2 (over x), tile: 16 (over z, y, core).
Axes of the slice: x: 2, y: 2, z: 4, core: 2. Of those that a mesh axis runs over, the one named last changes fastest.
Arguments:
- mask_params: float32 [64, 64, 128], P(('grp', 'tile')), parts along dimension 0, may hold values from -3 to 3
- target: float32 [64, 64, 128], P(('grp', 'tile')), parts along dimension 0, may hold values from 0 to 1
- weight: float32 [64, 64, 128], P(('grp', 'tile')), parts along dimension 0, may hold values from 0.3 to 3
- kernels: float32 [24, 2, 65, 65], replicated, may hold values from -0.25515518 to 0.25515518
- kernel_weight: float32 [24], replicated, may hold values from 0.05 to 1
- tile_ids: int32 [64], P(('grp', 'tile')), parts along dimension 0, may hold values from -1 to 134, as said below
- tile_links: int32 [64, 2], P(('grp', 'tile')), parts along dimension 0, may hold values from 0 to 1, as said below
Outputs:
- params_out: float32 [64, 64, 128], P(('grp', 'tile')), parts along dimension 0
- resist: float32 [64, 64, 128], P(('grp', 'tile')), parts along dimension 0
The draws below stay inside these ranges and needn't reach their ends.
There are 2 independent parts, one for each index of `grp`. The reference program is written for one: setup_inputs(seed, part) draws one part's arguments, and reference() takes and returns one part's arrays. A program takes and returns all parts, laid end to end along the dimension named above; an argument that names none is the same for every part. Nothing has to cross between parts.
Inputs may be any that keep to these rules, and one draw needn't show every extreme that they name: `tile_ids`: -1 marks an empty slot. Every device holds between 1 and 2 tiles in its first slots and some device holds 2; stripe columns rise strictly in the order of devices and slots, and the last live tile of the stripe holds column 134. `tile_links`: entry 0 is 1 exactly where the stripe column just before the slot's tile holds an active tile (then held by the previous live slot in order), entry 1 likewise for the column just after (the next live slot); both are 0 for empty slots.
All inputs are finite; a program needn't handle non-finite values.
Results may differ from the reference program's by a relative error of at most 0.00011.
Values sent between devices are 32-bit elements; how exact they have to be, the bound alone decides.
No kernel may reach another device: no remote copies, remote signals or barrier semaphores. Data moves between devices by JAX's collectives and lax.ppermute only.
A program may use at most 64 MiB of HBM per device.

```python
import math
import jax
import jax.numpy as jnp
from jax import lax

SX = 128
SY = 64
TD = 2
K = 24
FREQ = 65
ITERS = 2
TILES = 32


def layout_draw(key):
    base = jax.random.fold_in(key, 4111)
    key_list = jax.random.split(base, 6)
    device_total = TILES // TD
    busy_device = jax.random.randint(key_list[0], (device_total,), 0, 4) == 0
    extra_tiles = jax.random.randint(key_list[1], (device_total,), 0, max(TD - 1, 1))
    filled = jnp.where(busy_device, TD, 1 + extra_tiles)
    chosen = jax.random.randint(key_list[2], (), 0, device_total)
    filled = jnp.where(jnp.arange(device_total) == chosen, TD, filled)
    slot_index = jnp.arange(TD)
    active = (slot_index[None, :] < filled[:, None]).reshape(-1)
    skip_pick = jax.random.randint(key_list[3], (TILES,), 0, 4) == 0
    skip_size = jax.random.randint(key_list[4], (TILES,), 1, 4)
    skipped = jnp.where(skip_pick, skip_size, 0)
    start_col = jax.random.randint(key_list[5], (), 0, 8)
    advance = jnp.where(active, 1 + skipped, 0).astype(jnp.int32)
    column = jnp.cumsum(advance).astype(jnp.int32) - 1 + start_col
    last_column = jnp.max(jnp.where(active, column, -1)).astype(jnp.int32)
    shifted = column - last_column + (4 * TILES + 6)
    tile_ids = jnp.where(active, shifted, -1).astype(jnp.int32)
    position = jnp.arange(TILES, dtype=jnp.int32)
    left_link = (active & (skipped == 0) & (position > 0)).astype(jnp.int32)
    ahead_slot = lax.cummin(jnp.where(active, position, TILES), reverse=True)
    next_slot = jnp.concatenate([ahead_slot[1:].astype(jnp.int32), jnp.full((1,), TILES, jnp.int32)])
    has_next = active & (next_slot < TILES)
    right_link = jnp.where(has_next, left_link[jnp.clip(next_slot, 0, TILES - 1)], 0).astype(jnp.int32)
    return (tile_ids, jnp.stack([left_link, right_link], axis=1))


def draw_tile_ids(key, part):
    return layout_draw(key)[0]


def draw_tile_links(key, part):
    return layout_draw(key)[1]


def feature_layout(key):
    rows = jnp.arange(SY, dtype=jnp.int32)[None, :, None]
    cols = jnp.arange(SX, dtype=jnp.int32)[None, None, :]
    feature = jnp.zeros((TILES, SY, SX), dtype=bool)
    for rect in range(5):
        rect_keys = jax.random.split(jax.random.fold_in(key, 7919 + rect), 5)
        top = jax.random.randint(rect_keys[0], (TILES, 1, 1), 0, SY)
        height = jax.random.randint(rect_keys[1], (TILES, 1, 1), max(SY // 8, 1), SY // 2 + 1)
        left = jax.random.randint(rect_keys[2], (TILES, 1, 1), 0, SX)
        breadth = jax.random.randint(rect_keys[3], (TILES, 1, 1), max(SX // 4, 1), SX + 1)
        kept = jax.random.randint(rect_keys[4], (TILES, 1, 1), 0, 5) < 3
        inside = kept & (rows >= top) & (rows < top + height) & (cols >= left) & (cols < left + breadth)
        feature = feature | inside
    return jnp.where(feature, 1.0, -1.0).astype(jnp.float32)


def draw_mask_params(key, part):
    signs = feature_layout(jax.random.fold_in(key, 3301))
    noise_key = jax.random.fold_in(key, 3313)
    amplitude = 1.5
    noise = 0.6 * jax.random.normal(noise_key, (TILES, SY, SX), jnp.float32)
    return jnp.clip(amplitude * signs + noise, -3.0, 3.0).astype(jnp.float32)


def draw_kernels(key, part):
    spread = 0.35 / math.sqrt(K)
    bound = 1.25 / math.sqrt(K)
    shape = (K, 2, FREQ, FREQ)
    base_key = jax.random.fold_in(key, 5501)
    values = spread * jax.random.normal(base_key, shape, jnp.float32)
    return jnp.clip(values, -bound, bound).astype(jnp.float32)


def shard_levels(stream_key, dims, cuts, least, largest):
    loudness, own = 1.0, jax.random.fold_in(stream_key, 6)
    for dim, parts in cuts:
        draws = jnp.exp(jax.random.uniform(jax.random.fold_in(own, dim), (parts,), jnp.float32, least / len(cuts), largest / len(cuts)))
        loudness = loudness * jnp.repeat(draws, dims[dim] // parts).reshape([-1 if axis == dim else 1 for axis in range(len(dims))])
    return loudness


def setup_inputs(seed: int = 0, part: int = 0) -> dict:
    key_of = jax.random.split(jax.random.key(seed), 8)
    part_keys = jax.random.split(jax.random.fold_in(key_of[7], part), 8)
    mask_params = draw_mask_params(jax.random.fold_in(jax.random.fold_in(key_of[7], part), 71), part)
    target = jnp.clip(1.0 * jax.random.uniform(part_keys[1], (TILES, SY, SX), jnp.float32) ** shard_levels(part_keys[1], (TILES, SY, SX), ((0, 16),), -0.2, 0.2), 0.0, 1.0)
    weight = jnp.clip(jnp.exp(math.log(3.0) - 2.3025851 * jax.random.uniform(part_keys[2], (TILES, SY, SX), jnp.float32) ** shard_levels(part_keys[2], (TILES, SY, SX), ((0, 16),), -0.2, 0.2)), 0.3, 3.0)
    kernels = draw_kernels(jax.random.fold_in(key_of[7], 71), part)
    kernel_weight = jnp.clip(jnp.exp(jax.random.uniform(key_of[4], (K,), jnp.float32, math.log(0.05), math.log(1.0))), 0.05, 1.0)
    tile_ids = draw_tile_ids(jax.random.fold_in(jax.random.fold_in(key_of[7], part), 71), part)
    tile_links = draw_tile_links(jax.random.fold_in(jax.random.fold_in(key_of[7], part), 71), part)
    return {"mask_params": mask_params, "target": target, "weight": weight, "kernels": kernels, "kernel_weight": kernel_weight, "tile_ids": tile_ids, "tile_links": tile_links}


HIGHEST = lax.Precision.HIGHEST
RESIST_SLOPE = 4.0
THRESHOLD = 0.9
STEP_SCALE = 0.04

def phase_table(length, period, band_count, offset):
    half_band = (band_count - 1) // 2
    positions = jnp.arange(length, dtype=jnp.int32) + offset
    frequency = jnp.arange(band_count, dtype=jnp.int32) - half_band
    turn_count = positions[:, None] * frequency[None, :] % period
    angles = turn_count.astype(jnp.float32) * (2.0 * math.pi / period)
    return (jnp.cos(angles), jnp.sin(angles))

def matmul_high(matrix_a, matrix_b):
    return jnp.dot(matrix_a, matrix_b, precision=HIGHEST)

def einsum_high(pattern, first_op, second_op):
    return jnp.einsum(pattern, first_op, second_op, precision=HIGHEST)

def spectral_core(spec_real, spec_imag, target_tile, weight_tile, kernel_real, kernel_imag, kernel_weight, row_cos, row_sin, own_cos, own_sin):
    drive_real = kernel_real * spec_real - kernel_imag * spec_imag
    drive_imag = kernel_real * spec_imag + kernel_imag * spec_real
    rows_real = einsum_high('yf,kfg->kgy', row_cos, drive_real) - einsum_high('yf,kfg->kgy', row_sin, drive_imag)
    rows_imag = einsum_high('yf,kfg->kgy', row_cos, drive_imag) + einsum_high('yf,kfg->kgy', row_sin, drive_real)
    field_real = einsum_high('kgy,xg->kyx', rows_real, own_cos) - einsum_high('kgy,xg->kyx', rows_imag, own_sin)
    field_imag = einsum_high('kgy,xg->kyx', rows_real, own_sin) + einsum_high('kgy,xg->kyx', rows_imag, own_cos)
    intensity = einsum_high('k,kyx->yx', kernel_weight, field_real * field_real + field_imag * field_imag)
    resist_now = jax.nn.sigmoid(RESIST_SLOPE * (intensity - THRESHOLD))
    slope_map = 2.0 * weight_tile * (resist_now - target_tile) * RESIST_SLOPE * resist_now * (1.0 - resist_now)
    back_real = slope_map * field_real
    back_imag = -slope_map * field_imag
    cols_real = einsum_high('kyx,xg->kgy', back_real, own_cos) - einsum_high('kyx,xg->kgy', back_imag, own_sin)
    cols_imag = einsum_high('kyx,xg->kgy', back_real, own_sin) + einsum_high('kyx,xg->kgy', back_imag, own_cos)
    freq_real = einsum_high('yf,kgy->kfg', row_cos, cols_real) - einsum_high('yf,kgy->kfg', row_sin, cols_imag)
    freq_imag = einsum_high('yf,kgy->kfg', row_cos, cols_imag) + einsum_high('yf,kgy->kfg', row_sin, cols_real)
    sum_real = einsum_high('k,kfg->fg', kernel_weight, kernel_real * freq_real - kernel_imag * freq_imag)
    sum_imag = einsum_high('k,kfg->fg', kernel_weight, kernel_real * freq_imag + kernel_imag * freq_real)
    return (resist_now, sum_real, sum_imag)

def tile_spectrum(pixels, row_cos, row_sin, col_cos, col_sin, unit_area):
    part_real = matmul_high(pixels, col_cos)
    part_imag = -matmul_high(pixels, col_sin)
    spec_real = (matmul_high(row_cos.T, part_real) + matmul_high(row_sin.T, part_imag)) * unit_area
    spec_imag = (matmul_high(row_cos.T, part_imag) - matmul_high(row_sin.T, part_real)) * unit_area
    return (spec_real, spec_imag)

def back_to_pixels(sum_real, sum_imag, row_cos, row_sin, col_cos, col_sin, unit_area):
    upper_real = matmul_high(row_cos, sum_real) + matmul_high(row_sin, sum_imag)
    upper_imag = matmul_high(row_cos, sum_imag) - matmul_high(row_sin, sum_real)
    return (matmul_high(upper_real, col_cos.T) + matmul_high(upper_imag, col_sin.T)) * (2.0 * unit_area)

def reference(mask_params, target, weight, kernels, kernel_weight, tile_ids, tile_links):
    slot_total, tile_rows, tile_cols = mask_params.shape
    band_count = kernels.shape[2]
    unit_area = 1.0 / (tile_rows * tile_cols)
    step_size = STEP_SCALE * math.sqrt(tile_rows * tile_cols)
    row_cos, row_sin = phase_table(tile_rows, 2 * tile_rows, band_count, 0)
    domain_cos, domain_sin = phase_table(3 * tile_cols, 3 * tile_cols, band_count, 0)
    own_cos = domain_cos[tile_cols:2 * tile_cols]
    own_sin = domain_sin[tile_cols:2 * tile_cols]
    kernel_real = kernels[:, 0]
    kernel_imag = kernels[:, 1]
    active = tile_ids >= 0
    slot_index = jnp.arange(slot_total, dtype=jnp.int32)
    seen_live = lax.cummax(jnp.where(active, slot_index, -1))
    before_slot = jnp.concatenate([jnp.full((1,), -1, jnp.int32), seen_live[:-1].astype(jnp.int32)])
    ahead_slot = lax.cummin(jnp.where(active, slot_index, slot_total), reverse=True)
    after_slot = jnp.concatenate([ahead_slot[1:].astype(jnp.int32), jnp.full((1,), slot_total, jnp.int32)])
    before_slot = jnp.clip(before_slot, 0, slot_total - 1)
    after_slot = jnp.clip(after_slot, 0, slot_total - 1)
    left_on = (tile_links[:, 0] == 1)[:, None, None]
    right_on = (tile_links[:, 1] == 1)[:, None, None]
    active_grid = active[:, None, None]

    def domain_pass(pieces):
        domain, target_tile, weight_tile = pieces
        spec_real, spec_imag = tile_spectrum(domain, row_cos, row_sin, domain_cos, domain_sin, unit_area)
        resist_now, sum_real, sum_imag = spectral_core(spec_real, spec_imag, target_tile, weight_tile, kernel_real, kernel_imag, kernel_weight, row_cos, row_sin, own_cos, own_sin)
        return (resist_now, back_to_pixels(sum_real, sum_imag, row_cos, row_sin, domain_cos, domain_sin, unit_area))
    resist_now = jnp.zeros_like(mask_params)
    for sweep in range(ITERS):
        transmit = jnp.tanh(mask_params)
        left_tiles = jnp.where(left_on, transmit[before_slot], 0.0)
        right_tiles = jnp.where(right_on, transmit[after_slot], 0.0)
        domain = jnp.concatenate([left_tiles, transmit, right_tiles], axis=2)
        resist_now, domain_grads = lax.map(domain_pass, (domain, target, weight))
        gradient = domain_grads[:, :, tile_cols:2 * tile_cols]
        gradient = gradient + jnp.where(left_on, domain_grads[before_slot][:, :, 2 * tile_cols:], 0.0)
        gradient = gradient + jnp.where(right_on, domain_grads[after_slot][:, :, :tile_cols], 0.0)
        mask_params = jnp.where(active_grid, mask_params - step_size * gradient * (1.0 - transmit * transmit), mask_params)
    resist_out = jnp.where(active_grid, resist_now, 0.0)
    return (mask_params, resist_out)
```

```python
import functools
import math

import jax
import jax.numpy as jnp
import numpy as np
from jax import lax
from jax.experimental import pallas as pl
from jax.experimental.pallas import tpu as pltpu
from jax.sharding import PartitionSpec as P

ITERS = 2
RESIST_SLOPE = 4.0
THRESHOLD = 0.9
STEP_SCALE = 0.04
GROUP = 8
F32 = jnp.float32
BF16 = jnp.bfloat16


def snake_ring(groups, count, step):
    order = []
    for g in range(groups):
        span = range(count) if g % 2 == 0 else range(count - 1, -1, -1)
        order += [g * count + i for i in span]
    total = len(order)
    return [(order[j], order[(j + step) % total]) for j in range(total)]


def split_table(table):
    table = jnp.asarray(table, F32)
    high = table.astype(BF16)
    return high, (table - high.astype(F32)).astype(BF16)


class Tables:
    def __init__(self, rows, cols, bands, slots):
        half = (bands - 1) // 2
        self.half = half
        self.mid = 16
        self.grows = 2 * half + self.mid
        y = np.arange(rows)
        freq = np.concatenate([-np.arange(half, 0, -1), np.arange(1, half + 1)])
        turn = (freq[:, None] * y[None, :]) % (2 * rows)
        angle = turn * (2.0 * np.pi / (2 * rows))
        c, s = np.cos(angle), np.sin(angle)
        nf = len(freq)
        self.nf = nf
        order = np.zeros((self.grows, bands), jnp.bfloat16)
        for j in range(half):
            order[j, half + 1 + j] = 1.0
            order[half + self.mid + j, half - 1 - j] = 1.0
        order[half, half] = 1.0
        self.order = order
        w = slots * rows
        t1 = np.zeros((slots * 2 * nf, 2 * w))
        for t in range(slots):
            r0, y0 = t * 2 * nf, t * rows
            t1[r0 : r0 + nf, y0 : y0 + rows] = c
            t1[r0 : r0 + nf, w + y0 : w + y0 + rows] = s
            t1[r0 + nf : r0 + 2 * nf, y0 : y0 + rows] = -s
            t1[r0 + nf : r0 + 2 * nf, w + y0 : w + y0 + rows] = c
        t5 = np.zeros_like(t1)
        for t in range(slots):
            r0, y0 = t * 2 * nf, t * rows
            t5[r0 : r0 + nf, y0 : y0 + rows] = c
            t5[r0 : r0 + nf, w + y0 : w + y0 + rows] = -s
            t5[r0 + nf : r0 + 2 * nf, y0 : y0 + rows] = s
            t5[r0 + nf : r0 + 2 * nf, w + y0 : w + y0 + rows] = c
        area = 1.0 / (rows * cols)
        gpos = np.arange(1, half + 1)
        x = np.arange(3 * cols)
        gturn = (x[:, None] * gpos[None, :]) % (3 * cols)
        gangle = gturn * (2.0 * np.pi / (3 * cols))
        t6 = np.zeros((3 * cols, self.grows))
        t6[:, :half] = np.cos(gangle)
        t6[:, half] = 1.0
        t6[:, half + self.mid :] = np.sin(gangle)
        t2 = t6[cols : 2 * cols]
        ones = np.zeros((w, w))
        for t in range(slots):
            ones[t * rows : (t + 1) * rows, t * rows : (t + 1) * rows] = 1.0

        def right(table):
            h, l = split_np(table)
            return np.concatenate([h, h, l], 0)

        def left(table, pad):
            h, l = split_np(table)
            z = np.zeros((table.shape[0], pad), h.dtype)
            return np.concatenate([h, h, l, z], 1)

        def stacked(table):
            h, l = split_np(table)
            return np.concatenate(
                [np.concatenate([h, h], 1), np.concatenate([l, np.zeros_like(l)], 1)], 0
            )

        self.pad = 256 - 3 * self.grows
        self.arrays = dict(
            t1=right(t1),
            t4=right(t5.T),
            t5=right(t5),
            t8=right(t1.T * area),
            t2=left(t2, self.pad),
            t3=stacked(t2.T),
            t6=left(t6 * (2.0 * area), self.pad),
            t7=left(t6.T, 0),
            ones=ones.astype(jnp.bfloat16),
        )


def split_np(table):
    table = np.asarray(table, np.float32)
    high = table.astype(jnp.bfloat16)
    low = (table - high.astype(np.float32)).astype(jnp.bfloat16)
    return high, low


def split(v):
    high = v.astype(BF16)
    return high, (v - high.astype(F32)).astype(BF16)


def dot(a, b):
    return jnp.dot(a, b, preferred_element_type=F32)


def lanes3(v):
    high, low = split(v)
    return jnp.concatenate([high, low, high], 1)


def rows3(v, pad):
    high, low = split(v)
    parts = [high, low, high]
    if pad:
        parts.append(high[:pad])
    return jnp.concatenate(parts, 0)


def swap_halves(v):
    return pltpu.roll(v, v.shape[-1] // 2, v.ndim - 1)


def first_half(shape, axis):
    return lax.broadcasted_iota(jnp.int32, shape, axis) < shape[axis] // 2


def pack_tile(wide):
    half = wide.shape[0] // 2
    top, low = wide[:half], swap_halves(wide[half:])
    return jnp.where(first_half(top.shape, 1), top, low)


def unpack_tile(packed):
    return jnp.concatenate([packed, swap_halves(packed)], 0)


def join_tiles(first, second_low):
    return jnp.where(first_half(first.shape, 1), first, swap_halves(second_low))


def read_flags(ids, links):
    both = ids[1] >= 0
    even = lax.rem(lax.axis_index("grp"), 2) == 0
    return both, links[0, 0] == 1, links[1, 0] == 1, links[0, 1] == 1, links[1, 1] == 1, even


def pick(lane0, first, second):
    return jnp.logical_or(
        jnp.logical_and(lane0, first), jnp.logical_and(jnp.logical_not(lane0), second)
    )


def sort_received(flags, got_a, got_b):
    even = flags[5]
    return jnp.where(even, got_a, got_b), jnp.where(even, got_b, got_a)


def order_sent(flags, to_next, to_prev):
    even = flags[5]
    return jnp.where(even, to_next, to_prev), jnp.where(even, to_prev, to_next)


def domain_of(flags, own, prev_low, next_low):
    both = flags[0]
    lane0 = first_half(own.shape, 1)
    left = join_tiles(prev_low, own)
    swapped = swap_halves(own)
    right0 = jnp.where(both, swapped, next_low)
    right = join_tiles(right0, next_low)
    left_on = pick(lane0, flags[1], flags[2])
    right_on = pick(lane0, flags[3], flags[4])
    return jnp.where(left_on, left, 0.0), own, jnp.where(right_on, right, 0.0)


def core(tb, flags, dom, target, weight, ha_ref, hb_ref, h0r_ref, h0i_ref, t, e_ref):
    half, mid = tb.half, tb.mid
    lo_end = half + mid
    left, own, right = dom
    area_dom = jnp.concatenate([left, own, right], 0)
    g = dot(t["t7"][...], rows3(area_dom, 0))
    cosd, sind = g[:half], g[lo_end:]
    gre = jnp.concatenate([g[:lo_end], cosd], 0)
    gim = jnp.concatenate([-sind, jnp.zeros_like(g[half:lo_end]), sind], 0)
    glanes = lanes3(jnp.concatenate([gre, gim], 1))
    u = dot(glanes, t["t8"][...])
    area = 1.0 / (target.shape[0] * (target.shape[1] // 2))
    ones = t["ones"][...]

    def tile_sum(v):
        high, low = split(v)
        return dot(high, ones) + dot(low, ones)

    c0r = tile_sum(gre) * area
    c0i = tile_sum(gim) * area
    wl = 2 * tb.nf
    u0, u1 = u[:, :wl], u[:, wl:]
    v0, v1 = swap_halves(u0), swap_halves(u1)
    kcount = ha_ref.shape[0]
    w = target.shape[1]
    rows = tb.grows

    inten = jnp.zeros(target.shape, F32)
    for k0 in range(0, kcount, GROUP):
        ks = range(k0, min(k0 + GROUP, kcount))
        drive = []
        for k in ks:
            a, b = ha_ref[k], hb_ref[k]
            drive.append(jnp.concatenate([a * u0 + b * v0, a * u1 + b * v1], 1))
        r_all = dot(lanes3(jnp.concatenate(drive, 0)), t["t1"][...])
        for n, k in enumerate(ks):
            r = r_all[n * rows : (n + 1) * rows]
            hr, hi = h0r_ref[k], h0i_ref[k]
            re = r[:, :w] + (hr * c0r - hi * c0i)
            im = r[:, w:] + (hr * c0i + hi * c0r)
            wre = jnp.concatenate(
                [re[:half] + re[lo_end:], re[half:lo_end], im[lo_end:] - im[:half]], 0
            )
            wim = jnp.concatenate(
                [im[:half] + im[lo_end:], im[half:lo_end], re[:half] - re[lo_end:]], 0
            )
            e = dot(t["t2"][...], rows3(jnp.concatenate([wre, wim], 1), tb.pad))
            e_ref[k] = e
            inten = inten + (e[:, :w] * e[:, :w] + e[:, w:] * e[:, w:])
    resist = jax.nn.sigmoid(RESIST_SLOPE * (inten - THRESHOLD))
    slope = 2.0 * weight * (resist - target) * RESIST_SLOPE * resist * (1.0 - resist)
    slope2 = jnp.concatenate([slope, slope], 1)

    q1 = [jnp.zeros((rows, wl), F32) for _ in range(2)]
    q2 = [jnp.zeros((rows, wl), F32) for _ in range(2)]
    zre = jnp.zeros((rows, w), F32)
    zim = jnp.zeros((rows, w), F32)
    for k0 in range(0, kcount, GROUP):
        ks = range(k0, min(k0 + GROUP, kcount))
        cs = []
        for k in ks:
            high, low = split(e_ref[k] * slope2)
            o = dot(t["t3"][...], jnp.concatenate([high, low], 0))
            o = o[:rows] + o[rows:]
            b1, b2 = o[:, :w], o[:, w:]
            c1, c10, s1 = b1[:half], b1[half:lo_end], b1[lo_end:]
            c2, c20, s2 = b2[:half], b2[half:lo_end], b2[lo_end:]
            cre = jnp.concatenate([c1 + s2, c10, c1 - s2], 0)
            cim = jnp.concatenate([s1 - c2, -c20, -s1 - c2], 0)
            hr, hi = h0r_ref[k], h0i_ref[k]
            zre = zre + (hr * cre - hi * cim)
            zim = zim + (hr * cim + hi * cre)
            cs.append(jnp.concatenate([cre, cim], 1))
        f_all = dot(lanes3(jnp.concatenate(cs, 0)), t["t4"][...])
        for n, k in enumerate(ks):
            f = f_all[n * rows : (n + 1) * rows]
            a, b = ha_ref[k], hb_ref[k]
            for s in range(2):
                fs = f[:, s * wl : (s + 1) * wl]
                q1[s] = q1[s] + a * fs
                q2[s] = q2[s] + b * fs
    sums = jnp.concatenate([q1[s] - swap_halves(q2[s]) for s in range(2)], 1)
    ug = dot(lanes3(sums), t["t5"][...])
    ure = ug[:, :w] + tile_sum(zre)
    uim = ug[:, w:] + tile_sum(zim)
    w6 = jnp.concatenate(
        [ure[:half] + ure[lo_end:], ure[half:lo_end], uim[:half] - uim[lo_end:]], 0
    )
    dg = dot(t["t6"][...], rows3(w6, tb.pad))
    return resist, dg


def thirds(flags, dg):
    cols = dg.shape[0] // 3
    left, mid, right = dg[:cols], dg[cols : 2 * cols], dg[2 * cols :]
    both = flags[0]
    lane0 = first_half(mid.shape, 1)
    cross = jnp.where(lane0, swap_halves(left), swap_halves(right))
    use = pick(lane0, flags[3], flags[2])
    partial = mid + jnp.where(jnp.logical_and(use, both), cross, 0.0)
    to_next = pack_tile(jnp.where(both, swap_halves(right), right))
    to_prev = pack_tile(left)
    return partial, to_next, to_prev


def add_received(flags, partial, from_prev, from_next):
    prev_low, next_low = unpack_tile(from_prev), unpack_tile(from_next)
    both = flags[0]
    lane0 = first_half(partial.shape, 1)
    prev_on = jnp.logical_and(lane0, flags[1])
    next_on = pick(lane0, jnp.logical_and(flags[3], jnp.logical_not(both)), jnp.logical_and(flags[4], both))
    nxt = jnp.where(both, swap_halves(next_low), next_low)
    g = partial + jnp.where(prev_on, prev_low, 0.0)
    return g + jnp.where(next_on, nxt, 0.0)


def update(flags, params, gradient, step):
    transmit = jnp.tanh(params)
    live = jnp.logical_or(first_half(params.shape, 1), flags[0])
    return jnp.where(live, params - step * gradient * (1.0 - transmit * transmit), params)


def pick_sent(flags, wide):
    both = flags[0]
    return pack_tile(jnp.where(both, swap_halves(wide), wide)), pack_tile(wide)


def kernel_first(tb, names, ids, links, mp, got_a, got_b, target, weight, ha, hb, h0r, h0i, *rest):
    t = dict(zip(names, rest))
    partial_ref, params_ref, send_a, send_b, e_ref = rest[len(names) :]
    slots, rows, cols = mp.shape
    flags = read_flags(ids, links)
    prev, nxt = sort_received(flags, got_a[...], got_b[...])
    params = mp[...].reshape(slots * rows, cols).T
    own = jnp.tanh(params)
    beside = jnp.tanh(jnp.concatenate([prev, nxt], 0)).T
    dom = domain_of(flags, own, beside, swap_halves(beside))
    tgt = target[...].reshape(slots * rows, cols).T
    wgt = weight[...].reshape(slots * rows, cols).T
    _, dg = core(tb, flags, dom, tgt, wgt, ha, hb, h0r, h0i, t, e_ref)
    partial, to_next, to_prev = thirds(flags, dg)
    partial_ref[...] = partial
    params_ref[...] = params
    send_a[...], send_b[...] = order_sent(flags, to_next, to_prev)


def kernel_update(step, ids, links, partial, params, got_a, got_b, out, send_a, send_b):
    flags = read_flags(ids, links)
    prev, nxt = sort_received(flags, got_a[...], got_b[...])
    gradient = add_received(flags, partial[...], prev, nxt)
    new = update(flags, params[...], gradient, step)
    out[...] = new
    send_a[...], send_b[...] = order_sent(flags, *pick_sent(flags, new))


def kernel_again(tb, names, ids, links, params, got_a, got_b, target, weight, ha, hb, h0r, h0i, *rest):
    t = dict(zip(names, rest))
    partial_ref, resist_ref, send_a, send_b, e_ref = rest[len(names) :]
    slots, rows, cols = target.shape
    flags = read_flags(ids, links)
    prev, nxt = sort_received(flags, got_a[...], got_b[...])
    dom = domain_of(
        flags,
        jnp.tanh(params[...]),
        jnp.tanh(unpack_tile(prev)),
        jnp.tanh(unpack_tile(nxt)),
    )
    tgt = target[...].reshape(slots * rows, cols).T
    wgt = weight[...].reshape(slots * rows, cols).T
    resist, dg = core(tb, flags, dom, tgt, wgt, ha, hb, h0r, h0i, t, e_ref)
    partial, to_next, to_prev = thirds(flags, dg)
    partial_ref[...] = partial
    live = jnp.logical_or(first_half(resist.shape, 1), flags[0])
    resist_ref[...] = jnp.where(live, resist, 0.0).T.reshape(slots, rows, cols)
    send_a[...], send_b[...] = order_sent(flags, to_next, to_prev)


def kernel_last(step, ids, links, partial, params, got_a, got_b, out):
    flags = read_flags(ids, links)
    prev, nxt = sort_received(flags, got_a[...], got_b[...])
    gradient = add_received(flags, partial[...], prev, nxt)
    out[...] = update(flags, params[...], gradient, step).T.reshape(out.shape)


def call(body, ins, outs, scratch=(), scalars=2, limit=32 << 20):
    smem = pl.BlockSpec(memory_space=pltpu.SMEM)
    vmem = pl.BlockSpec(memory_space=pltpu.VMEM)
    return pl.pallas_call(
        body,
        in_specs=[smem] * scalars + [vmem] * (len(ins) - scalars),
        out_specs=[vmem] * len(outs),
        out_shape=[jax.ShapeDtypeStruct(s, F32) for s in outs],
        scratch_shapes=list(scratch),
        compiler_params=pltpu.CompilerParams(vmem_limit_bytes=limit),
    )(*ins)


def kernel_arrange(tb, root, kernels, order, out_a, out_b, out_0r, out_0i):
    half, nf = tb.half, tb.nf
    rows = order[...]
    lane = lax.broadcasted_iota(jnp.int32, (tb.grows, 2 * nf), 1)

    def turn(h):
        high, low = split(h)
        dims = (((1,), (1,)), ((), ()))
        v = lax.dot_general(rows, high, dims, preferred_element_type=F32)
        v = v + lax.dot_general(rows, low, dims, preferred_element_type=F32)
        zero = jnp.broadcast_to(v[:, half : half + 1], lane.shape)
        v = jnp.concatenate([v, jnp.zeros((tb.grows, 2 * nf - v.shape[1]), F32)], 1)
        v = jnp.where(lane < half, v, pltpu.roll(v, 2 * nf - 1, 1))
        return jnp.where(lane < nf, v, pltpu.roll(v, nf, 1)), zero

    for k in range(kernels.shape[0]):
        real, zero_r = turn(kernels[k, 0] * root[k])
        imag, zero_i = turn(kernels[k, 1] * root[k])
        out_a[k] = real
        out_b[k] = jnp.where(lane < nf, -imag, imag)
        out_0r[k] = zero_r
        out_0i[k] = zero_i


def local(mesh_shape, mask_params, target, weight, kernels, kernel_weight, tile_ids, tile_links):
    slots, rows, cols = mask_params.shape
    bands = kernels.shape[2]
    kcount = kernels.shape[0]
    groups, count = mesh_shape
    step = STEP_SCALE * math.sqrt(rows * cols)
    tb = Tables(rows, cols, bands, slots)
    names = tuple(tb.arrays)
    tables = [jnp.asarray(tb.arrays[n]) for n in names]
    axes = ("grp", "tile")
    ring_a = snake_ring(groups, count, 1)
    ring_b = snake_ring(groups, count, -1)

    def exchange(a, b):
        return lax.ppermute(a, axes, ring_a), lax.ppermute(b, axes, ring_b)

    last_slot = (tile_ids[1] >= 0).astype(jnp.int32)
    even = lax.rem(lax.axis_index("grp"), 2) == 0
    got = exchange(
        lax.dynamic_index_in_dim(mask_params, jnp.where(even, last_slot, 0), 0, False),
        lax.dynamic_index_in_dim(mask_params, jnp.where(even, 0, last_slot), 0, False),
    )
    arranged = call(
        functools.partial(kernel_arrange, tb),
        [jnp.sqrt(kernel_weight), kernels, jnp.asarray(tb.order)],
        [(kcount, tb.grows, 2 * tb.nf)] * 4,
        scalars=1,
    )
    field = pltpu.VMEM((kcount, cols, 2 * slots * rows), F32)
    wide = (cols, slots * rows)
    packed = (cols // 2, slots * rows)
    partial, params, sa, sb = call(
        functools.partial(kernel_first, tb, names),
        [tile_ids, tile_links, mask_params, *got, target, weight, *arranged, *tables],
        [wide, wide, packed, packed],
        [field],
    )
    got = exchange(sa, sb)
    params, sa, sb = call(
        functools.partial(kernel_update, step),
        [tile_ids, tile_links, partial, params, *got],
        [wide, packed, packed],
    )
    got = exchange(sa, sb)
    partial, resist, sa, sb = call(
        functools.partial(kernel_again, tb, names),
        [tile_ids, tile_links, params, *got, target, weight, *arranged, *tables],
        [wide, mask_params.shape, packed, packed],
        [field],
    )
    got = exchange(sa, sb)
    (out,) = call(
        functools.partial(kernel_last, step),
        [tile_ids, tile_links, partial, params, *got],
        [mask_params.shape],
    )
    return (out, resist)


def solution(mesh):
    tiles = P(("grp", "tile"), None, None)
    return jax.shard_map(
        functools.partial(local, (mesh.shape["grp"], mesh.shape["tile"])),
        mesh=mesh,
        in_specs=(tiles, tiles, tiles, P(), P(), P(("grp", "tile")), P(("grp", "tile"), None)),
        out_specs=(tiles, tiles),
        check_vma=False,
    )
```

```python
import functools
import math

import jax
import jax.numpy as jnp
import numpy as np
from jax import lax
from jax.experimental import pallas as pl
from jax.experimental.pallas import tpu as pltpu
from jax.sharding import PartitionSpec as P

ITERS = 2
RESIST_SLOPE = 4.0
THRESHOLD = 0.9
STEP_SCALE = 0.04
GROUP = 8
MID = 16
F32 = jnp.float32
BF16 = jnp.bfloat16


def snake_ring(groups, count, step):
    order = []
    for g in range(groups):
        span = range(count) if g % 2 == 0 else range(count - 1, -1, -1)
        order += [g * count + i for i in span]
    total = len(order)
    return [(order[j], order[(j + step) % total]) for j in range(total)]


def split_np(table):
    table = np.asarray(table, np.float32)
    high = table.astype(jnp.bfloat16)
    low = (table - high.astype(np.float32)).astype(jnp.bfloat16)
    return high, low


class Tables:
    def __init__(self, rows, cols, bands):
        half = (bands - 1) // 2
        self.half = half
        area = 1.0 / (rows * cols)
        self.area = area
        pos = np.arange(1, half + 1)
        angle = (np.arange(rows)[:, None] * pos[None, :] % (2 * rows)) * (np.pi / rows)
        ty = np.zeros((rows, 2 * half + MID))
        ty[:, :half] = np.cos(angle)
        ty[:, half] = 1.0
        ty[:, half + MID :] = np.sin(angle)
        freq = np.concatenate([np.arange(-half, 0), np.arange(1, half + 1)])
        self.nf = len(freq)
        period = 3 * cols
        theta = (np.arange(period)[:, None] * freq[None, :] % period) * (2.0 * np.pi / period)
        c, s = np.cos(theta), np.sin(theta)
        co, so = c[cols : 2 * cols].T, s[cols : 2 * cols].T
        forward = np.block([[co, so], [-so, co]])
        adjoint = np.block([[co.T, so.T], [so.T, -co.T]])
        gradient = np.concatenate([c.T, s.T], 0) * (2.0 * area)
        spectrum = np.concatenate([c, -s], 1) * area

        def left(table):
            h, l = split_np(table)
            return np.concatenate([h, h, l], 1)

        def right(table):
            h, l = split_np(table)
            return np.concatenate([h, h, l], 0)

        part = np.arange(2 * self.nf) // (self.nf // 2) % 2
        ones = np.zeros((2 * self.nf, 2 * cols))
        ones[part == 0, :cols] = 1.0
        ones[part == 1, cols:] = 1.0
        sums = np.concatenate([ones.T, ones.T, np.zeros_like(ones.T)], 0).astype(jnp.bfloat16)
        sums[cols : 2 * cols] *= -1
        sums[3 * cols : 4 * cols] *= -1
        picks = np.zeros((self.nf // 2, MID, 2 * self.nf), jnp.bfloat16)
        for k in range(self.nf // 2):
            picks[k, :, k :: self.nf // 2] = 1.0

        def wide(table):
            h, l = split_np(table)
            top = np.concatenate([h, l], 1)
            return np.concatenate([top, np.concatenate([h, np.zeros_like(l)], 1)], 0)

        self.arrays = dict(
            ty=left(ty),
            tyt=left(ty.T),
            fwd=np.concatenate([right(forward), ones.astype(jnp.bfloat16)], 0),
            picks=picks,
            adj=np.concatenate([right(adjoint), sums], 1),
            grad=right(gradient),
            spec=np.stack([wide(spectrum[j * cols : (j + 1) * cols]) for j in range(3)]),
        )
        order = np.zeros((2 * half + 8, 2 * half + 8), jnp.bfloat16)
        for j in range(half):
            order[j, half + 1 + j] = 1.0
            order[half + 8 + j, half - 1 - j] = 1.0
        order[half, half] = 1.0
        self.order = order


def split(v):
    high = v.astype(BF16)
    return high, (v - high.astype(F32)).astype(BF16)


def dot(a, b):
    return jnp.dot(a, b, preferred_element_type=F32)


def lanes3(v):
    high, low = split(v)
    return jnp.concatenate([high, low, high], 1)


def rows3(v):
    high, low = split(v)
    return jnp.concatenate([high, low, high], 0)


def wide_dot(v, table):
    high, low = split(v)
    o = dot(jnp.concatenate([high, low], 1), table)
    n = o.shape[1] // 2
    return o[:, :n] + o[:, n:]


def lane_of(shape):
    return lax.broadcasted_iota(jnp.int32, shape, 1)


def swap(v, block):
    n = v.shape[1]
    if 2 * block == n:
        return pltpu.roll(v, block, 1)
    even = lax.rem(lax.div(lane_of(v.shape), block), 2) == 0
    return jnp.where(even, pltpu.roll(v, n - block, 1), pltpu.roll(v, block, 1))


def conj(v, block):
    even = lax.rem(lax.div(lane_of((1, v.shape[1])), block), 2) == 0
    return v * jnp.where(even, 1.0, -1.0)


def minus_i(v, block):
    return conj(swap(v, block), block)


def fold(half, plus, zero, minus):
    gap = jnp.zeros((MID - 8, plus.shape[1]), F32)
    return jnp.concatenate([plus, zero, gap, minus], 0)


def spread(half, o, block):
    cosine, zero, sine = o[:half], o[half : half + 8], minus_i(o[half + MID :], block)
    return jnp.concatenate([cosine + sine, zero, cosine - sine], 0)


def drive(half, a, b, u):
    p, m = slice(0, half), slice(half + 8, 2 * half + 8)
    d = a * u[0] + b * u[1]
    turned_p = a[p] * u[2][p] + b[p] * u[3][p]
    turned_m = a[m] * u[2][m] + b[m] * u[3][m]
    return fold(half, d[p] + d[m], d[half : half + 8], turned_p - turned_m)


def phases(u, block):
    v = swap(u, block)
    return u, v, -conj(v, block), conj(u, block)


def gather(half, q, a, b, o, block):
    p, z, m = slice(0, half), slice(half, half + 8), slice(half + 8, 2 * half + 8)
    c, zero, s = o[:half], o[half : half + 8], conj(o[half + MID :], block)
    parts = [
        a[p] * c + b[p] * s,
        a[z] * zero,
        a[m] * c - b[m] * s,
        b[p] * c - a[p] * s,
        b[z] * zero,
        b[m] * c + a[m] * s,
    ]
    return parts if q is None else [x + y for x, y in zip(q, parts)]


def back_rows(half, q, block):
    p, z, m = (q[j] - swap(q[j + 3], block) for j in range(3))
    return fold(half, p + m, z, minus_i(p - m, block))


def lane_sum(v):
    return jnp.sum(v, axis=1, keepdims=True)


def core(tb, dom, target, weight, ha_ref, hb_ref, h0, t, e_ref, keep=None):
    half, nf = tb.half, tb.nf
    slots, rows, cols = target.shape
    kcount = ha_ref.shape[0]
    wl = 2 * nf
    zb = wl // (2 * slots)
    ty, tyt = t["ty"], t["tyt"]
    thirds_of = [dom[:, j * cols : (j + 1) * cols] for j in range(3)]
    g = sum(wide_dot(v, t["spec"][j]) for j, v in enumerate(thirds_of))
    gw = jnp.concatenate([g[s * rows : (s + 1) * rows] for s in range(slots)], 1)
    spec = dot(tyt[...], rows3(gw))
    us = [phases(spread(half, spec[:, s * wl : (s + 1) * wl], nf), nf) for s in range(slots)]
    g0 = lane_sum(thirds_of[0] + thirds_of[1] + thirds_of[2]) * tb.area
    block = lax.div(lane_of((rows, wl)), zb)
    g0w = jnp.zeros((rows, wl), F32)
    for s in range(slots):
        g0w = jnp.where(block == 2 * s, g0[s * rows : (s + 1) * rows], g0w)
    u0 = phases(spread(half, dot(tyt[...], rows3(g0w)), zb), zb)
    a0, b0 = h0[0], h0[1]
    r0 = dot(ty[...], rows3(drive(half, a0, b0, u0)))
    r0h, r0l = split(r0)
    r0l = pltpu.roll(r0l.astype(F32), wl // 2, 1)
    r0s = [
        jnp.where(lax.div(block, 2) == s, r0h.astype(F32), r0l).astype(BF16) for s in range(slots)
    ]
    inner = lax.rem(lane_of((rows, wl)), zb)
    groups = [range(k0, min(k0 + GROUP, kcount)) for k0 in range(0, kcount, GROUP)]

    def in_pairs(ks):
        return [ks[i : i + 2] for i in range(0, len(ks), 2)]

    def row_stage(s, ks):
        out, extra = [], []
        for pair in in_pairs(ks):
            w = jnp.concatenate([drive(half, ha_ref[k], hb_ref[k], us[s]) for k in pair], 1)
            r = dot(ty[...], rows3(w))
            for n, k in enumerate(pair):
                out.append(r[:, n * wl : (n + 1) * wl])
                extra += [r0s[s][i : i + MID] * t["picks"][k] for i in range(0, rows, MID)]
        return jnp.concatenate([lanes3(jnp.concatenate(out, 0)), jnp.concatenate(extra, 0)], 1)

    def field_stage(s, ks, ready, inten):
        field = dot(ready, t["fwd"][...])
        for n, k in enumerate(ks):
            e = field[n * rows : (n + 1) * rows]
            e_ref[s, k] = e
            inten = inten + (e[:, :cols] * e[:, :cols] + e[:, cols:] * e[:, cols:])
        return inten

    def slope_of(s, inten):
        resist = jax.nn.sigmoid(RESIST_SLOPE * (inten - THRESHOLD))
        slope = 2.0 * weight[s] * (resist - target[s]) * RESIST_SLOPE * resist * (1.0 - resist)
        return resist, jnp.concatenate([slope, slope], 1)

    def column_stage(s, ks, slope2):
        back = jnp.concatenate([e_ref[s, k] * slope2 for k in ks], 0)
        return dot(lanes3(back), t["adj"][...])

    def sum_stage(s, ks, ready, c0, q):
        for m, pair in enumerate(in_pairs(ks)):
            parts = [ready[(2 * m + n) * rows : (2 * m + n + 1) * rows] for n in range(len(pair))]
            o = dot(tyt[...], rows3(jnp.concatenate([v[:, :wl] for v in parts], 1)))
            for n, k in enumerate(pair):
                c0 = jnp.where(inner == k, parts[n][:, wl:], c0)
                q = gather(half, q, ha_ref[k], hb_ref[k], o[:, n * wl : (n + 1) * wl], nf)
        return c0, q

    def finish(s, c0, q):
        own = lax.div(block, 2) == s
        q0 = gather(half, None, a0, b0, dot(tyt[...], rows3(jnp.where(own, c0, 0.0))), zb)
        ug = dot(ty[...], rows3(back_rows(half, q, nf)))
        ug0 = dot(ty[...], rows3(back_rows(half, q0, zb)))
        flat = lane_sum(jnp.where(block == 2 * s, ug0, 0.0))
        return dot(lanes3(ug), t["grad"][...]) + (2.0 * tb.area) * flat

    grads = []
    slope2 = None
    for s in range(slots + 1):
        forward, backward = s < slots, s > 0
        inten = jnp.zeros((rows, cols), F32)
        c0, q = jnp.zeros((rows, wl), F32), None
        ahead_f = row_stage(s, groups[0]) if forward else None
        ahead_b = column_stage(s - 1, groups[0], slope2) if backward else None
        for j, ks in enumerate(groups):
            now_f, now_b = ahead_f, ahead_b
            more = j + 1 < len(groups)
            if forward and more:
                ahead_f = row_stage(s, groups[j + 1])
            if backward and more:
                ahead_b = column_stage(s - 1, groups[j + 1], slope2)
            if forward:
                inten = field_stage(s, ks, now_f, inten)
            if backward:
                c0, q = sum_stage(s - 1, ks, now_b, c0, q)
        if backward:
            grads.append(finish(s - 1, c0, q))
        if forward:
            resist, slope2 = slope_of(s, inten)
            if keep is not None:
                keep(s, resist)
    return grads


def read_flags(ids, links):
    both = ids[1] >= 0
    even = lax.rem(lax.axis_index("grp"), 2) == 0
    return both, links[0, 0] == 1, links[1, 0] == 1, links[0, 1] == 1, links[1, 1] == 1, even


def in_order(even, first, second):
    return jnp.where(even, first, second), jnp.where(even, second, first)


def domain_of(flags, prev, own0, own1, nxt):
    both, l0, l1, r0, r1, _ = flags
    zero = jnp.zeros_like(own0)
    first = [jnp.where(l0, prev, zero), own0, jnp.where(r0, jnp.where(both, own1, nxt), zero)]
    second = [jnp.where(l1, own0, zero), own1, jnp.where(r1, nxt, zero)]
    return jnp.concatenate([jnp.concatenate(first, 1), jnp.concatenate(second, 1)], 0)


def thirds(flags, dg):
    both, l0, l1, r0, r1, _ = flags
    cols = dg[0].shape[1] // 3
    left0, mid0, right0 = (dg[0][:, j * cols : (j + 1) * cols] for j in range(3))
    left1, mid1, right1 = (dg[1][:, j * cols : (j + 1) * cols] for j in range(3))
    part0 = mid0 + jnp.where(jnp.logical_and(r0, both), left1, 0.0)
    part1 = mid1 + jnp.where(l1, right0, 0.0)
    return part0, part1, jnp.where(both, right1, right0), left0


def own_gradient(flags, part0, part1, from_prev, from_next):
    both, l0, l1, r0, r1, _ = flags
    g0 = part0 + jnp.where(l0, from_prev, 0.0)
    g0 = g0 + jnp.where(jnp.logical_and(r0, jnp.logical_not(both)), from_next, 0.0)
    return g0, part1 + jnp.where(jnp.logical_and(r1, both), from_next, 0.0)


def stepped(step, params, gradient):
    transmit = jnp.tanh(params)
    return params - step * gradient * (1.0 - transmit * transmit)


def kernel_first(tb, names, ids, links, mp, got_a, got_b, target, weight, ha, hb, h0, *rest):
    t = dict(zip(names, rest))
    part, send_a, send_b, e_ref = rest[len(names) :]
    flags = read_flags(ids, links)
    prev, nxt = in_order(flags[5], got_a[...], got_b[...])
    tile = [jnp.tanh(v) for v in (prev, mp[0], mp[1], nxt)]
    dg = core(tb, domain_of(flags, *tile), target, weight, ha, hb, h0, t, e_ref)
    part[0], part[1], to_next, to_prev = thirds(flags, dg)
    send_a[...], send_b[...] = in_order(flags[5], to_next, to_prev)


def kernel_update(step, ids, links, part, params, got_a, got_b, out, send_a, send_b):
    flags = read_flags(ids, links)
    prev, nxt = in_order(flags[5], got_a[...], got_b[...])
    g0, g1 = own_gradient(flags, part[0], part[1], prev, nxt)
    new0 = stepped(step, params[0], g0)
    new1 = jnp.where(flags[0], stepped(step, params[1], g1), params[1])
    out[0], out[1] = new0, new1
    send_a[...], send_b[...] = in_order(flags[5], jnp.where(flags[0], new1, new0), new0)


def kernel_second(tb, names, ids, links, mp, got_a, got_b, target, weight, ha, hb, h0, *rest):
    t = dict(zip(names, rest))
    part, resist_out, send_a, send_b, e_ref, resist_v, sems = rest[len(names) :]
    flags = read_flags(ids, links)
    prev, nxt = in_order(flags[5], got_a[...], got_b[...])
    tile = [jnp.tanh(v) for v in (prev, mp[0], mp[1], nxt)]
    moves = []

    def keep(s, resist):
        resist_v[s] = resist if s == 0 else jnp.where(flags[0], resist, 0.0)
        moves.append(pltpu.make_async_copy(resist_v.at[s], resist_out.at[s], sems.at[s]))
        moves[-1].start()

    dg = core(tb, domain_of(flags, *tile), target, weight, ha, hb, h0, t, e_ref, keep)
    part[0], part[1], to_next, to_prev = thirds(flags, dg)
    send_a[...], send_b[...] = in_order(flags[5], to_next, to_prev)
    for move in moves:
        move.wait()


def kernel_last(step, ids, links, part, params, got_a, got_b, out):
    flags = read_flags(ids, links)
    prev, nxt = in_order(flags[5], got_a[...], got_b[...])
    g0, g1 = own_gradient(flags, part[0], part[1], prev, nxt)
    out[0] = stepped(step, params[0], g0)
    out[1] = jnp.where(flags[0], stepped(step, params[1], g1), params[1])


def kernel_arrange(tb, slots, weights, kernels, order, out_a, out_b, out_0, padded):
    half, nf = tb.half, tb.nf
    frows, wl = 2 * half + 8, 2 * nf
    bands = kernels.shape[3]
    zb = wl // (2 * slots)
    lane = lane_of((frows, wl))
    inner = lax.rem(lane, zb)
    roots = jnp.sqrt(weights[...])
    zeros = [jnp.zeros((frows, wl), F32) for _ in range(2)]
    padded[...] = jnp.zeros(padded.shape, F32)
    for k in range(kernels.shape[0]):
        root = jnp.broadcast_to(roots[:, k : k + 1], (1, bands))
        for part in range(2):
            padded[k, part, :bands, :bands] = kernels[k, part] * root
    for k in range(kernels.shape[0]):
        for part in range(2):
            high, low = split(padded[k, part])
            v = dot(order[...], high) + dot(order[...], low)
            zero = jnp.broadcast_to(v[:, half : half + 1], (frows, wl))
            zeros[part] = jnp.where(inner == k, zero, zeros[part])
            v = jnp.where(lane < half, v, pltpu.roll(v, wl - 1, 1))
            v = jnp.where(lane < nf, v, pltpu.roll(v, nf, 1))
            if part == 0:
                out_a[k] = v
            else:
                out_b[k] = -conj(v, nf)
    out_0[0] = zeros[0]
    out_0[1] = -conj(zeros[1], zb)


def kernel_choose(ids, params, send_a, send_b, ids_s, params_v, sems):
    move_ids = pltpu.make_async_copy(ids, ids_s, sems.at[0])
    move = pltpu.make_async_copy(params, params_v, sems.at[1])
    move_ids.start()
    move.start()
    move_ids.wait()
    move.wait()
    even = lax.rem(lax.axis_index("grp"), 2) == 0
    last = jnp.where(ids_s[1] >= 0, params_v[1], params_v[0])
    send_a[...], send_b[...] = in_order(even, last, params_v[0])


def choose(tile_ids, mask_params):
    tile = mask_params.shape[1:]
    anywhere = pl.BlockSpec(memory_space=pltpu.HBM)
    return pl.pallas_call(
        kernel_choose,
        in_specs=[anywhere] * 2,
        out_specs=[pl.BlockSpec(memory_space=pltpu.VMEM)] * 2,
        out_shape=[jax.ShapeDtypeStruct(tile, F32)] * 2,
        scratch_shapes=[
            pltpu.SMEM(tile_ids.shape, jnp.int32),
            pltpu.VMEM(mask_params.shape, F32),
            pltpu.SemaphoreType.DMA((2,)),
        ],
        compiler_params=pltpu.CompilerParams(vmem_limit_bytes=4 << 20),
    )(*(pltpu.with_memory_space_constraint(v, pltpu.HBM) for v in (tile_ids, mask_params)))


def call(body, ins, outs, scratch=(), scalars=2, limit=32 << 20, moved=()):
    smem = pl.BlockSpec(memory_space=pltpu.SMEM)
    vmem = pl.BlockSpec(memory_space=pltpu.VMEM)
    return pl.pallas_call(
        body,
        in_specs=[smem] * scalars + [vmem] * (len(ins) - scalars),
        out_specs=[
            pl.BlockSpec(memory_space=pltpu.HBM) if i in moved else vmem for i in range(len(outs))
        ],
        out_shape=[jax.ShapeDtypeStruct(s, F32) for s in outs],
        scratch_shapes=list(scratch),
        compiler_params=pltpu.CompilerParams(vmem_limit_bytes=limit),
    )(*ins)


def local(mesh_shape, mask_params, target, weight, kernels, kernel_weight, tile_ids, tile_links):
    slots, rows, cols = mask_params.shape
    bands = kernels.shape[2]
    kcount = kernels.shape[0]
    groups, count = mesh_shape
    step = STEP_SCALE * math.sqrt(rows * cols)
    tb = Tables(rows, cols, bands)
    names = tuple(tb.arrays)
    tables = [jnp.asarray(tb.arrays[n]) for n in names]
    axes = ("grp", "tile")

    ring_a = snake_ring(groups, count, 1)
    ring_b = snake_ring(groups, count, -1)

    def exchange(a, b):
        return lax.ppermute(a, axes, ring_a), lax.ppermute(b, axes, ring_b)

    got = exchange(*choose(tile_ids, mask_params))
    frows = 2 * tb.half + 8
    arranged = call(
        functools.partial(kernel_arrange, tb, slots),
        [kernel_weight[None], kernels, jnp.asarray(tb.order)],
        [(kcount, frows, 2 * tb.nf)] * 2 + [(2, frows, 2 * tb.nf)],
        [pltpu.VMEM((kcount, 2, frows, 2 * tb.nf), F32)],
        scalars=0,
    )
    field = pltpu.VMEM((slots, kcount, rows, 2 * cols), F32)
    whole, tile = mask_params.shape, (rows, cols)
    part, sa, sb = call(
        functools.partial(kernel_first, tb, names),
        [tile_ids, tile_links, mask_params, *got, target, weight, *arranged, *tables],
        [whole, tile, tile],
        [field],
    )
    params, sa, sb = call(
        functools.partial(kernel_update, step),
        [tile_ids, tile_links, part, mask_params, *exchange(sa, sb)],
        [whole, tile, tile],
    )
    part, resist, sa, sb = call(
        functools.partial(kernel_second, tb, names),
        [tile_ids, tile_links, params, *exchange(sa, sb), target, weight, *arranged, *tables],
        [whole, whole, tile, tile],
        [field, pltpu.VMEM(whole, F32), pltpu.SemaphoreType.DMA((slots,))],
        moved=(1,),
    )
    (out,) = call(
        functools.partial(kernel_last, step),
        [tile_ids, tile_links, part, params, *exchange(sa, sb)],
        [whole],
    )
    return (out, resist)


def solution(mesh):
    tiles = P(("grp", "tile"), None, None)
    return jax.shard_map(
        functools.partial(local, (mesh.shape["grp"], mesh.shape["tile"])),
        mesh=mesh,
        in_specs=(tiles, tiles, tiles, P(), P(), P(("grp", "tile")), P(("grp", "tile"), None)),
        out_specs=(tiles, tiles),
        check_vma=False,
    )
```

```python
import functools
import math

import jax
import jax.numpy as jnp
import numpy as np
from jax import lax
from jax.experimental import pallas as pl
from jax.experimental.pallas import tpu as pltpu
from jax.sharding import PartitionSpec as P

ITERS = 2
RESIST_SLOPE = 4.0
THRESHOLD = 0.9
STEP_SCALE = 0.04
GROUP = 8
FIRST = 6
MID = 16
F32 = jnp.float32
BF16 = jnp.bfloat16


def snake_ring(groups, count, step):
    order = []
    for g in range(groups):
        span = range(count) if g % 2 == 0 else range(count - 1, -1, -1)
        order += [g * count + i for i in span]
    total = len(order)
    return [(order[j], order[(j + step) % total]) for j in range(total)]


def split_np(table):
    table = np.asarray(table, np.float32)
    high = table.astype(jnp.bfloat16)
    low = (table - high.astype(np.float32)).astype(jnp.bfloat16)
    return high, low


class Tables:
    def __init__(self, rows, cols, bands):
        half = (bands - 1) // 2
        self.half = half
        area = 1.0 / (rows * cols)
        self.area = area
        pos = np.arange(1, half + 1)
        angle = (np.arange(rows)[:, None] * pos[None, :] % (2 * rows)) * (np.pi / rows)
        ty = np.zeros((rows, 2 * half + MID))
        ty[:, :half] = np.cos(angle)
        ty[:, half] = 1.0
        ty[:, half + MID :] = np.sin(angle)
        freq = np.concatenate([np.arange(-half, 0), np.arange(1, half + 1)])
        self.nf = len(freq)
        period = 3 * cols
        theta = (np.arange(period)[:, None] * freq[None, :] % period) * (2.0 * np.pi / period)
        c, s = np.cos(theta), np.sin(theta)
        co, so = c[cols : 2 * cols].T, s[cols : 2 * cols].T
        forward = np.block([[co, so], [-so, co]])
        adjoint = np.block([[co.T, so.T], [so.T, -co.T]])
        gradient = np.concatenate([c.T, s.T], 0) * (2.0 * area)
        spectrum = np.concatenate([c, -s], 1) * area

        def left(table):
            h, l = split_np(table)
            return np.concatenate([h, h, l], 1)

        def right(table):
            h, l = split_np(table)
            return np.concatenate([h, h, l], 0)

        part = np.arange(2 * self.nf) // (self.nf // 2) % 2
        ones = np.zeros((2 * self.nf, 2 * cols))
        ones[part == 0, :cols] = 1.0
        ones[part == 1, cols:] = 1.0
        sums = np.concatenate([ones.T, ones.T, np.zeros_like(ones.T)], 0).astype(jnp.bfloat16)
        sums[cols : 2 * cols] *= -1
        sums[3 * cols : 4 * cols] *= -1
        picks = np.zeros((self.nf // 2, MID, 2 * self.nf), jnp.bfloat16)
        for k in range(self.nf // 2):
            picks[k, :, k :: self.nf // 2] = 1.0

        def wide(table):
            h, l = split_np(table)
            top = np.concatenate([h, l], 1)
            return np.concatenate([top, np.concatenate([h, np.zeros_like(l)], 1)], 0)

        self.arrays = dict(
            ty=left(ty),
            tyt=left(ty.T),
            fwd=np.concatenate([right(forward), ones.astype(jnp.bfloat16)], 0),
            picks=picks,
            adj=np.concatenate([right(adjoint), sums], 1),
            grad=right(gradient),
            spec=np.stack([wide(spectrum[j * cols : (j + 1) * cols]) for j in range(3)]),
        )
        order = np.zeros((2 * half + 8, 2 * half + 8), jnp.bfloat16)
        for j in range(half):
            order[j, half + 1 + j] = 1.0
            order[half + 8 + j, half - 1 - j] = 1.0
        order[half, half] = 1.0
        self.order = order


def split(v):
    high = v.astype(BF16)
    return high, (v - high.astype(F32)).astype(BF16)


def dot(a, b):
    return jnp.dot(a, b, preferred_element_type=F32)


def lanes3(v):
    high, low = split(v)
    return jnp.concatenate([high, low, high], 1)


def rows3(v):
    high, low = split(v)
    return jnp.concatenate([high, low, high], 0)


def wide_dot(v, table):
    high, low = split(v)
    o = dot(jnp.concatenate([high, low], 1), table)
    n = o.shape[1] // 2
    return o[:, :n] + o[:, n:]


def lane_of(shape):
    return lax.broadcasted_iota(jnp.int32, shape, 1)


def swap(v, block):
    n = v.shape[1]
    if 2 * block == n:
        return pltpu.roll(v, block, 1)
    even = lax.rem(lax.div(lane_of(v.shape), block), 2) == 0
    return jnp.where(even, pltpu.roll(v, n - block, 1), pltpu.roll(v, block, 1))


def conj(v, block):
    even = lax.rem(lax.div(lane_of((1, v.shape[1])), block), 2) == 0
    return v * jnp.where(even, 1.0, -1.0)


def minus_i(v, block):
    return conj(swap(v, block), block)


def fold(half, plus, zero, minus):
    gap = jnp.zeros((MID - 8, plus.shape[1]), F32)
    return jnp.concatenate([plus, zero, gap, minus], 0)


def spread(half, o, block):
    cosine, zero, sine = o[:half], o[half : half + 8], minus_i(o[half + MID :], block)
    return jnp.concatenate([cosine + sine, zero, cosine - sine], 0)


def drive(half, a, b, u):
    p, m = slice(0, half), slice(half + 8, 2 * half + 8)
    d = a * u[0] + b * u[1]
    turned_p = a[p] * u[2][p] + b[p] * u[3][p]
    turned_m = a[m] * u[2][m] + b[m] * u[3][m]
    return fold(half, d[p] + d[m], d[half : half + 8], turned_p - turned_m)


def phases(u, block):
    v = swap(u, block)
    return u, v, -conj(v, block), conj(u, block)


def gather(half, q, a, b, o, block):
    p, z, m = slice(0, half), slice(half, half + 8), slice(half + 8, 2 * half + 8)
    c, zero, s = o[:half], o[half : half + 8], conj(o[half + MID :], block)
    parts = [
        a[p] * c + b[p] * s,
        a[z] * zero,
        a[m] * c - b[m] * s,
        b[p] * c - a[p] * s,
        b[z] * zero,
        b[m] * c + a[m] * s,
    ]
    return parts if q is None else [x + y for x, y in zip(q, parts)]


def back_rows(half, q, block):
    p, z, m = (q[j] - swap(q[j + 3], block) for j in range(3))
    return fold(half, p + m, z, minus_i(p - m, block))


def lane_sum(v):
    return jnp.sum(v, axis=1, keepdims=True)


class Spectra:
    def __init__(self, refs):
        self.runs = (refs[:2], refs[3:5])
        self.zeros = (refs[2], refs[5])
        self.count = sum(run[0].shape[0] for run in self.runs)

    def __getitem__(self, k):
        first = self.runs[0][0].shape[0]
        run, k = (self.runs[0], k) if k < first else (self.runs[1], k - first)
        return run[0][k], run[1][k]

    def at_zero(self):
        return [self.zeros[0][i] + self.zeros[1][i] for i in range(2)]


def core(tb, dom, target, weight, spectra, t, e_ref, keep=None):
    half, nf = tb.half, tb.nf
    slots, rows, cols = target.shape
    kcount = spectra.count
    wl = 2 * nf
    zb = wl // (2 * slots)
    ty, tyt = t["ty"], t["tyt"]
    thirds_of = [dom[:, j * cols : (j + 1) * cols] for j in range(3)]
    g = sum(wide_dot(v, t["spec"][j]) for j, v in enumerate(thirds_of))
    gw = jnp.concatenate([g[s * rows : (s + 1) * rows] for s in range(slots)], 1)
    spec = dot(tyt[...], rows3(gw))
    us = [phases(spread(half, spec[:, s * wl : (s + 1) * wl], nf), nf) for s in range(slots)]
    g0 = lane_sum(thirds_of[0] + thirds_of[1] + thirds_of[2]) * tb.area
    block = lax.div(lane_of((rows, wl)), zb)
    g0w = jnp.zeros((rows, wl), F32)
    for s in range(slots):
        g0w = jnp.where(block == 2 * s, g0[s * rows : (s + 1) * rows], g0w)
    u0 = phases(spread(half, dot(tyt[...], rows3(g0w)), zb), zb)
    a0, b0 = spectra.at_zero()
    r0 = dot(ty[...], rows3(drive(half, a0, b0, u0)))
    r0h, r0l = split(r0)
    r0l = pltpu.roll(r0l.astype(F32), wl // 2, 1)
    r0s = [
        jnp.where(lax.div(block, 2) == s, r0h.astype(F32), r0l).astype(BF16) for s in range(slots)
    ]
    inner = lax.rem(lane_of((rows, wl)), zb)
    groups = [range(k0, min(k0 + GROUP, kcount)) for k0 in range(0, kcount, GROUP)]

    def in_pairs(ks):
        return [ks[i : i + 2] for i in range(0, len(ks), 2)]

    def row_stage(s, ks):
        out, extra = [], []
        for pair in in_pairs(ks):
            w = jnp.concatenate([drive(half, *spectra[k], us[s]) for k in pair], 1)
            r = dot(ty[...], rows3(w))
            for n, k in enumerate(pair):
                out.append(r[:, n * wl : (n + 1) * wl])
                extra += [r0s[s][i : i + MID] * t["picks"][k] for i in range(0, rows, MID)]
        return jnp.concatenate([lanes3(jnp.concatenate(out, 0)), jnp.concatenate(extra, 0)], 1)

    def field_stage(s, ks, ready, inten):
        field = dot(ready, t["fwd"][...])
        for n, k in enumerate(ks):
            e = field[n * rows : (n + 1) * rows]
            e_ref[s, k] = e
            inten = inten + (e[:, :cols] * e[:, :cols] + e[:, cols:] * e[:, cols:])
        return inten

    def slope_of(s, inten):
        resist = jax.nn.sigmoid(RESIST_SLOPE * (inten - THRESHOLD))
        slope = 2.0 * weight[s] * (resist - target[s]) * RESIST_SLOPE * resist * (1.0 - resist)
        return resist, jnp.concatenate([slope, slope], 1)

    def column_stage(s, ks, slope2):
        back = jnp.concatenate([e_ref[s, k] * slope2 for k in ks], 0)
        return dot(lanes3(back), t["adj"][...])

    def sum_stage(s, ks, ready, c0, q):
        for m, pair in enumerate(in_pairs(ks)):
            parts = [ready[(2 * m + n) * rows : (2 * m + n + 1) * rows] for n in range(len(pair))]
            o = dot(tyt[...], rows3(jnp.concatenate([v[:, :wl] for v in parts], 1)))
            for n, k in enumerate(pair):
                c0 = jnp.where(inner == k, parts[n][:, wl:], c0)
                q = gather(half, q, *spectra[k], o[:, n * wl : (n + 1) * wl], nf)
        return c0, q

    def finish(s, c0, q):
        own = lax.div(block, 2) == s
        q0 = gather(half, None, a0, b0, dot(tyt[...], rows3(jnp.where(own, c0, 0.0))), zb)
        ug = dot(ty[...], rows3(back_rows(half, q, nf)))
        ug0 = dot(ty[...], rows3(back_rows(half, q0, zb)))
        flat = lane_sum(jnp.where(block == 2 * s, ug0, 0.0))
        return dot(lanes3(ug), t["grad"][...]) + (2.0 * tb.area) * flat

    grads = []
    slope2 = None
    for s in range(slots + 1):
        forward, backward = s < slots, s > 0
        inten = jnp.zeros((rows, cols), F32)
        c0, q = jnp.zeros((rows, wl), F32), None
        ahead_f = row_stage(s, groups[0]) if forward else None
        ahead_b = column_stage(s - 1, groups[0], slope2) if backward else None
        for j, ks in enumerate(groups):
            now_f, now_b = ahead_f, ahead_b
            more = j + 1 < len(groups)
            if forward and more:
                ahead_f = row_stage(s, groups[j + 1])
            if backward and more:
                ahead_b = column_stage(s - 1, groups[j + 1], slope2)
            if forward:
                inten = field_stage(s, ks, now_f, inten)
            if backward:
                c0, q = sum_stage(s - 1, ks, now_b, c0, q)
        if backward:
            grads.append(finish(s - 1, c0, q))
        if forward:
            resist, slope2 = slope_of(s, inten)
            if keep is not None:
                keep(s, resist)
    return grads


def read_flags(flags, shape):
    return tuple(jnp.broadcast_to(flags[i : i + 1], shape) > 0.5 for i in range(6))


def in_order(even, first, second):
    return jnp.where(even, first, second), jnp.where(even, second, first)


def domain_of(flags, prev, own0, own1, nxt):
    both, l0, l1, r0, r1, _ = flags
    zero = jnp.zeros_like(own0)
    first = [jnp.where(l0, prev, zero), own0, jnp.where(r0, jnp.where(both, own1, nxt), zero)]
    second = [jnp.where(l1, own0, zero), own1, jnp.where(r1, nxt, zero)]
    return jnp.concatenate([jnp.concatenate(first, 1), jnp.concatenate(second, 1)], 0)


def thirds(flags, dg):
    both, l0, l1, r0, r1, _ = flags
    cols = dg[0].shape[1] // 3
    left0, mid0, right0 = (dg[0][:, j * cols : (j + 1) * cols] for j in range(3))
    left1, mid1, right1 = (dg[1][:, j * cols : (j + 1) * cols] for j in range(3))
    part0 = mid0 + jnp.where(jnp.logical_and(r0, both), left1, 0.0)
    part1 = mid1 + jnp.where(l1, right0, 0.0)
    return part0, part1, jnp.where(both, right1, right0), left0


def own_gradient(flags, part0, part1, from_prev, from_next):
    both, l0, l1, r0, r1, _ = flags
    g0 = part0 + jnp.where(l0, from_prev, 0.0)
    g0 = g0 + jnp.where(jnp.logical_and(r0, jnp.logical_not(both)), from_next, 0.0)
    return g0, part1 + jnp.where(jnp.logical_and(r1, both), from_next, 0.0)


def stepped(step, params, gradient):
    transmit = jnp.tanh(params)
    return params - step * gradient * (1.0 - transmit * transmit)


def kernel_first(tb, names, marks, mp, got_a, got_b, target, weight, *rest):
    spectra, rest = Spectra(rest[:6]), rest[6:]
    t = dict(zip(names, rest))
    part, send_a, send_b, e_ref = rest[len(names) :]
    flags = read_flags(marks, got_a.shape)
    prev, nxt = in_order(flags[5], got_a[...], got_b[...])
    tile = [jnp.tanh(v) for v in (prev, mp[0], mp[1], nxt)]
    dg = core(tb, domain_of(flags, *tile), target, weight, spectra, t, e_ref)
    part[0], part[1], to_next, to_prev = thirds(flags, dg)
    send_a[...], send_b[...] = in_order(flags[5], to_next, to_prev)


def kernel_update(step, marks, part, params, got_a, got_b, out, send_a, send_b):
    flags = read_flags(marks, got_a.shape)
    prev, nxt = in_order(flags[5], got_a[...], got_b[...])
    g0, g1 = own_gradient(flags, part[0], part[1], prev, nxt)
    new0 = stepped(step, params[0], g0)
    new1 = jnp.where(flags[0], stepped(step, params[1], g1), params[1])
    out[0], out[1] = new0, new1
    send_a[...], send_b[...] = in_order(flags[5], jnp.where(flags[0], new1, new0), new0)


def kernel_second(tb, names, marks, mp, got_a, got_b, target, weight, *rest):
    spectra, rest = Spectra(rest[:6]), rest[6:]
    t = dict(zip(names, rest))
    part, resist_out, send_a, send_b, e_ref, resist_v, sems = rest[len(names) :]
    flags = read_flags(marks, got_a.shape)
    prev, nxt = in_order(flags[5], got_a[...], got_b[...])
    tile = [jnp.tanh(v) for v in (prev, mp[0], mp[1], nxt)]
    moves = []

    def keep(s, resist):
        resist_v[s] = resist if s == 0 else jnp.where(flags[0], resist, 0.0)
        moves.append(pltpu.make_async_copy(resist_v.at[s], resist_out.at[s], sems.at[s]))
        moves[-1].start()

    dg = core(tb, domain_of(flags, *tile), target, weight, spectra, t, e_ref, keep)
    part[0], part[1], to_next, to_prev = thirds(flags, dg)
    send_a[...], send_b[...] = in_order(flags[5], to_next, to_prev)
    for move in moves:
        move.wait()


def kernel_last(step, marks, part, params, got_a, got_b, out):
    flags = read_flags(marks, got_a.shape)
    prev, nxt = in_order(flags[5], got_a[...], got_b[...])
    g0, g1 = own_gradient(flags, part[0], part[1], prev, nxt)
    out[0] = stepped(step, params[0], g0)
    out[1] = jnp.where(flags[0], stepped(step, params[1], g1), params[1])


def kernel_arrange(tb, slots, span, weights, kernels, order, carried, out_a, out_b, out_0, passed, padded):
    half, nf = tb.half, tb.nf
    frows, wl = 2 * half + 8, 2 * nf
    bands = kernels.shape[3]
    zb = wl // (2 * slots)
    lane = lane_of((frows, wl))
    inner = lax.rem(lane, zb)
    roots = jnp.sqrt(weights[...])
    zeros = [jnp.zeros((frows, wl), F32) for _ in range(2)]
    padded[...] = jnp.zeros(padded.shape, F32)
    for n, k in enumerate(span):
        root = jnp.broadcast_to(roots[:, k : k + 1], (1, bands))
        for part in range(2):
            padded[n, part, :bands, :bands] = kernels[k, part] * root
    for n, k in enumerate(span):
        for part in range(2):
            high, low = split(padded[n, part])
            v = dot(order[...], high) + dot(order[...], low)
            zero = jnp.broadcast_to(v[:, half : half + 1], (frows, wl))
            zeros[part] = jnp.where(inner == k, zero, zeros[part])
            v = jnp.where(lane < half, v, pltpu.roll(v, wl - 1, 1))
            v = jnp.where(lane < nf, v, pltpu.roll(v, nf, 1))
            if part == 0:
                out_a[n] = v
            else:
                out_b[n] = -conj(v, nf)
    out_0[0] = zeros[0]
    out_0[1] = -conj(zeros[1], zb)
    passed[...] = carried[...]


def kernel_choose(ids, links, params, marks, send_a, send_b, ids_s, links_s, params_v, sems):
    moves = [
        pltpu.make_async_copy(source, target, sems.at[i])
        for i, (source, target) in enumerate(((ids, ids_s), (links, links_s), (params, params_v)))
    ]
    for move in moves:
        move.start()
    for move in moves:
        move.wait()
    both = ids_s[1] >= 0
    even = lax.rem(lax.axis_index("grp"), 2) == 0
    last = jnp.where(both, params_v[1], params_v[0])
    send_a[...], send_b[...] = in_order(even, last, params_v[0])
    flags = [both] + [links_s[s, side] == 1 for side in range(2) for s in range(2)] + [even]
    row = lax.broadcasted_iota(jnp.int32, marks.shape, 0)
    out = jnp.zeros(marks.shape, F32)
    for i, flag in enumerate(flags):
        out = jnp.where(row == i, jnp.where(flag, 1.0, 0.0), out)
    marks[...] = out


def choose(*ins):
    tile_ids, tile_links, mask_params = ins
    tile = mask_params.shape[1:]
    far = pl.BlockSpec(memory_space=pltpu.HBM)
    return pl.pallas_call(
        kernel_choose,
        in_specs=[far] * 3,
        out_specs=[pl.BlockSpec(memory_space=pltpu.VMEM)] * 3,
        out_shape=[jax.ShapeDtypeStruct(s, F32) for s in ((8, tile[1]), tile, tile)],
        scratch_shapes=[
            pltpu.SMEM(tile_ids.shape, jnp.int32),
            pltpu.SMEM(tile_links.shape, jnp.int32),
            pltpu.VMEM(mask_params.shape, F32),
            pltpu.SemaphoreType.DMA((3,)),
        ],
        compiler_params=pltpu.CompilerParams(vmem_limit_bytes=4 << 20),
    )(*(pltpu.with_memory_space_constraint(v, pltpu.HBM) for v in ins))


def call(body, ins, outs, scratch=(), limit=32 << 20, moved=()):
    vmem = pl.BlockSpec(memory_space=pltpu.VMEM)
    return pl.pallas_call(
        body,
        in_specs=[vmem] * len(ins),
        out_specs=[
            pl.BlockSpec(memory_space=pltpu.HBM) if i in moved else vmem for i in range(len(outs))
        ],
        out_shape=[jax.ShapeDtypeStruct(s, F32) for s in outs],
        scratch_shapes=list(scratch),
        compiler_params=pltpu.CompilerParams(vmem_limit_bytes=limit),
    )(*ins)


def local(mesh_shape, mask_params, target, weight, kernels, kernel_weight, tile_ids, tile_links):
    slots, rows, cols = mask_params.shape
    bands = kernels.shape[2]
    kcount = kernels.shape[0]
    groups, count = mesh_shape
    step = STEP_SCALE * math.sqrt(rows * cols)
    tb = Tables(rows, cols, bands)
    names = tuple(tb.arrays)
    tables = [jnp.asarray(tb.arrays[n]) for n in names]
    axes = ("grp", "tile")

    ring_a = snake_ring(groups, count, 1)
    ring_b = snake_ring(groups, count, -1)

    def exchange(a, b):
        return lax.ppermute(a, axes, ring_a), lax.ppermute(b, axes, ring_b)

    frows = 2 * tb.half + 8
    whole, tile = mask_params.shape, (rows, cols)

    def arrange(span, carried):
        return call(
            functools.partial(kernel_arrange, tb, slots, span),
            [kernel_weight[None], kernels, jnp.asarray(tb.order), carried],
            [(len(span), frows, 2 * tb.nf)] * 2 + [(2, frows, 2 * tb.nf), carried.shape],
            [pltpu.VMEM((len(span), 2, frows, 2 * tb.nf), F32)],
        )

    marks, sa, sb = choose(tile_ids, tile_links, mask_params)
    *early, sb = arrange(range(FIRST), sb)
    *late, marks = arrange(range(FIRST, kcount), marks)
    got = exchange(sa, sb)
    arranged = early + late
    field = pltpu.VMEM((slots, kcount, rows, 2 * cols), F32)
    part, sa, sb = call(
        functools.partial(kernel_first, tb, names),
        [marks, mask_params, *got, target, weight, *arranged, *tables],
        [whole, tile, tile],
        [field],
    )
    params, sa, sb = call(
        functools.partial(kernel_update, step),
        [marks, part, mask_params, *exchange(sa, sb)],
        [whole, tile, tile],
    )
    part, resist, sa, sb = call(
        functools.partial(kernel_second, tb, names),
        [marks, params, *exchange(sa, sb), target, weight, *arranged, *tables],
        [whole, whole, tile, tile],
        [field, pltpu.VMEM(whole, F32), pltpu.SemaphoreType.DMA((slots,))],
        moved=(1,),
    )
    (out,) = call(
        functools.partial(kernel_last, step),
        [marks, part, params, *exchange(sa, sb)],
        [whole],
    )
    return (out, resist)


def solution(mesh):
    tiles = P(("grp", "tile"), None, None)
    return jax.shard_map(
        functools.partial(local, (mesh.shape["grp"], mesh.shape["tile"])),
        mesh=mesh,
        in_specs=(tiles, tiles, tiles, P(), P(), P(("grp", "tile")), P(("grp", "tile"), None)),
        out_specs=(tiles, tiles),
        check_vma=False,
    )
```

```python
import functools
import math

import jax
import jax.numpy as jnp
import numpy as np
from jax import lax
from jax.experimental import pallas as pl
from jax.experimental.pallas import tpu as pltpu
from jax.sharding import PartitionSpec as P

ITERS = 2
RESIST_SLOPE = 4.0
THRESHOLD = 0.9
STEP_SCALE = 0.04
GROUP = 8
RUN = 4
MID = 16
F32 = jnp.float32
BF16 = jnp.bfloat16


def snake_ring(groups, count, step):
    order = []
    for g in range(groups):
        span = range(count) if g % 2 == 0 else range(count - 1, -1, -1)
        order += [g * count + i for i in span]
    total = len(order)
    return [(order[j], order[(j + step) % total]) for j in range(total)]


def split_np(table):
    table = np.asarray(table, np.float32)
    high = table.astype(jnp.bfloat16)
    low = (table - high.astype(np.float32)).astype(jnp.bfloat16)
    return high, low


class Tables:
    def __init__(self, rows, cols, bands):
        half = (bands - 1) // 2
        self.half = half
        area = 1.0 / (rows * cols)
        self.area = area
        pos = np.arange(1, half + 1)
        angle = (np.arange(rows)[:, None] * pos[None, :] % (2 * rows)) * (np.pi / rows)
        ty = np.zeros((rows, 2 * half + MID))
        ty[:, :half] = np.cos(angle)
        ty[:, half] = 1.0
        ty[:, half + MID :] = np.sin(angle)
        freq = np.concatenate([np.arange(-half, 0), np.arange(1, half + 1)])
        self.nf = len(freq)
        period = 3 * cols
        theta = (np.arange(period)[:, None] * freq[None, :] % period) * (2.0 * np.pi / period)
        c, s = np.cos(theta), np.sin(theta)
        co, so = c[cols : 2 * cols].T, s[cols : 2 * cols].T
        forward = np.block([[co, so], [-so, co]])
        adjoint = np.block([[co.T, so.T], [so.T, -co.T]])
        gradient = np.concatenate([c.T, s.T], 0) * (2.0 * area)
        spectrum = np.concatenate([c, -s], 1) * area

        def left(table):
            h, l = split_np(table)
            return np.concatenate([h, h, l], 1)

        def right(table):
            h, l = split_np(table)
            return np.concatenate([h, h, l], 0)

        part = np.arange(2 * self.nf) // (self.nf // 2) % 2
        ones = np.zeros((2 * self.nf, 2 * cols))
        ones[part == 0, :cols] = 1.0
        ones[part == 1, cols:] = 1.0
        sums = np.concatenate([ones.T, ones.T, np.zeros_like(ones.T)], 0).astype(jnp.bfloat16)
        sums[cols : 2 * cols] *= -1
        sums[3 * cols : 4 * cols] *= -1
        picks = np.zeros((self.nf // 2, MID, 2 * self.nf), jnp.bfloat16)
        for k in range(self.nf // 2):
            picks[k, :, k :: self.nf // 2] = 1.0

        def wide(table):
            h, l = split_np(table)
            top = np.concatenate([h, l], 1)
            return np.concatenate([top, np.concatenate([h, np.zeros_like(l)], 1)], 0)

        self.arrays = dict(
            ty=left(ty),
            tyt=left(ty.T),
            fwd=np.concatenate([right(forward), ones.astype(jnp.bfloat16)], 0),
            picks=picks,
            adj=np.concatenate([right(adjoint), sums], 1),
            grad=right(gradient),
            spec=np.stack([wide(spectrum[j * cols : (j + 1) * cols]) for j in range(3)]),
        )
        chunk = RUN * 2 * bands
        frows = 2 * half + 8
        self.window = 2 * frows
        order = np.zeros((RUN, 2 * frows, self.window), jnp.bfloat16)
        self.starts = []
        for j in range(RUN):
            start = min(2 * bands * j // 8 * 8, chunk - self.window)
            self.starts.append(start)
            for part in range(2):
                first = 2 * bands * j - start + part
                base = part * frows
                for f in range(half):
                    order[j, base + f, first + 2 * (half + 1 + f)] = 1.0
                    order[j, base + half + 8 + f, first + 2 * (half - 1 - f)] = 1.0
                order[j, base + half, first + 2 * half] = 1.0
        self.order = np.concatenate([order, order], 2)
        lanes = np.zeros((2 * self.nf, 4 * self.nf), jnp.bfloat16)
        for j, g in enumerate([*range(half), *range(half + 1, bands)]):
            lanes[g, j] = lanes[g, self.nf + j] = 1.0
        lanes[half, 2 * self.nf :] = 1.0
        self.lanes = np.concatenate([lanes, lanes], 0)


def split(v):
    high = v.astype(BF16)
    return high, (v - high.astype(F32)).astype(BF16)


def dot(a, b):
    return jnp.dot(a, b, preferred_element_type=F32)


def lanes3(v):
    high, low = split(v)
    return jnp.concatenate([high, low, high], 1)


def rows3(v):
    high, low = split(v)
    return jnp.concatenate([high, low, high], 0)


def wide_dot(v, table):
    high, low = split(v)
    o = dot(jnp.concatenate([high, low], 1), table)
    n = o.shape[1] // 2
    return o[:, :n] + o[:, n:]


def lane_of(shape):
    return lax.broadcasted_iota(jnp.int32, shape, 1)


def swap(v, block):
    n = v.shape[1]
    if 2 * block == n:
        return pltpu.roll(v, block, 1)
    even = lax.rem(lax.div(lane_of(v.shape), block), 2) == 0
    return jnp.where(even, pltpu.roll(v, n - block, 1), pltpu.roll(v, block, 1))


def conj(v, block):
    even = lax.rem(lax.div(lane_of((1, v.shape[1])), block), 2) == 0
    return v * jnp.where(even, 1.0, -1.0)


def minus_i(v, block):
    return conj(swap(v, block), block)


def fold(half, plus, zero, minus):
    gap = jnp.zeros((MID - 8, plus.shape[1]), F32)
    return jnp.concatenate([plus, zero, gap, minus], 0)


def spread(half, o, block):
    cosine, zero, sine = o[:half], o[half : half + 8], minus_i(o[half + MID :], block)
    return jnp.concatenate([cosine + sine, zero, cosine - sine], 0)


def drive(half, a, b, u):
    p, m = slice(0, half), slice(half + 8, 2 * half + 8)
    d = a * u[0] + b * u[1]
    turned_p = a[p] * u[2][p] + b[p] * u[3][p]
    turned_m = a[m] * u[2][m] + b[m] * u[3][m]
    return fold(half, d[p] + d[m], d[half : half + 8], turned_p - turned_m)


def phases(u, block):
    v = swap(u, block)
    return u, v, -conj(v, block), conj(u, block)


def gather(half, q, a, b, o, block):
    p, z, m = slice(0, half), slice(half, half + 8), slice(half + 8, 2 * half + 8)
    c, zero, s = o[:half], o[half : half + 8], conj(o[half + MID :], block)
    parts = [
        a[p] * c + b[p] * s,
        a[z] * zero,
        a[m] * c - b[m] * s,
        b[p] * c - a[p] * s,
        b[z] * zero,
        b[m] * c + a[m] * s,
    ]
    return parts if q is None else [x + y for x, y in zip(q, parts)]


def back_rows(half, q, block):
    p, z, m = (q[j] - swap(q[j + 3], block) for j in range(3))
    return fold(half, p + m, z, minus_i(p - m, block))


def lane_sum(v):
    return jnp.sum(v, axis=1, keepdims=True)


class Spectra:
    def __init__(self, real, imag, at_zero):
        self.real, self.imag, self.zero = real, imag, at_zero
        self.count = real.shape[0]

    def __getitem__(self, k):
        return self.real[k], self.imag[k]

    def at_zero(self):
        return self.zero[0], self.zero[1]


def core(tb, dom, target, weight, spectra, t, e_ref, keep=None):
    half, nf = tb.half, tb.nf
    slots, rows, cols = target.shape
    kcount = spectra.count
    wl = 2 * nf
    zb = wl // (2 * slots)
    ty, tyt = t["ty"], t["tyt"]
    thirds_of = [dom[:, j * cols : (j + 1) * cols] for j in range(3)]
    g = sum(wide_dot(v, t["spec"][j]) for j, v in enumerate(thirds_of))
    gw = jnp.concatenate([g[s * rows : (s + 1) * rows] for s in range(slots)], 1)
    spec = dot(tyt[...], rows3(gw))
    us = [phases(spread(half, spec[:, s * wl : (s + 1) * wl], nf), nf) for s in range(slots)]
    g0 = lane_sum(thirds_of[0] + thirds_of[1] + thirds_of[2]) * tb.area
    block = lax.div(lane_of((rows, wl)), zb)
    g0w = jnp.zeros((rows, wl), F32)
    for s in range(slots):
        g0w = jnp.where(block == 2 * s, g0[s * rows : (s + 1) * rows], g0w)
    u0 = phases(spread(half, dot(tyt[...], rows3(g0w)), zb), zb)
    a0, b0 = spectra.at_zero()
    r0 = dot(ty[...], rows3(drive(half, a0, b0, u0)))
    r0h, r0l = split(r0)
    r0l = pltpu.roll(r0l.astype(F32), wl // 2, 1)
    r0s = [
        jnp.where(lax.div(block, 2) == s, r0h.astype(F32), r0l).astype(BF16) for s in range(slots)
    ]
    inner = lax.rem(lane_of((rows, wl)), zb)
    groups = [range(k0, min(k0 + GROUP, kcount)) for k0 in range(0, kcount, GROUP)]

    def in_pairs(ks):
        return [ks[i : i + 2] for i in range(0, len(ks), 2)]

    def row_stage(s, ks):
        out, extra = [], []
        for pair in in_pairs(ks):
            w = jnp.concatenate([drive(half, *spectra[k], us[s]) for k in pair], 1)
            r = dot(ty[...], rows3(w))
            for n, k in enumerate(pair):
                out.append(r[:, n * wl : (n + 1) * wl])
                extra += [r0s[s][i : i + MID] * t["picks"][k] for i in range(0, rows, MID)]
        return jnp.concatenate([lanes3(jnp.concatenate(out, 0)), jnp.concatenate(extra, 0)], 1)

    def field_stage(s, ks, ready, inten):
        field = dot(ready, t["fwd"][...])
        for n, k in enumerate(ks):
            e = field[n * rows : (n + 1) * rows]
            e_ref[s, k] = e
            inten = inten + (e[:, :cols] * e[:, :cols] + e[:, cols:] * e[:, cols:])
        return inten

    def slope_of(s, inten):
        resist = jax.nn.sigmoid(RESIST_SLOPE * (inten - THRESHOLD))
        slope = 2.0 * weight[s] * (resist - target[s]) * RESIST_SLOPE * resist * (1.0 - resist)
        return resist, jnp.concatenate([slope, slope], 1)

    def column_stage(s, ks, slope2):
        back = jnp.concatenate([e_ref[s, k] * slope2 for k in ks], 0)
        return dot(lanes3(back), t["adj"][...])

    def sum_stage(s, ks, ready, c0, q):
        for m, pair in enumerate(in_pairs(ks)):
            parts = [ready[(2 * m + n) * rows : (2 * m + n + 1) * rows] for n in range(len(pair))]
            o = dot(tyt[...], rows3(jnp.concatenate([v[:, :wl] for v in parts], 1)))
            for n, k in enumerate(pair):
                c0 = jnp.where(inner == k, parts[n][:, wl:], c0)
                q = gather(half, q, *spectra[k], o[:, n * wl : (n + 1) * wl], nf)
        return c0, q

    def finish(s, c0, q):
        own = lax.div(block, 2) == s
        q0 = gather(half, None, a0, b0, dot(tyt[...], rows3(jnp.where(own, c0, 0.0))), zb)
        ug = dot(ty[...], rows3(back_rows(half, q, nf)))
        ug0 = dot(ty[...], rows3(back_rows(half, q0, zb)))
        flat = lane_sum(jnp.where(block == 2 * s, ug0, 0.0))
        return dot(lanes3(ug), t["grad"][...]) + (2.0 * tb.area) * flat

    grads = []
    slope2 = None
    for s in range(slots + 1):
        forward, backward = s < slots, s > 0
        inten = jnp.zeros((rows, cols), F32)
        c0, q = jnp.zeros((rows, wl), F32), None
        ahead_f = row_stage(s, groups[0]) if forward else None
        ahead_b = column_stage(s - 1, groups[0], slope2) if backward else None
        for j, ks in enumerate(groups):
            now_f, now_b = ahead_f, ahead_b
            more = j + 1 < len(groups)
            if forward and more:
                ahead_f = row_stage(s, groups[j + 1])
            if backward and more:
                ahead_b = column_stage(s - 1, groups[j + 1], slope2)
            if forward:
                inten = field_stage(s, ks, now_f, inten)
            if backward:
                c0, q = sum_stage(s - 1, ks, now_b, c0, q)
        if backward:
            grads.append(finish(s - 1, c0, q))
        if forward:
            resist, slope2 = slope_of(s, inten)
            if keep is not None:
                keep(s, resist)
    return grads


def read_flags(flags, shape):
    return tuple(jnp.broadcast_to(flags[i : i + 1], shape) > 0.5 for i in range(6))


def in_order(even, first, second):
    return jnp.where(even, first, second), jnp.where(even, second, first)


def domain_of(flags, prev, own0, own1, nxt):
    both, l0, l1, r0, r1, _ = flags
    zero = jnp.zeros_like(own0)
    first = [jnp.where(l0, prev, zero), own0, jnp.where(r0, jnp.where(both, own1, nxt), zero)]
    second = [jnp.where(l1, own0, zero), own1, jnp.where(r1, nxt, zero)]
    return jnp.concatenate([jnp.concatenate(first, 1), jnp.concatenate(second, 1)], 0)


def thirds(flags, dg):
    both, l0, l1, r0, r1, _ = flags
    cols = dg[0].shape[1] // 3
    left0, mid0, right0 = (dg[0][:, j * cols : (j + 1) * cols] for j in range(3))
    left1, mid1, right1 = (dg[1][:, j * cols : (j + 1) * cols] for j in range(3))
    part0 = mid0 + jnp.where(jnp.logical_and(r0, both), left1, 0.0)
    part1 = mid1 + jnp.where(l1, right0, 0.0)
    return part0, part1, jnp.where(both, right1, right0), left0


def own_gradient(flags, part0, part1, from_prev, from_next):
    both, l0, l1, r0, r1, _ = flags
    g0 = part0 + jnp.where(l0, from_prev, 0.0)
    g0 = g0 + jnp.where(jnp.logical_and(r0, jnp.logical_not(both)), from_next, 0.0)
    return g0, part1 + jnp.where(jnp.logical_and(r1, both), from_next, 0.0)


def stepped(step, params, gradient):
    transmit = jnp.tanh(params)
    return params - step * gradient * (1.0 - transmit * transmit)


def kernel_first(tb, names, marks, mp, got_a, got_b, target, weight, *rest):
    spectra, rest = Spectra(*rest[:3]), rest[3:]
    t = dict(zip(names, rest))
    part, send_a, send_b, e_ref = rest[len(names) :]
    flags = read_flags(marks, got_a.shape)
    prev, nxt = in_order(flags[5], got_a[...], got_b[...])
    tile = [jnp.tanh(v) for v in (prev, mp[0], mp[1], nxt)]
    dg = core(tb, domain_of(flags, *tile), target, weight, spectra, t, e_ref)
    part[0], part[1], to_next, to_prev = thirds(flags, dg)
    send_a[...], send_b[...] = in_order(flags[5], to_next, to_prev)


def kernel_update(step, marks, part, params, got_a, got_b, out, send_a, send_b):
    flags = read_flags(marks, got_a.shape)
    prev, nxt = in_order(flags[5], got_a[...], got_b[...])
    g0, g1 = own_gradient(flags, part[0], part[1], prev, nxt)
    new0 = stepped(step, params[0], g0)
    new1 = jnp.where(flags[0], stepped(step, params[1], g1), params[1])
    out[0], out[1] = new0, new1
    send_a[...], send_b[...] = in_order(flags[5], jnp.where(flags[0], new1, new0), new0)


def kernel_second(tb, names, marks, mp, got_a, got_b, target, weight, *rest):
    spectra, rest = Spectra(*rest[:3]), rest[3:]
    t = dict(zip(names, rest))
    part, resist_out, send_a, send_b, e_ref, resist_v, sems = rest[len(names) :]
    flags = read_flags(marks, got_a.shape)
    prev, nxt = in_order(flags[5], got_a[...], got_b[...])
    tile = [jnp.tanh(v) for v in (prev, mp[0], mp[1], nxt)]
    moves = []

    def keep(s, resist):
        resist_v[s] = resist if s == 0 else jnp.where(flags[0], resist, 0.0)
        moves.append(pltpu.make_async_copy(resist_v.at[s], resist_out.at[s], sems.at[s]))
        moves[-1].start()

    dg = core(tb, domain_of(flags, *tile), target, weight, spectra, t, e_ref, keep)
    part[0], part[1], to_next, to_prev = thirds(flags, dg)
    send_a[...], send_b[...] = in_order(flags[5], to_next, to_prev)
    for move in moves:
        move.wait()


def kernel_last(step, marks, part, params, got_a, got_b, out):
    flags = read_flags(marks, got_a.shape)
    prev, nxt = in_order(flags[5], got_a[...], got_b[...])
    g0, g1 = own_gradient(flags, part[0], part[1], prev, nxt)
    out[0] = stepped(step, params[0], g0)
    out[1] = jnp.where(flags[0], stepped(step, params[1], g1), params[1])


def kernel_arrange(tb, slots, kernels, weights, order, lanes, out_a, out_b, out_0, padded):
    half, nf = tb.half, tb.nf
    frows, wl = 2 * half + 8, 2 * nf
    bands = kernels.shape[1]
    kcount = out_a.shape[0]
    zb = wl // (2 * slots)
    chunk = RUN * 2 * bands
    padded[...] = jnp.zeros(padded.shape, F32)
    inner = lax.rem(lane_of((frows, wl)), zb)
    sign = jnp.where(lane_of((1, wl)) < nf, -1.0, 1.0)
    zeros = [jnp.zeros((frows, wl), F32) for _ in range(2)]
    roots = jnp.sqrt(weights[...])

    def order_rows(i):
        found = {}
        for j in range(RUN):
            ks = (i * RUN + j, (i + 1) * RUN + j)
            for n, k in enumerate(ks):
                window = pl.ds((i + n) * chunk + tb.starts[j], tb.window)
                padded[k, :, :bands] = kernels[window, :]
            high, low = split(jnp.concatenate([padded[k] for k in ks], 1))
            v = dot(order[j], jnp.concatenate([high, low], 0))
            for n, k in enumerate(ks):
                root = jnp.broadcast_to(roots[:, k : k + 1], (1, wl))
                found[k] = v[:, n * wl : (n + 1) * wl] * root
        return found

    def order_lanes(found):
        ks = sorted(found)
        high, low = split(jnp.concatenate([found[k] for k in ks], 0))
        v = dot(jnp.concatenate([high, low], 1), lanes[...])
        for n, k in enumerate(ks):
            real = v[2 * n * frows : (2 * n + 1) * frows]
            imag = v[(2 * n + 1) * frows : (2 * n + 2) * frows]
            out_a[k] = real[:, :wl]
            out_b[k] = imag[:, :wl] * sign
            zeros[0] = jnp.where(inner == k, real[:, wl:], zeros[0])
            zeros[1] = jnp.where(inner == k, imag[:, wl:], zeros[1])

    waiting = None
    for i in range(0, kcount // RUN, 2):
        found = order_rows(i)
        if waiting is not None:
            order_lanes(waiting)
        waiting = found
    order_lanes(waiting)
    out_0[0] = zeros[0]
    out_0[1] = -conj(zeros[1], zb)


def arrange(tb, slots, parts, ins):
    bands, kcount = ins[0].shape[1], ins[1].shape[1]
    frows, wl = 2 * tb.half + 8, 2 * tb.nf
    return call(
        functools.partial(kernel_arrange, tb, slots),
        list(ins),
        [(kcount, frows, wl)] * 2 + [(2, frows, wl)],
        [pltpu.VMEM((kcount, parts * frows, wl), F32)],
    )


def kernel_choose(ids, links, params, *refs):
    count = (len(refs) - 7) // 2
    far, (marks, send_a, send_b) = refs[:count], refs[count : count + 3]
    near, (ids_s, links_s, params_v, sems) = refs[count + 3 : 2 * count + 3], refs[2 * count + 3 :]
    pairs = [(ids, ids_s), (links, links_s), (params, params_v), *zip(far, near)]
    moves = [pltpu.make_async_copy(*pair, sems.at[i]) for i, pair in enumerate(pairs)]
    for move in moves:
        move.start()
    for move in moves[:3]:
        move.wait()
    both = ids_s[1] >= 0
    even = lax.rem(lax.axis_index("grp"), 2) == 0
    last = jnp.where(both, params_v[1], params_v[0])
    send_a[...], send_b[...] = in_order(even, last, params_v[0])
    flags = [both] + [links_s[s, side] == 1 for side in range(2) for s in range(2)] + [even]
    row = lax.broadcasted_iota(jnp.int32, marks.shape, 0)
    out = jnp.zeros(marks.shape, F32)
    for i, flag in enumerate(flags):
        out = jnp.where(row == i, jnp.where(flag, 1.0, 0.0), out)
    marks[...] = out
    for move in moves[3:]:
        move.wait()


def choose(tile_ids, tile_links, mask_params, far):
    tile = mask_params.shape[1:]
    ins = (tile_ids, tile_links, mask_params, *far)
    shapes = [jax.ShapeDtypeStruct(s, F32) for s in ((8, tile[1]), tile, tile)]
    shapes += [jax.ShapeDtypeStruct(v.shape, v.dtype) for v in far]
    return pl.pallas_call(
        kernel_choose,
        in_specs=[pl.BlockSpec(memory_space=pltpu.HBM)] * len(ins),
        out_specs=[pl.BlockSpec(memory_space=pltpu.VMEM)] * len(shapes),
        out_shape=shapes,
        scratch_shapes=[
            pltpu.SMEM(tile_ids.shape, jnp.int32),
            pltpu.SMEM(tile_links.shape, jnp.int32),
            pltpu.VMEM(mask_params.shape, F32),
            pltpu.SemaphoreType.DMA((len(ins),)),
        ],
        compiler_params=pltpu.CompilerParams(vmem_limit_bytes=8 << 20),
    )(*(pltpu.with_memory_space_constraint(v, pltpu.HBM) for v in ins))


def call(body, ins, outs, scratch=(), limit=32 << 20, moved=()):
    vmem = pl.BlockSpec(memory_space=pltpu.VMEM)
    return pl.pallas_call(
        body,
        in_specs=[vmem] * len(ins),
        out_specs=[
            pl.BlockSpec(memory_space=pltpu.HBM) if i in moved else vmem for i in range(len(outs))
        ],
        out_shape=[jax.ShapeDtypeStruct(s, F32) for s in outs],
        scratch_shapes=list(scratch),
        compiler_params=pltpu.CompilerParams(vmem_limit_bytes=limit),
    )(*ins)


def local(mesh_shape, mask_params, target, weight, kernels, kernel_weight, tile_ids, tile_links):
    slots, rows, cols = mask_params.shape
    bands = kernels.shape[2]
    kcount = kernels.shape[0]
    groups, count = mesh_shape
    step = STEP_SCALE * math.sqrt(rows * cols)
    tb = Tables(rows, cols, bands)
    names = tuple(tb.arrays)
    tables = [jnp.asarray(tb.arrays[n]) for n in names]
    axes = ("grp", "tile")

    ring_a = snake_ring(groups, count, 1)
    ring_b = snake_ring(groups, count, -1)

    def exchange(a, b):
        return lax.ppermute(a, axes, ring_a), lax.ppermute(b, axes, ring_b)

    whole, tile = mask_params.shape, (rows, cols)

    flat = jnp.swapaxes(kernels, 1, 2).reshape(-1, bands)
    far = (flat, kernel_weight[None], jnp.asarray(tb.order), jnp.asarray(tb.lanes))
    marks, sa, sb, *near = choose(tile_ids, tile_links, mask_params, far)
    got = exchange(sa, sb)
    arranged = arrange(tb, slots, kernels.shape[1], near)
    field = pltpu.VMEM((slots, kcount, rows, 2 * cols), F32)
    part, sa, sb = call(
        functools.partial(kernel_first, tb, names),
        [marks, mask_params, *got, target, weight, *arranged, *tables],
        [whole, tile, tile],
        [field],
    )
    params, sa, sb = call(
        functools.partial(kernel_update, step),
        [marks, part, mask_params, *exchange(sa, sb)],
        [whole, tile, tile],
    )
    part, resist, sa, sb = call(
        functools.partial(kernel_second, tb, names),
        [marks, params, *exchange(sa, sb), target, weight, *arranged, *tables],
        [whole, whole, tile, tile],
        [field, pltpu.VMEM(whole, F32), pltpu.SemaphoreType.DMA((slots,))],
        moved=(1,),
    )
    (out,) = call(
        functools.partial(kernel_last, step),
        [marks, part, params, *exchange(sa, sb)],
        [whole],
    )
    return (out, resist)


def solution(mesh):
    tiles = P(("grp", "tile"), None, None)
    return jax.shard_map(
        functools.partial(local, (mesh.shape["grp"], mesh.shape["tile"])),
        mesh=mesh,
        in_specs=(tiles, tiles, tiles, P(), P(), P(("grp", "tile")), P(("grp", "tile"), None)),
        out_specs=(tiles, tiles),
        check_vma=False,
    )
```

```python
import functools
import math

import jax
import jax.numpy as jnp
import numpy as np
from jax import lax
from jax.experimental import pallas as pl
from jax.experimental.pallas import tpu as pltpu
from jax.sharding import PartitionSpec as P

ITERS = 2
RESIST_SLOPE = 4.0
THRESHOLD = 0.9
STEP_SCALE = 0.04
GROUP = 8
RUN = 4
MID = 16
F32 = jnp.float32
BF16 = jnp.bfloat16


def snake_ring(groups, count, step):
    order = []
    for g in range(groups):
        span = range(count) if g % 2 == 0 else range(count - 1, -1, -1)
        order += [g * count + i for i in span]
    total = len(order)
    return [(order[j], order[(j + step) % total]) for j in range(total)]


def split_np(table):
    table = np.asarray(table, np.float32)
    high = table.astype(jnp.bfloat16)
    low = (table - high.astype(np.float32)).astype(jnp.bfloat16)
    return high, low


class Tables:
    def __init__(self, rows, cols, bands):
        half = (bands - 1) // 2
        self.half = half
        area = 1.0 / (rows * cols)
        self.area = area
        pos = np.arange(1, half + 1)
        angle = (np.arange(rows)[:, None] * pos[None, :] % (2 * rows)) * (np.pi / rows)
        ty = np.zeros((rows, 2 * half + MID))
        ty[:, :half] = np.cos(angle)
        ty[:, half] = 1.0
        ty[:, half + MID :] = np.sin(angle)
        freq = np.concatenate([np.arange(-half, 0), np.arange(1, half + 1)])
        self.nf = len(freq)
        period = 3 * cols
        theta = (np.arange(period)[:, None] * freq[None, :] % period) * (2.0 * np.pi / period)
        c, s = np.cos(theta), np.sin(theta)
        co, so = c[cols : 2 * cols].T, s[cols : 2 * cols].T
        forward = np.block([[co, so], [-so, co]])
        adjoint = np.block([[co.T, so.T], [so.T, -co.T]])
        gradient = np.concatenate([c.T, s.T], 0) * (2.0 * area)
        spectrum = np.concatenate([c, -s], 1) * area

        def left(table):
            h, l = split_np(table)
            return np.concatenate([h, h, l], 1)

        def right(table):
            h, l = split_np(table)
            return np.concatenate([h, h, l], 0)

        part = np.arange(2 * self.nf) // (self.nf // 2) % 2
        ones = np.zeros((2 * self.nf, 2 * cols))
        ones[part == 0, :cols] = 1.0
        ones[part == 1, cols:] = 1.0
        sums = np.concatenate([ones.T, ones.T, np.zeros_like(ones.T)], 0).astype(jnp.bfloat16)
        sums[cols : 2 * cols] *= -1
        sums[3 * cols : 4 * cols] *= -1
        picks = np.zeros((self.nf // 2, MID, 2 * self.nf), jnp.bfloat16)
        for k in range(self.nf // 2):
            picks[k, :, k :: self.nf // 2] = 1.0

        def wide(table):
            h, l = split_np(table)
            top = np.concatenate([h, l], 1)
            return np.concatenate([top, np.concatenate([h, np.zeros_like(l)], 1)], 0)

        self.arrays = dict(
            ty=left(ty),
            tyt=left(ty.T),
            fwd=np.concatenate([right(forward), ones.astype(jnp.bfloat16)], 0),
            picks=picks,
            adj=wide(adjoint),
            grad=right(gradient),
            spec=np.stack([wide(spectrum[j * cols : (j + 1) * cols]) for j in range(3)]),
        )
        chunk = RUN * 2 * bands
        frows = 2 * half + 8
        self.window = 2 * frows
        order = np.zeros((RUN, 2 * frows, self.window), jnp.bfloat16)
        self.starts = []
        for j in range(RUN):
            start = min(2 * bands * j // 8 * 8, chunk - self.window)
            self.starts.append(start)
            for part in range(2):
                first = 2 * bands * j - start + part
                base = part * frows
                for f in range(half):
                    order[j, base + f, first + 2 * (half + 1 + f)] = 1.0
                    order[j, base + half + 8 + f, first + 2 * (half - 1 - f)] = 1.0
                order[j, base + half, first + 2 * half] = 1.0
        self.order = np.concatenate([order, order], 2)
        lanes = np.zeros((2 * self.nf, 4 * self.nf), jnp.bfloat16)
        for j, g in enumerate([*range(half), *range(half + 1, bands)]):
            lanes[g, j] = lanes[g, self.nf + j] = 1.0
        lanes[half, 2 * self.nf :] = 1.0
        self.lanes = np.concatenate([lanes, lanes], 0)


def split(v):
    high = v.astype(BF16)
    return high, (v - high.astype(F32)).astype(BF16)


def dot(a, b):
    return jnp.dot(a, b, preferred_element_type=F32)


def lanes3(v):
    high, low = split(v)
    return jnp.concatenate([high, low, high], 1)


def rows3(v):
    high, low = split(v)
    return jnp.concatenate([high, low, high], 0)


def wide_dot(v, table):
    high, low = split(v)
    o = dot(jnp.concatenate([high, low], 1), table)
    n = o.shape[1] // 2
    return o[:, :n] + o[:, n:]


def lane_of(shape):
    return lax.broadcasted_iota(jnp.int32, shape, 1)


def swap(v, block):
    n = v.shape[1]
    if 2 * block == n:
        return pltpu.roll(v, block, 1)
    even = lax.rem(lax.div(lane_of(v.shape), block), 2) == 0
    return jnp.where(even, pltpu.roll(v, n - block, 1), pltpu.roll(v, block, 1))


def conj(v, block):
    even = lax.rem(lax.div(lane_of((1, v.shape[1])), block), 2) == 0
    return v * jnp.where(even, 1.0, -1.0)


def minus_i(v, block):
    return conj(swap(v, block), block)


def fold(half, plus, zero, minus):
    gap = jnp.zeros((MID - 8, plus.shape[1]), F32)
    return jnp.concatenate([plus, zero, gap, minus], 0)


def drive(half, a, b, u):
    p, m = slice(0, half), slice(half + 8, 2 * half + 8)
    d = a * u[0] + b * u[1]
    turned_p = a[p] * u[2][p] + b[p] * u[3][p]
    turned_m = a[m] * u[2][m] + b[m] * u[3][m]
    return fold(half, d[p] + d[m], d[half : half + 8], turned_p - turned_m)


def phases(half, o, block):
    cosine, zero, sine = o[:half], o[half : half + 8], o[half + MID :]
    turned = conj(swap(sine, block), block)
    u = jnp.concatenate([cosine + turned, zero, cosine - turned], 0)
    other, back = swap(o[: half + 8], block), conj(sine, block)
    v = jnp.concatenate([other[:half] - back, other[half:], other[:half] + back], 0)
    return u, v, -conj(v, block), conj(u, block)


def gather(half, q, a, b, o, block):
    p, z, m = slice(0, half), slice(half, half + 8), slice(half + 8, 2 * half + 8)
    c, zero, s = o[:half], o[half : half + 8], conj(o[half + MID :], block)
    parts = [
        a[p] * c + b[p] * s,
        a[z] * zero,
        a[m] * c - b[m] * s,
        b[p] * c - a[p] * s,
        b[z] * zero,
        b[m] * c + a[m] * s,
    ]
    return parts if q is None else [x + y for x, y in zip(q, parts)]


def back_rows(half, q, block):
    plus = q[0] + q[2] - swap(q[3] + q[5], block)
    zero = q[1] - swap(q[4], block)
    turned = conj(swap(q[0] - q[2], block) - (q[3] - q[5]), block)
    return fold(half, plus, zero, turned)


def lane_sum(v):
    return jnp.sum(v, axis=1, keepdims=True)


class Spectra:
    def __init__(self, real, imag, at_zero):
        self.real, self.imag, self.zero = real, imag, at_zero
        self.count = real.shape[0]

    def __getitem__(self, k):
        return self.real[k], self.imag[k]

    def at_zero(self):
        return self.zero[0], self.zero[1]


def core(tb, dom, target, weight, spectra, t, e_ref, keep=None):
    half, nf = tb.half, tb.nf
    slots, rows, cols = target.shape
    kcount = spectra.count
    wl = 2 * nf
    zb = wl // (2 * slots)
    ty, tyt = t["ty"], t["tyt"]
    thirds_of = [dom[:, j * cols : (j + 1) * cols] for j in range(3)]
    g = sum(wide_dot(v, t["spec"][j]) for j, v in enumerate(thirds_of))
    gw = jnp.concatenate([g[s * rows : (s + 1) * rows] for s in range(slots)], 1)
    spec = dot(tyt[...], rows3(gw))
    us = [phases(half, spec[:, s * wl : (s + 1) * wl], nf) for s in range(slots)]
    g0 = lane_sum(thirds_of[0] + thirds_of[1] + thirds_of[2]) * tb.area
    block = lax.div(lane_of((rows, wl)), zb)
    g0w = jnp.zeros((rows, wl), F32)
    for s in range(slots):
        g0w = jnp.where(block == 2 * s, g0[s * rows : (s + 1) * rows], g0w)
    u0 = phases(half, dot(tyt[...], rows3(g0w)), zb)
    a0, b0 = spectra.at_zero()
    r0 = dot(ty[...], rows3(drive(half, a0, b0, u0)))
    r0h, r0l = split(r0)
    r0l = pltpu.roll(r0l.astype(F32), wl // 2, 1)
    r0s = [
        jnp.where(lax.div(block, 2) == s, r0h.astype(F32), r0l).astype(BF16) for s in range(slots)
    ]
    inner = lax.rem(lane_of((rows, wl)), zb)
    groups = [range(k0, min(k0 + GROUP, kcount)) for k0 in range(0, kcount, GROUP)]

    def in_pairs(ks):
        return [ks[i : i + 2] for i in range(0, len(ks), 2)]

    def row_stage(s, ks):
        out, extra = [], []
        for pair in in_pairs(ks):
            w = jnp.concatenate([drive(half, *spectra[k], us[s]) for k in pair], 1)
            r = dot(ty[...], rows3(w))
            for n, k in enumerate(pair):
                out.append(r[:, n * wl : (n + 1) * wl])
                extra += [r0s[s][i : i + MID] * t["picks"][k] for i in range(0, rows, MID)]
        return jnp.concatenate([lanes3(jnp.concatenate(out, 0)), jnp.concatenate(extra, 0)], 1)

    def field_stage(s, ks, ready, inten):
        field = dot(ready, t["fwd"][...])
        for n, k in enumerate(ks):
            e = field[n * rows : (n + 1) * rows]
            e_ref[s, k] = e
            inten = inten + (e[:, :cols] * e[:, :cols] + e[:, cols:] * e[:, cols:])
        return inten

    def slope_of(s, inten):
        resist = jax.nn.sigmoid(RESIST_SLOPE * (inten - THRESHOLD))
        slope = 2.0 * weight[s] * (resist - target[s]) * RESIST_SLOPE * resist * (1.0 - resist)
        return resist, jnp.concatenate([slope, slope], 1)

    def column_stage(s, ks, slope2):
        back = [e_ref[s, k] * slope2 for k in ks]
        flat = [(lane_sum(v[:, :cols]), -lane_sum(v[:, cols:])) for v in back]
        return wide_dot(jnp.concatenate(back, 0), t["adj"][...]), flat

    def sum_stage(s, ks, ready, c0, q):
        for m, pair in enumerate(in_pairs(ks)):
            parts = [
                ready[0][(2 * m + n) * rows : (2 * m + n + 1) * rows] for n in range(len(pair))
            ]
            o = dot(tyt[...], rows3(jnp.concatenate([v[:, :wl] for v in parts], 1)))
            for n, k in enumerate(pair):
                zr, zi = ready[1][2 * m + n]
                c0 = jnp.where(inner == k, jnp.where(lax.rem(block, 2) == 0, zr, zi), c0)
                q = gather(half, q, *spectra[k], o[:, n * wl : (n + 1) * wl], nf)
        return c0, q

    def finish(s, c0, q):
        own = lax.div(block, 2) == s
        q0 = gather(half, None, a0, b0, dot(tyt[...], rows3(jnp.where(own, c0, 0.0))), zb)
        ug = dot(ty[...], rows3(back_rows(half, q, nf)))
        ug0 = dot(ty[...], rows3(back_rows(half, q0, zb)))
        flat = lane_sum(jnp.where(block == 2 * s, ug0, 0.0))
        return dot(lanes3(ug), t["grad"][...]) + (2.0 * tb.area) * flat

    grads = []
    slope2 = None
    for s in range(slots + 1):
        forward, backward = s < slots, s > 0
        inten = jnp.zeros((rows, cols), F32)
        c0, q = jnp.zeros((rows, wl), F32), None
        ahead_f = row_stage(s, groups[0]) if forward else None
        ahead_b = column_stage(s - 1, groups[0], slope2) if backward else None
        for j, ks in enumerate(groups):
            now_f, now_b = ahead_f, ahead_b
            more = j + 1 < len(groups)
            if forward and more:
                ahead_f = row_stage(s, groups[j + 1])
            if backward and more:
                ahead_b = column_stage(s - 1, groups[j + 1], slope2)
            if forward:
                inten = field_stage(s, ks, now_f, inten)
            if backward:
                c0, q = sum_stage(s - 1, ks, now_b, c0, q)
        if backward:
            grads.append(finish(s - 1, c0, q))
        if forward:
            resist, slope2 = slope_of(s, inten)
            if keep is not None:
                keep(s, resist)
    return grads


def read_flags(flags, shape):
    return tuple(jnp.broadcast_to(flags[i : i + 1], shape) > 0.5 for i in range(6))


def in_order(even, first, second):
    return jnp.where(even, first, second), jnp.where(even, second, first)


def domain_of(flags, prev, own0, own1, nxt):
    both, l0, l1, r0, r1, _ = flags
    zero = jnp.zeros_like(own0)
    first = [jnp.where(l0, prev, zero), own0, jnp.where(r0, jnp.where(both, own1, nxt), zero)]
    second = [jnp.where(l1, own0, zero), own1, jnp.where(r1, nxt, zero)]
    return jnp.concatenate([jnp.concatenate(first, 1), jnp.concatenate(second, 1)], 0)


def thirds(flags, dg):
    both, l0, l1, r0, r1, _ = flags
    cols = dg[0].shape[1] // 3
    left0, mid0, right0 = (dg[0][:, j * cols : (j + 1) * cols] for j in range(3))
    left1, mid1, right1 = (dg[1][:, j * cols : (j + 1) * cols] for j in range(3))
    part0 = mid0 + jnp.where(jnp.logical_and(r0, both), left1, 0.0)
    part1 = mid1 + jnp.where(l1, right0, 0.0)
    return part0, part1, jnp.where(both, right1, right0), left0


def own_gradient(flags, part0, part1, from_prev, from_next):
    both, l0, l1, r0, r1, _ = flags
    g0 = part0 + jnp.where(l0, from_prev, 0.0)
    g0 = g0 + jnp.where(jnp.logical_and(r0, jnp.logical_not(both)), from_next, 0.0)
    return g0, part1 + jnp.where(jnp.logical_and(r1, both), from_next, 0.0)


def stepped(step, params, gradient):
    transmit = jnp.tanh(params)
    return params - step * gradient * (1.0 - transmit * transmit)


def kernel_first(tb, names, marks, mp, got_a, got_b, target, weight, *rest):
    spectra, rest = Spectra(*rest[:3]), rest[3:]
    t = dict(zip(names, rest))
    part, send_a, send_b, e_ref = rest[len(names) :]
    flags = read_flags(marks, got_a.shape)
    prev, nxt = in_order(flags[5], got_a[...], got_b[...])
    tile = [jnp.tanh(v) for v in (prev, mp[0], mp[1], nxt)]
    dg = core(tb, domain_of(flags, *tile), target, weight, spectra, t, e_ref)
    part[0], part[1], to_next, to_prev = thirds(flags, dg)
    send_a[...], send_b[...] = in_order(flags[5], to_next, to_prev)


def kernel_update(step, marks, part, params, got_a, got_b, out, send_a, send_b):
    flags = read_flags(marks, got_a.shape)
    prev, nxt = in_order(flags[5], got_a[...], got_b[...])
    g0, g1 = own_gradient(flags, part[0], part[1], prev, nxt)
    new0 = stepped(step, params[0], g0)
    new1 = jnp.where(flags[0], stepped(step, params[1], g1), params[1])
    out[0], out[1] = new0, new1
    send_a[...], send_b[...] = in_order(flags[5], jnp.where(flags[0], new1, new0), new0)


def kernel_second(tb, names, marks, mp, got_a, got_b, target, weight, *rest):
    spectra, rest = Spectra(*rest[:3]), rest[3:]
    t = dict(zip(names, rest))
    part, resist_out, send_a, send_b, e_ref = rest[len(names) :]
    flags = read_flags(marks, got_a.shape)
    prev, nxt = in_order(flags[5], got_a[...], got_b[...])
    tile = [jnp.tanh(v) for v in (prev, mp[0], mp[1], nxt)]
    def keep(s, resist):
        resist_out[s] = resist if s == 0 else jnp.where(flags[0], resist, 0.0)

    dg = core(tb, domain_of(flags, *tile), target, weight, spectra, t, e_ref, keep)
    part[0], part[1], to_next, to_prev = thirds(flags, dg)
    send_a[...], send_b[...] = in_order(flags[5], to_next, to_prev)


def kernel_store(image, out, sem):
    move = pltpu.make_async_copy(image, out, sem)
    move.start()
    move.wait()


def kernel_last(step, marks, part, params, got_a, got_b, out):
    flags = read_flags(marks, got_a.shape)
    prev, nxt = in_order(flags[5], got_a[...], got_b[...])
    g0, g1 = own_gradient(flags, part[0], part[1], prev, nxt)
    out[0] = stepped(step, params[0], g0)
    out[1] = jnp.where(flags[0], stepped(step, params[1], g1), params[1])


def kernel_arrange(tb, slots, kernels, weights, order, lanes, out_a, out_b, out_0, padded):
    half, nf = tb.half, tb.nf
    frows, wl = 2 * half + 8, 2 * nf
    bands = kernels.shape[1]
    kcount = out_a.shape[0]
    zb = wl // (2 * slots)
    chunk = RUN * 2 * bands
    padded[...] = jnp.zeros(padded.shape, F32)
    inner = lax.rem(lane_of((frows, wl)), zb)
    sign = jnp.where(lane_of((1, wl)) < nf, -1.0, 1.0)
    zeros = [jnp.zeros((frows, wl), F32) for _ in range(2)]
    roots = jnp.sqrt(weights[...])

    def order_rows(i):
        found = {}
        for j in range(RUN):
            ks = (i * RUN + j, (i + 1) * RUN + j)
            for n, k in enumerate(ks):
                window = pl.ds((i + n) * chunk + tb.starts[j], tb.window)
                padded[k, :, :bands] = kernels[window, :]
            high, low = split(jnp.concatenate([padded[k] for k in ks], 1))
            v = dot(order[j], jnp.concatenate([high, low], 0))
            for n, k in enumerate(ks):
                root = jnp.broadcast_to(roots[:, k : k + 1], (1, wl))
                found[k] = v[:, n * wl : (n + 1) * wl] * root
        return found

    def order_lanes(found):
        ks = sorted(found)
        high, low = split(jnp.concatenate([found[k] for k in ks], 0))
        v = dot(jnp.concatenate([high, low], 1), lanes[...])
        for n, k in enumerate(ks):
            real = v[2 * n * frows : (2 * n + 1) * frows]
            imag = v[(2 * n + 1) * frows : (2 * n + 2) * frows]
            out_a[k] = real[:, :wl]
            out_b[k] = imag[:, :wl] * sign
            zeros[0] = jnp.where(inner == k, real[:, wl:], zeros[0])
            zeros[1] = jnp.where(inner == k, imag[:, wl:], zeros[1])

    waiting = None
    for i in range(0, kcount // RUN, 2):
        found = order_rows(i)
        if waiting is not None:
            order_lanes(waiting)
        waiting = found
    order_lanes(waiting)
    out_0[0] = zeros[0]
    out_0[1] = -conj(zeros[1], zb)


def arrange(tb, slots, parts, ins):
    bands, kcount = ins[0].shape[1], ins[1].shape[1]
    frows, wl = 2 * tb.half + 8, 2 * tb.nf
    return call(
        functools.partial(kernel_arrange, tb, slots),
        list(ins),
        [(kcount, frows, wl)] * 2 + [(2, frows, wl)],
        [pltpu.VMEM((kcount, parts * frows, wl), F32)],
    )


def kernel_choose(ids, links, params, *refs):
    count = (len(refs) - 7) // 2
    far, (marks, send_a, send_b) = refs[:count], refs[count : count + 3]
    near, (ids_s, links_s, params_v, sems) = refs[count + 3 : 2 * count + 3], refs[2 * count + 3 :]
    pairs = [(ids, ids_s), (links, links_s), (params, params_v), *zip(far, near)]
    moves = [pltpu.make_async_copy(*pair, sems.at[i]) for i, pair in enumerate(pairs)]
    for move in moves:
        move.start()
    for move in moves[:3]:
        move.wait()
    both = ids_s[1] >= 0
    even = lax.rem(lax.axis_index("grp"), 2) == 0
    last = jnp.where(both, params_v[1], params_v[0])
    send_a[...], send_b[...] = in_order(even, last, params_v[0])
    flags = [both] + [links_s[s, side] == 1 for side in range(2) for s in range(2)] + [even]
    row = lax.broadcasted_iota(jnp.int32, marks.shape, 0)
    out = jnp.zeros(marks.shape, F32)
    for i, flag in enumerate(flags):
        out = jnp.where(row == i, jnp.where(flag, 1.0, 0.0), out)
    marks[...] = out
    for move in moves[3:]:
        move.wait()


def choose(tile_ids, tile_links, mask_params, far):
    tile = mask_params.shape[1:]
    ins = (tile_ids, tile_links, mask_params, *far)
    shapes = [jax.ShapeDtypeStruct(s, F32) for s in ((8, tile[1]), tile, tile)]
    shapes += [jax.ShapeDtypeStruct(v.shape, v.dtype) for v in far]
    return pl.pallas_call(
        kernel_choose,
        in_specs=[pl.BlockSpec(memory_space=pltpu.HBM)] * len(ins),
        out_specs=[pl.BlockSpec(memory_space=pltpu.VMEM)] * len(shapes),
        out_shape=shapes,
        scratch_shapes=[
            pltpu.SMEM(tile_ids.shape, jnp.int32),
            pltpu.SMEM(tile_links.shape, jnp.int32),
            pltpu.VMEM(mask_params.shape, F32),
            pltpu.SemaphoreType.DMA((len(ins),)),
        ],
        compiler_params=pltpu.CompilerParams(vmem_limit_bytes=8 << 20),
    )(*(pltpu.with_memory_space_constraint(v, pltpu.HBM) for v in ins))


def call(body, ins, outs, scratch=(), limit=32 << 20, moved=()):
    vmem = pl.BlockSpec(memory_space=pltpu.VMEM)
    return pl.pallas_call(
        body,
        in_specs=[vmem] * len(ins),
        out_specs=[
            pl.BlockSpec(memory_space=pltpu.HBM) if i in moved else vmem for i in range(len(outs))
        ],
        out_shape=[jax.ShapeDtypeStruct(s, F32) for s in outs],
        scratch_shapes=list(scratch),
        compiler_params=pltpu.CompilerParams(vmem_limit_bytes=limit),
    )(*ins)


def local(mesh_shape, mask_params, target, weight, kernels, kernel_weight, tile_ids, tile_links):
    slots, rows, cols = mask_params.shape
    bands = kernels.shape[2]
    kcount = kernels.shape[0]
    groups, count = mesh_shape
    step = STEP_SCALE * math.sqrt(rows * cols)
    tb = Tables(rows, cols, bands)
    names = tuple(tb.arrays)
    tables = [jnp.asarray(tb.arrays[n]) for n in names]
    axes = ("grp", "tile")

    ring_a = snake_ring(groups, count, 1)
    ring_b = snake_ring(groups, count, -1)

    def exchange(a, b):
        return lax.ppermute(a, axes, ring_a), lax.ppermute(b, axes, ring_b)

    whole, tile = mask_params.shape, (rows, cols)

    flat = jnp.swapaxes(kernels, 1, 2).reshape(-1, bands)
    far = (flat, kernel_weight[None], jnp.asarray(tb.order), jnp.asarray(tb.lanes))
    marks, sa, sb, *near = choose(tile_ids, tile_links, mask_params, far)
    got = exchange(sa, sb)
    arranged = arrange(tb, slots, kernels.shape[1], near)
    field = pltpu.VMEM((slots, kcount, rows, 2 * cols), F32)
    part, sa, sb = call(
        functools.partial(kernel_first, tb, names),
        [marks, mask_params, *got, target, weight, *arranged, *tables],
        [whole, tile, tile],
        [field],
    )
    params, sa, sb = call(
        functools.partial(kernel_update, step),
        [marks, part, mask_params, *exchange(sa, sb)],
        [whole, tile, tile],
    )
    part, resist, sa, sb = call(
        functools.partial(kernel_second, tb, names),
        [marks, params, *exchange(sa, sb), target, weight, *arranged, *tables],
        [whole, whole, tile, tile],
        [field],
    )
    got = exchange(sa, sb)
    (resist,) = call(kernel_store, [resist], [whole], [pltpu.SemaphoreType.DMA], moved=(0,))
    (out,) = call(
        functools.partial(kernel_last, step),
        [marks, part, params, *got],
        [whole],
    )
    return (out, resist)


def solution(mesh):
    tiles = P(("grp", "tile"), None, None)
    return jax.shard_map(
        functools.partial(local, (mesh.shape["grp"], mesh.shape["tile"])),
        mesh=mesh,
        in_specs=(tiles, tiles, tiles, P(), P(), P(("grp", "tile")), P(("grp", "tile"), None)),
        out_specs=(tiles, tiles),
        check_vma=False,
    )
```

```python
import functools
import math

import jax
import jax.numpy as jnp
import numpy as np
from jax import lax
from jax.experimental import pallas as pl
from jax.experimental.pallas import tpu as pltpu
from jax.sharding import PartitionSpec as P

ITERS = 2
RESIST_SLOPE = 4.0
THRESHOLD = 0.9
STEP_SCALE = 0.04
GROUP = 8
RUN = 4
MID = 16
F32 = jnp.float32
BF16 = jnp.bfloat16


def swap_pairs(groups, count, first):
    pairs = []
    for g in range(groups):
        for i in range(count):
            j = i + 1 if (i - first) % 2 == 0 else i - 1
            other = g
            if not 0 <= j < count:
                j, other = i, g ^ 1 if groups % 2 == 0 else g
            pairs.append((g * count + i, other * count + j))
    return pairs


def split_np(table):
    table = np.asarray(table, np.float32)
    high = table.astype(jnp.bfloat16)
    low = (table - high.astype(np.float32)).astype(jnp.bfloat16)
    return high, low


class Tables:
    def __init__(self, rows, cols, bands):
        half = (bands - 1) // 2
        self.half = half
        area = 1.0 / (rows * cols)
        self.area = area
        pos = np.arange(1, half + 1)
        angle = (np.arange(rows)[:, None] * pos[None, :] % (2 * rows)) * (np.pi / rows)
        ty = np.zeros((rows, 2 * half + MID))
        ty[:, :half] = np.cos(angle)
        ty[:, half] = 1.0
        ty[:, half + MID :] = np.sin(angle)
        freq = np.concatenate([np.arange(-half, 0), np.arange(1, half + 1)])
        self.nf = len(freq)
        period = 3 * cols
        theta = (np.arange(period)[:, None] * freq[None, :] % period) * (2.0 * np.pi / period)
        c, s = np.cos(theta), np.sin(theta)
        co, so = c[cols : 2 * cols].T, s[cols : 2 * cols].T
        forward = np.block([[co, so], [-so, co]])
        adjoint = np.block([[co.T, so.T], [so.T, -co.T]])
        gradient = np.concatenate([c.T, s.T], 0) * (2.0 * area)
        spectrum = np.concatenate([c, -s], 1) * area

        def left(table):
            h, l = split_np(table)
            return np.concatenate([h, h, l], 1)

        def right(table):
            h, l = split_np(table)
            return np.concatenate([h, h, l], 0)

        part = np.arange(2 * self.nf) // (self.nf // 2) % 2
        ones = np.zeros((2 * self.nf, 2 * cols))
        ones[part == 0, :cols] = 1.0
        ones[part == 1, cols:] = 1.0
        sums = np.concatenate([ones.T, ones.T, np.zeros_like(ones.T)], 0).astype(jnp.bfloat16)
        sums[cols : 2 * cols] *= -1
        sums[3 * cols : 4 * cols] *= -1
        picks = np.zeros((self.nf // 2, MID, 2 * self.nf), jnp.bfloat16)
        for k in range(self.nf // 2):
            picks[k, :, k :: self.nf // 2] = 1.0

        def wide(table):
            h, l = split_np(table)
            top = np.concatenate([h, l], 1)
            return np.concatenate([top, np.concatenate([h, np.zeros_like(l)], 1)], 0)

        self.arrays = dict(
            ty=left(ty),
            tyt=left(ty.T),
            fwd=np.concatenate([right(forward), ones.astype(jnp.bfloat16)], 0),
            picks=picks,
            adj=wide(adjoint),
            grad=right(gradient),
            spec=np.stack([wide(spectrum[j * cols : (j + 1) * cols]) for j in range(3)]),
        )
        chunk = RUN * 2 * bands
        frows = 2 * half + 8
        self.window = 2 * frows
        order = np.zeros((RUN, 2 * frows, self.window), jnp.bfloat16)
        self.starts = []
        for j in range(RUN):
            start = min(2 * bands * j // 8 * 8, chunk - self.window)
            self.starts.append(start)
            for part in range(2):
                first = 2 * bands * j - start + part
                base = part * frows
                for f in range(half):
                    order[j, base + f, first + 2 * (half + 1 + f)] = 1.0
                    order[j, base + half + 8 + f, first + 2 * (half - 1 - f)] = 1.0
                order[j, base + half, first + 2 * half] = 1.0
        self.order = np.concatenate([order, order], 2)
        lanes = np.zeros((2 * self.nf, 4 * self.nf), jnp.bfloat16)
        for j, g in enumerate([*range(half), *range(half + 1, bands)]):
            lanes[g, j] = lanes[g, self.nf + j] = 1.0
        lanes[half, 2 * self.nf :] = 1.0
        self.lanes = np.concatenate([lanes, lanes], 0)


def split(v):
    high = v.astype(BF16)
    return high, (v - high.astype(F32)).astype(BF16)


def dot(a, b):
    return jnp.dot(a, b, preferred_element_type=F32)


def lanes3(v):
    high, low = split(v)
    return jnp.concatenate([high, low, high], 1)


def rows3(v):
    high, low = split(v)
    return jnp.concatenate([high, low, high], 0)


def wide_dot(v, table):
    high, low = split(v)
    o = dot(jnp.concatenate([high, low], 1), table)
    n = o.shape[1] // 2
    return o[:, :n] + o[:, n:]


def lane_of(shape):
    return lax.broadcasted_iota(jnp.int32, shape, 1)


def swap(v, block):
    n = v.shape[1]
    if 2 * block == n:
        return pltpu.roll(v, block, 1)
    even = lax.rem(lax.div(lane_of(v.shape), block), 2) == 0
    return jnp.where(even, pltpu.roll(v, n - block, 1), pltpu.roll(v, block, 1))


def conj(v, block):
    even = lax.rem(lax.div(lane_of((1, v.shape[1])), block), 2) == 0
    return v * jnp.where(even, 1.0, -1.0)


def minus_i(v, block):
    return conj(swap(v, block), block)


def fold(half, plus, zero, minus):
    gap = jnp.zeros((MID - 8, plus.shape[1]), F32)
    return jnp.concatenate([plus, zero, gap, minus], 0)


def drive(half, a, b, u):
    p, m = slice(0, half), slice(half + 8, 2 * half + 8)
    d = a * u[0] + b * u[1]
    turned_p = a[p] * u[2][p] + b[p] * u[3][p]
    turned_m = a[m] * u[2][m] + b[m] * u[3][m]
    return fold(half, d[p] + d[m], d[half : half + 8], turned_p - turned_m)


def phases(half, o, block):
    cosine, zero, sine = o[:half], o[half : half + 8], o[half + MID :]
    turned = conj(swap(sine, block), block)
    u = jnp.concatenate([cosine + turned, zero, cosine - turned], 0)
    other, back = swap(o[: half + 8], block), conj(sine, block)
    v = jnp.concatenate([other[:half] - back, other[half:], other[:half] + back], 0)
    return u, v, -conj(v, block), conj(u, block)


def gather(half, q, a, b, o, block):
    p, z, m = slice(0, half), slice(half, half + 8), slice(half + 8, 2 * half + 8)
    c, zero, s = o[:half], o[half : half + 8], conj(o[half + MID :], block)
    parts = [
        a[p] * c + b[p] * s,
        a[z] * zero,
        a[m] * c - b[m] * s,
        b[p] * c - a[p] * s,
        b[z] * zero,
        b[m] * c + a[m] * s,
    ]
    return parts if q is None else [x + y for x, y in zip(q, parts)]


def back_rows(half, q, block):
    plus = q[0] + q[2] - swap(q[3] + q[5], block)
    zero = q[1] - swap(q[4], block)
    turned = conj(swap(q[0] - q[2], block) - (q[3] - q[5]), block)
    return fold(half, plus, zero, turned)


def lane_sum(v):
    return jnp.sum(v, axis=1, keepdims=True)


class Spectra:
    def __init__(self, real, imag, at_zero):
        self.real, self.imag, self.zero = real, imag, at_zero
        self.count = real.shape[0]

    def __getitem__(self, k):
        return self.real[k], self.imag[k]

    def at_zero(self):
        return self.zero[0], self.zero[1]


def core(tb, dom, target, weight, spectra, t, e_ref, keep=None):
    half, nf = tb.half, tb.nf
    slots, rows, cols = target.shape
    kcount = spectra.count
    wl = 2 * nf
    zb = wl // (2 * slots)
    ty, tyt = t["ty"], t["tyt"]
    thirds_of = [dom[:, j * cols : (j + 1) * cols] for j in range(3)]
    g = sum(wide_dot(v, t["spec"][j]) for j, v in enumerate(thirds_of))
    gw = jnp.concatenate([g[s * rows : (s + 1) * rows] for s in range(slots)], 1)
    spec = dot(tyt[...], rows3(gw))
    us = [phases(half, spec[:, s * wl : (s + 1) * wl], nf) for s in range(slots)]
    g0 = lane_sum(thirds_of[0] + thirds_of[1] + thirds_of[2]) * tb.area
    block = lax.div(lane_of((rows, wl)), zb)
    g0w = jnp.zeros((rows, wl), F32)
    for s in range(slots):
        g0w = jnp.where(block == 2 * s, g0[s * rows : (s + 1) * rows], g0w)
    u0 = phases(half, dot(tyt[...], rows3(g0w)), zb)
    a0, b0 = spectra.at_zero()
    r0 = dot(ty[...], rows3(drive(half, a0, b0, u0)))
    r0h, r0l = split(r0)
    r0l = pltpu.roll(r0l.astype(F32), wl // 2, 1)
    r0s = [
        jnp.where(lax.div(block, 2) == s, r0h.astype(F32), r0l).astype(BF16) for s in range(slots)
    ]
    inner = lax.rem(lane_of((rows, wl)), zb)
    groups = [range(k0, min(k0 + GROUP, kcount)) for k0 in range(0, kcount, GROUP)]

    def in_pairs(ks):
        return [ks[i : i + 2] for i in range(0, len(ks), 2)]

    def row_stage(s, ks):
        out, extra = [], []
        for pair in in_pairs(ks):
            w = jnp.concatenate([drive(half, *spectra[k], us[s]) for k in pair], 1)
            r = dot(ty[...], rows3(w))
            for n, k in enumerate(pair):
                out.append(r[:, n * wl : (n + 1) * wl])
                extra += [r0s[s][i : i + MID] * t["picks"][k] for i in range(0, rows, MID)]
        return jnp.concatenate([lanes3(jnp.concatenate(out, 0)), jnp.concatenate(extra, 0)], 1)

    def field_stage(s, ks, ready, inten):
        field = dot(ready, t["fwd"][...])
        for n, k in enumerate(ks):
            e = field[n * rows : (n + 1) * rows]
            e_ref[s, k] = e
            inten = inten + (e[:, :cols] * e[:, :cols] + e[:, cols:] * e[:, cols:])
        return inten

    def slope_of(s, inten):
        resist = jax.nn.sigmoid(RESIST_SLOPE * (inten - THRESHOLD))
        slope = 2.0 * weight[s] * (resist - target[s]) * RESIST_SLOPE * resist * (1.0 - resist)
        return resist, jnp.concatenate([slope, slope], 1)

    def column_stage(s, ks, slope2):
        back = [e_ref[s, k] * slope2 for k in ks]
        flat = [(lane_sum(v[:, :cols]), -lane_sum(v[:, cols:])) for v in back]
        return wide_dot(jnp.concatenate(back, 0), t["adj"][...]), flat

    def sum_stage(s, ks, ready, c0, q):
        for m, pair in enumerate(in_pairs(ks)):
            parts = [
                ready[0][(2 * m + n) * rows : (2 * m + n + 1) * rows] for n in range(len(pair))
            ]
            o = dot(tyt[...], rows3(jnp.concatenate([v[:, :wl] for v in parts], 1)))
            for n, k in enumerate(pair):
                zr, zi = ready[1][2 * m + n]
                c0 = jnp.where(inner == k, jnp.where(lax.rem(block, 2) == 0, zr, zi), c0)
                q = gather(half, q, *spectra[k], o[:, n * wl : (n + 1) * wl], nf)
        return c0, q

    def finish(s, c0, q):
        own = lax.div(block, 2) == s
        q0 = gather(half, None, a0, b0, dot(tyt[...], rows3(jnp.where(own, c0, 0.0))), zb)
        ug = dot(ty[...], rows3(back_rows(half, q, nf)))
        ug0 = dot(ty[...], rows3(back_rows(half, q0, zb)))
        flat = lane_sum(jnp.where(block == 2 * s, ug0, 0.0))
        return dot(lanes3(ug), t["grad"][...]) + (2.0 * tb.area) * flat

    grads = []
    slope2 = None
    for s in range(slots + 1):
        forward, backward = s < slots, s > 0
        inten = jnp.zeros((rows, cols), F32)
        c0, q = jnp.zeros((rows, wl), F32), None
        ahead_f = row_stage(s, groups[0]) if forward else None
        ahead_b = column_stage(s - 1, groups[0], slope2) if backward else None
        for j, ks in enumerate(groups):
            now_f, now_b = ahead_f, ahead_b
            more = j + 1 < len(groups)
            if forward and more:
                ahead_f = row_stage(s, groups[j + 1])
            if backward and more:
                ahead_b = column_stage(s - 1, groups[j + 1], slope2)
            if forward:
                inten = field_stage(s, ks, now_f, inten)
            if backward:
                c0, q = sum_stage(s - 1, ks, now_b, c0, q)
        if backward:
            grads.append(finish(s - 1, c0, q))
        if forward:
            resist, slope2 = slope_of(s, inten)
            if keep is not None:
                keep(s, resist)
    return grads


def read_flags(flags, shape):
    return tuple(jnp.broadcast_to(flags[i : i + 1], shape) > 0.5 for i in range(6))


def in_order(even, first, second):
    return jnp.where(even, first, second), jnp.where(even, second, first)


def domain_of(flags, prev, own0, own1, nxt):
    both, l0, l1, r0, r1, _ = flags
    zero = jnp.zeros_like(own0)
    first = [jnp.where(l0, prev, zero), own0, jnp.where(r0, jnp.where(both, own1, nxt), zero)]
    second = [jnp.where(l1, own0, zero), own1, jnp.where(r1, nxt, zero)]
    return jnp.concatenate([jnp.concatenate(first, 1), jnp.concatenate(second, 1)], 0)


def thirds(flags, dg):
    both, l0, l1, r0, r1, _ = flags
    cols = dg[0].shape[1] // 3
    left0, mid0, right0 = (dg[0][:, j * cols : (j + 1) * cols] for j in range(3))
    left1, mid1, right1 = (dg[1][:, j * cols : (j + 1) * cols] for j in range(3))
    part0 = mid0 + jnp.where(jnp.logical_and(r0, both), left1, 0.0)
    part1 = mid1 + jnp.where(l1, right0, 0.0)
    return part0, part1, jnp.where(both, right1, right0), left0


def own_gradient(flags, part0, part1, from_prev, from_next):
    both, l0, l1, r0, r1, _ = flags
    g0 = part0 + jnp.where(l0, from_prev, 0.0)
    g0 = g0 + jnp.where(jnp.logical_and(r0, jnp.logical_not(both)), from_next, 0.0)
    return g0, part1 + jnp.where(jnp.logical_and(r1, both), from_next, 0.0)


def stepped(step, params, gradient):
    transmit = jnp.tanh(params)
    return params - step * gradient * (1.0 - transmit * transmit)


def kernel_first(tb, names, marks, mp, got_a, got_b, target, weight, *rest):
    spectra, rest = Spectra(*rest[:3]), rest[3:]
    t = dict(zip(names, rest))
    part, send_a, send_b, e_ref = rest[len(names) :]
    flags = read_flags(marks, got_a.shape)
    prev, nxt = in_order(flags[5], got_b[...], got_a[...])
    tile = [jnp.tanh(v) for v in (prev, mp[0], mp[1], nxt)]
    dg = core(tb, domain_of(flags, *tile), target, weight, spectra, t, e_ref)
    part[0], part[1], to_next, to_prev = thirds(flags, dg)
    send_a[...], send_b[...] = in_order(flags[5], to_next, to_prev)


def kernel_update(step, marks, part, params, got_a, got_b, out, send_a, send_b):
    flags = read_flags(marks, got_a.shape)
    prev, nxt = in_order(flags[5], got_b[...], got_a[...])
    g0, g1 = own_gradient(flags, part[0], part[1], prev, nxt)
    new0 = stepped(step, params[0], g0)
    new1 = jnp.where(flags[0], stepped(step, params[1], g1), params[1])
    out[0], out[1] = new0, new1
    send_a[...], send_b[...] = in_order(flags[5], jnp.where(flags[0], new1, new0), new0)


def kernel_second(tb, names, marks, mp, got_a, got_b, target, weight, *rest):
    spectra, rest = Spectra(*rest[:3]), rest[3:]
    t = dict(zip(names, rest))
    part, resist_out, send_a, send_b, e_ref = rest[len(names) :]
    flags = read_flags(marks, got_a.shape)
    prev, nxt = in_order(flags[5], got_b[...], got_a[...])
    tile = [jnp.tanh(v) for v in (prev, mp[0], mp[1], nxt)]
    def keep(s, resist):
        resist_out[s] = resist if s == 0 else jnp.where(flags[0], resist, 0.0)

    dg = core(tb, domain_of(flags, *tile), target, weight, spectra, t, e_ref, keep)
    part[0], part[1], to_next, to_prev = thirds(flags, dg)
    send_a[...], send_b[...] = in_order(flags[5], to_next, to_prev)


def kernel_store(image, out, sem):
    move = pltpu.make_async_copy(image, out, sem)
    move.start()
    move.wait()


def kernel_last(step, marks, part, params, got_a, got_b, out):
    flags = read_flags(marks, got_a.shape)
    prev, nxt = in_order(flags[5], got_b[...], got_a[...])
    g0, g1 = own_gradient(flags, part[0], part[1], prev, nxt)
    out[0] = stepped(step, params[0], g0)
    out[1] = jnp.where(flags[0], stepped(step, params[1], g1), params[1])


def kernel_arrange(tb, slots, kernels, weights, order, lanes, out_a, out_b, out_0, padded):
    half, nf = tb.half, tb.nf
    frows, wl = 2 * half + 8, 2 * nf
    bands = kernels.shape[1]
    kcount = out_a.shape[0]
    zb = wl // (2 * slots)
    chunk = RUN * 2 * bands
    padded[...] = jnp.zeros(padded.shape, F32)
    inner = lax.rem(lane_of((frows, wl)), zb)
    sign = jnp.where(lane_of((1, wl)) < nf, -1.0, 1.0)
    zeros = [jnp.zeros((frows, wl), F32) for _ in range(2)]
    roots = jnp.sqrt(weights[...])

    def order_rows(i):
        found = {}
        for j in range(RUN):
            ks = (i * RUN + j, (i + 1) * RUN + j)
            for n, k in enumerate(ks):
                window = pl.ds((i + n) * chunk + tb.starts[j], tb.window)
                padded[k, :, :bands] = kernels[window, :]
            high, low = split(jnp.concatenate([padded[k] for k in ks], 1))
            v = dot(order[j], jnp.concatenate([high, low], 0))
            for n, k in enumerate(ks):
                root = jnp.broadcast_to(roots[:, k : k + 1], (1, wl))
                found[k] = v[:, n * wl : (n + 1) * wl] * root
        return found

    def order_lanes(found):
        ks = sorted(found)
        high, low = split(jnp.concatenate([found[k] for k in ks], 0))
        v = dot(jnp.concatenate([high, low], 1), lanes[...])
        for n, k in enumerate(ks):
            real = v[2 * n * frows : (2 * n + 1) * frows]
            imag = v[(2 * n + 1) * frows : (2 * n + 2) * frows]
            out_a[k] = real[:, :wl]
            out_b[k] = imag[:, :wl] * sign
            zeros[0] = jnp.where(inner == k, real[:, wl:], zeros[0])
            zeros[1] = jnp.where(inner == k, imag[:, wl:], zeros[1])

    waiting = None
    for i in range(0, kcount // RUN, 2):
        found = order_rows(i)
        if waiting is not None:
            order_lanes(waiting)
        waiting = found
    order_lanes(waiting)
    out_0[0] = zeros[0]
    out_0[1] = -conj(zeros[1], zb)


def arrange(tb, slots, parts, ins):
    bands, kcount = ins[0].shape[1], ins[1].shape[1]
    frows, wl = 2 * tb.half + 8, 2 * tb.nf
    return call(
        functools.partial(kernel_arrange, tb, slots),
        list(ins),
        [(kcount, frows, wl)] * 2 + [(2, frows, wl)],
        [pltpu.VMEM((kcount, parts * frows, wl), F32)],
    )


def kernel_choose(ids, links, params, *refs):
    count = (len(refs) - 7) // 2
    far, (marks, send_a, send_b) = refs[:count], refs[count : count + 3]
    near, (ids_s, links_s, params_v, sems) = refs[count + 3 : 2 * count + 3], refs[2 * count + 3 :]
    pairs = [(ids, ids_s), (links, links_s), (params, params_v), *zip(far, near)]
    moves = [pltpu.make_async_copy(*pair, sems.at[i]) for i, pair in enumerate(pairs)]
    for move in moves:
        move.start()
    for move in moves[:3]:
        move.wait()
    both = ids_s[1] >= 0
    even = lax.rem(lax.axis_index("tile"), 2) == 0
    last = jnp.where(both, params_v[1], params_v[0])
    send_a[...], send_b[...] = in_order(even, last, params_v[0])
    flags = [both] + [links_s[s, side] == 1 for side in range(2) for s in range(2)] + [even]
    row = lax.broadcasted_iota(jnp.int32, marks.shape, 0)
    out = jnp.zeros(marks.shape, F32)
    for i, flag in enumerate(flags):
        out = jnp.where(row == i, jnp.where(flag, 1.0, 0.0), out)
    marks[...] = out
    for move in moves[3:]:
        move.wait()


def choose(tile_ids, tile_links, mask_params, far):
    tile = mask_params.shape[1:]
    ins = (tile_ids, tile_links, mask_params, *far)
    shapes = [jax.ShapeDtypeStruct(s, F32) for s in ((8, tile[1]), tile, tile)]
    shapes += [jax.ShapeDtypeStruct(v.shape, v.dtype) for v in far]
    return pl.pallas_call(
        kernel_choose,
        in_specs=[pl.BlockSpec(memory_space=pltpu.HBM)] * len(ins),
        out_specs=[pl.BlockSpec(memory_space=pltpu.VMEM)] * len(shapes),
        out_shape=shapes,
        scratch_shapes=[
            pltpu.SMEM(tile_ids.shape, jnp.int32),
            pltpu.SMEM(tile_links.shape, jnp.int32),
            pltpu.VMEM(mask_params.shape, F32),
            pltpu.SemaphoreType.DMA((len(ins),)),
        ],
        compiler_params=pltpu.CompilerParams(vmem_limit_bytes=8 << 20),
    )(*(pltpu.with_memory_space_constraint(v, pltpu.HBM) for v in ins))


def call(body, ins, outs, scratch=(), limit=32 << 20, moved=()):
    vmem = pl.BlockSpec(memory_space=pltpu.VMEM)
    return pl.pallas_call(
        body,
        in_specs=[vmem] * len(ins),
        out_specs=[
            pl.BlockSpec(memory_space=pltpu.HBM) if i in moved else vmem for i in range(len(outs))
        ],
        out_shape=[jax.ShapeDtypeStruct(s, F32) for s in outs],
        scratch_shapes=list(scratch),
        compiler_params=pltpu.CompilerParams(vmem_limit_bytes=limit),
    )(*ins)


def local(mesh_shape, mask_params, target, weight, kernels, kernel_weight, tile_ids, tile_links):
    slots, rows, cols = mask_params.shape
    bands = kernels.shape[2]
    kcount = kernels.shape[0]
    groups, count = mesh_shape
    step = STEP_SCALE * math.sqrt(rows * cols)
    tb = Tables(rows, cols, bands)
    names = tuple(tb.arrays)
    tables = [jnp.asarray(tb.arrays[n]) for n in names]
    axes = ("grp", "tile")

    inner = swap_pairs(groups, count, 0)
    outer = swap_pairs(groups, count, 1)

    def exchange(a, b):
        return lax.ppermute(a, axes, inner), lax.ppermute(b, axes, outer)

    whole, tile = mask_params.shape, (rows, cols)

    flat = jnp.swapaxes(kernels, 1, 2).reshape(-1, bands)
    far = (flat, kernel_weight[None], jnp.asarray(tb.order), jnp.asarray(tb.lanes))
    marks, sa, sb, *near = choose(tile_ids, tile_links, mask_params, far)
    got = exchange(sa, sb)
    arranged = arrange(tb, slots, kernels.shape[1], near)
    field = pltpu.VMEM((slots, kcount, rows, 2 * cols), F32)
    part, sa, sb = call(
        functools.partial(kernel_first, tb, names),
        [marks, mask_params, *got, target, weight, *arranged, *tables],
        [whole, tile, tile],
        [field],
    )
    params, sa, sb = call(
        functools.partial(kernel_update, step),
        [marks, part, mask_params, *exchange(sa, sb)],
        [whole, tile, tile],
    )
    part, resist, sa, sb = call(
        functools.partial(kernel_second, tb, names),
        [marks, params, *exchange(sa, sb), target, weight, *arranged, *tables],
        [whole, whole, tile, tile],
        [field],
    )
    got = exchange(sa, sb)
    (resist,) = call(kernel_store, [resist], [whole], [pltpu.SemaphoreType.DMA], moved=(0,))
    (out,) = call(
        functools.partial(kernel_last, step),
        [marks, part, params, *got],
        [whole],
    )
    return (out, resist)


def solution(mesh):
    tiles = P(("grp", "tile"), None, None)
    return jax.shard_map(
        functools.partial(local, (mesh.shape["grp"], mesh.shape["tile"])),
        mesh=mesh,
        in_specs=(tiles, tiles, tiles, P(), P(), P(("grp", "tile")), P(("grp", "tile"), None)),
        out_specs=(tiles, tiles),
        check_vma=False,
    )
```

```python
import functools
import math

import jax
import jax.numpy as jnp
import numpy as np
from jax import lax
from jax.experimental import pallas as pl
from jax.experimental.pallas import tpu as pltpu
from jax.sharding import PartitionSpec as P

ITERS = 2
RESIST_SLOPE = 4.0
THRESHOLD = 0.9
STEP_SCALE = 0.04
GROUP = 8
RUN = 4
MID = 16
F32 = jnp.float32
BF16 = jnp.bfloat16


def swap_pairs(groups, count, first):
    pairs = []
    for g in range(groups):
        for i in range(count):
            j = i + 1 if (i - first) % 2 == 0 else i - 1
            other = g
            if not 0 <= j < count:
                j, other = i, g ^ 1 if groups % 2 == 0 else g
            pairs.append((g * count + i, other * count + j))
    return pairs


def split_np(table):
    table = np.asarray(table, np.float32)
    high = table.astype(jnp.bfloat16)
    low = (table - high.astype(np.float32)).astype(jnp.bfloat16)
    return high, low


class Tables:
    def __init__(self, rows, cols, bands):
        half = (bands - 1) // 2
        self.half = half
        area = 1.0 / (rows * cols)
        self.area = area
        pos = np.arange(1, half + 1)
        angle = (np.arange(rows)[:, None] * pos[None, :] % (2 * rows)) * (np.pi / rows)
        ty = np.zeros((rows, 2 * half + MID))
        ty[:, :half] = np.cos(angle)
        ty[:, half] = 1.0
        ty[:, half + MID :] = np.sin(angle)
        freq = np.concatenate([np.arange(-half, 0), np.arange(1, half + 1)])
        self.nf = len(freq)
        period = 3 * cols
        theta = (np.arange(period)[:, None] * freq[None, :] % period) * (2.0 * np.pi / period)
        c, s = np.cos(theta), np.sin(theta)
        co, so = c[cols : 2 * cols].T, s[cols : 2 * cols].T
        forward = np.block([[co, so], [-so, co]])
        adjoint = np.block([[co.T, so.T], [so.T, -co.T]])
        gradient = np.concatenate([c.T, s.T], 0) * (2.0 * area)
        spectrum = np.concatenate([c, -s], 1) * area

        def left(table):
            h, l = split_np(table)
            return np.concatenate([h, h, l], 1)

        def right(table):
            h, l = split_np(table)
            return np.concatenate([h, h, l], 0)

        part = np.arange(2 * self.nf) // (self.nf // 2) % 2
        ones = np.zeros((2 * self.nf, 2 * cols))
        ones[part == 0, :cols] = 1.0
        ones[part == 1, cols:] = 1.0
        sums = np.concatenate([ones.T, ones.T, np.zeros_like(ones.T)], 0).astype(jnp.bfloat16)
        sums[cols : 2 * cols] *= -1
        sums[3 * cols : 4 * cols] *= -1
        picks = np.zeros((self.nf // 2, MID, 2 * self.nf), jnp.bfloat16)
        for k in range(self.nf // 2):
            picks[k, :, k :: self.nf // 2] = 1.0

        def wide(table):
            h, l = split_np(table)
            top = np.concatenate([h, l], 1)
            return np.concatenate([top, np.concatenate([h, np.zeros_like(l)], 1)], 0)

        self.arrays = dict(
            ty=left(ty),
            tyt=left(ty.T),
            fwd=np.concatenate([right(forward), ones.astype(jnp.bfloat16)], 0),
            picks=picks,
            adj=wide(adjoint),
            grad=right(gradient),
            spec=np.stack([wide(spectrum[j * cols : (j + 1) * cols]) for j in range(3)]),
        )
        chunk = RUN * 2 * bands
        frows = 2 * half + 8
        self.window = 2 * frows
        order = np.zeros((RUN, 2 * frows, self.window), jnp.bfloat16)
        self.starts = []
        for j in range(RUN):
            start = min(2 * bands * j // 8 * 8, chunk - self.window)
            self.starts.append(start)
            for part in range(2):
                first = 2 * bands * j - start + part
                base = part * frows
                for f in range(half):
                    order[j, base + f, first + 2 * (half + 1 + f)] = 1.0
                    order[j, base + half + 8 + f, first + 2 * (half - 1 - f)] = 1.0
                order[j, base + half, first + 2 * half] = 1.0
        self.order = np.concatenate([order, order], 2)
        lanes = np.zeros((2 * self.nf, 4 * self.nf), jnp.bfloat16)
        for j, g in enumerate([*range(half), *range(half + 1, bands)]):
            lanes[g, j] = lanes[g, self.nf + j] = 1.0
        lanes[half, 2 * self.nf :] = 1.0
        self.lanes = np.concatenate([lanes, lanes], 0)


def split(v):
    high = v.astype(BF16)
    return high, (v - high.astype(F32)).astype(BF16)


def dot(a, b):
    return jnp.dot(a, b, preferred_element_type=F32)


def lanes3(v):
    high, low = split(v)
    return jnp.concatenate([high, low, high], 1)


def rows3(v):
    high, low = split(v)
    return jnp.concatenate([high, low, high], 0)


def wide_dot(v, table):
    high, low = split(v)
    o = dot(jnp.concatenate([high, low], 1), table)
    n = o.shape[1] // 2
    return o[:, :n] + o[:, n:]


def lane_of(shape):
    return lax.broadcasted_iota(jnp.int32, shape, 1)


def swap(v, block):
    n = v.shape[1]
    if 2 * block == n:
        return pltpu.roll(v, block, 1)
    even = lax.rem(lax.div(lane_of(v.shape), block), 2) == 0
    return jnp.where(even, pltpu.roll(v, n - block, 1), pltpu.roll(v, block, 1))


def conj(v, block):
    even = lax.rem(lax.div(lane_of((1, v.shape[1])), block), 2) == 0
    return v * jnp.where(even, 1.0, -1.0)


def minus_i(v, block):
    return conj(swap(v, block), block)


def fold(half, plus, zero, minus):
    gap = jnp.zeros((MID - 8, plus.shape[1]), F32)
    return jnp.concatenate([plus, zero, gap, minus], 0)


def drive(half, a, b, u):
    p, m = slice(0, half), slice(half + 8, 2 * half + 8)
    d = a * u[0] + b * u[1]
    turned_p = a[p] * u[2][p] + b[p] * u[3][p]
    turned_m = a[m] * u[2][m] + b[m] * u[3][m]
    return fold(half, d[p] + d[m], d[half : half + 8], turned_p - turned_m)


def phases(half, o, block):
    cosine, zero, sine = o[:half], o[half : half + 8], o[half + MID :]
    turned = conj(swap(sine, block), block)
    u = jnp.concatenate([cosine + turned, zero, cosine - turned], 0)
    other, back = swap(o[: half + 8], block), conj(sine, block)
    v = jnp.concatenate([other[:half] - back, other[half:], other[:half] + back], 0)
    return u, v, -conj(v, block), conj(u, block)


def gather(half, q, a, b, o, block):
    p, z, m = slice(0, half), slice(half, half + 8), slice(half + 8, 2 * half + 8)
    c, zero, s = o[:half], o[half : half + 8], conj(o[half + MID :], block)
    parts = [
        a[p] * c + b[p] * s,
        a[z] * zero,
        a[m] * c - b[m] * s,
        b[p] * c - a[p] * s,
        b[z] * zero,
        b[m] * c + a[m] * s,
    ]
    return parts if q is None else [x + y for x, y in zip(q, parts)]


def back_rows(half, q, block):
    plus = q[0] + q[2] - swap(q[3] + q[5], block)
    zero = q[1] - swap(q[4], block)
    turned = conj(swap(q[0] - q[2], block) - (q[3] - q[5]), block)
    return fold(half, plus, zero, turned)


def lane_sum(v):
    return jnp.sum(v, axis=1, keepdims=True)


class Spectra:
    def __init__(self, real, imag, at_zero):
        self.real, self.imag, self.zero = real, imag, at_zero
        self.count = real.shape[0]

    def __getitem__(self, k):
        return self.real[k], self.imag[k]

    def at_zero(self):
        return self.zero[0], self.zero[1]


def core(tb, dom, target, weight, spectra, t, e_ref, keep=None):
    half, nf = tb.half, tb.nf
    slots, rows, cols = target.shape
    kcount = spectra.count
    wl = 2 * nf
    zb = wl // (2 * slots)
    ty, tyt = t["ty"], t["tyt"]
    thirds_of = [dom[:, j * cols : (j + 1) * cols] for j in range(3)]
    g = sum(wide_dot(v, t["spec"][j]) for j, v in enumerate(thirds_of))
    gw = jnp.concatenate([g[s * rows : (s + 1) * rows] for s in range(slots)], 1)
    spec = dot(tyt[...], rows3(gw))
    us = [phases(half, spec[:, s * wl : (s + 1) * wl], nf) for s in range(slots)]
    g0 = lane_sum(thirds_of[0] + thirds_of[1] + thirds_of[2]) * tb.area
    block = lax.div(lane_of((rows, wl)), zb)
    g0w = jnp.zeros((rows, wl), F32)
    for s in range(slots):
        g0w = jnp.where(block == 2 * s, g0[s * rows : (s + 1) * rows], g0w)
    u0 = phases(half, dot(tyt[...], rows3(g0w)), zb)
    a0, b0 = spectra.at_zero()
    r0 = dot(ty[...], rows3(drive(half, a0, b0, u0)))
    r0h, r0l = split(r0)
    r0l = pltpu.roll(r0l.astype(F32), wl // 2, 1)
    r0s = [
        jnp.where(lax.div(block, 2) == s, r0h.astype(F32), r0l).astype(BF16) for s in range(slots)
    ]
    inner = lax.rem(lane_of((rows, wl)), zb)
    groups = [range(k0, min(k0 + GROUP, kcount)) for k0 in range(0, kcount, GROUP)]

    def in_pairs(ks):
        return [ks[i : i + 2] for i in range(0, len(ks), 2)]

    def row_stage(s, ks):
        out, extra = [], []
        for pair in in_pairs(ks):
            w = jnp.concatenate([drive(half, *spectra[k], us[s]) for k in pair], 1)
            r = dot(ty[...], rows3(w))
            for n, k in enumerate(pair):
                out.append(r[:, n * wl : (n + 1) * wl])
                extra += [r0s[s][i : i + MID] * t["picks"][k] for i in range(0, rows, MID)]
        return jnp.concatenate([lanes3(jnp.concatenate(out, 0)), jnp.concatenate(extra, 0)], 1)

    def field_stage(s, ks, ready, inten):
        field = dot(ready, t["fwd"][...])
        for n, k in enumerate(ks):
            e = field[n * rows : (n + 1) * rows]
            e_ref[s, k] = e
            inten = inten + (e[:, :cols] * e[:, :cols] + e[:, cols:] * e[:, cols:])
        return inten

    def slope_of(s, inten):
        resist = jax.nn.sigmoid(RESIST_SLOPE * (inten - THRESHOLD))
        slope = 2.0 * weight[s] * (resist - target[s]) * RESIST_SLOPE * resist * (1.0 - resist)
        return resist, jnp.concatenate([slope, slope], 1)

    def column_stage(s, ks, slope2):
        back = [e_ref[s, k] * slope2 for k in ks]
        flat = [(lane_sum(v[:, :cols]), -lane_sum(v[:, cols:])) for v in back]
        return wide_dot(jnp.concatenate(back, 0), t["adj"][...]), flat

    def sum_stage(s, ks, ready, c0, q):
        for m, pair in enumerate(in_pairs(ks)):
            parts = [
                ready[0][(2 * m + n) * rows : (2 * m + n + 1) * rows] for n in range(len(pair))
            ]
            o = dot(tyt[...], rows3(jnp.concatenate([v[:, :wl] for v in parts], 1)))
            for n, k in enumerate(pair):
                zr, zi = ready[1][2 * m + n]
                c0 = jnp.where(inner == k, jnp.where(lax.rem(block, 2) == 0, zr, zi), c0)
                q = gather(half, q, *spectra[k], o[:, n * wl : (n + 1) * wl], nf)
        return c0, q

    def finish(s, c0, q):
        own = lax.div(block, 2) == s
        q0 = gather(half, None, a0, b0, dot(tyt[...], rows3(jnp.where(own, c0, 0.0))), zb)
        ug = dot(ty[...], rows3(back_rows(half, q, nf)))
        ug0 = dot(ty[...], rows3(back_rows(half, q0, zb)))
        flat = lane_sum(jnp.where(block == 2 * s, ug0, 0.0))
        return dot(lanes3(ug), t["grad"][...]) + (2.0 * tb.area) * flat

    grads = []
    slope2 = None
    for s in range(slots + 1):
        forward, backward = s < slots, s > 0
        inten = jnp.zeros((rows, cols), F32)
        c0, q = jnp.zeros((rows, wl), F32), None
        ahead_f = row_stage(s, groups[0]) if forward else None
        ahead_b = column_stage(s - 1, groups[0], slope2) if backward else None
        for j, ks in enumerate(groups):
            now_f, now_b = ahead_f, ahead_b
            more = j + 1 < len(groups)
            if forward and more:
                ahead_f = row_stage(s, groups[j + 1])
            if backward and more:
                ahead_b = column_stage(s - 1, groups[j + 1], slope2)
            if forward:
                inten = field_stage(s, ks, now_f, inten)
            if backward:
                c0, q = sum_stage(s - 1, ks, now_b, c0, q)
        if backward:
            grads.append(finish(s - 1, c0, q))
        if forward:
            resist, slope2 = slope_of(s, inten)
            if keep is not None:
                keep(s, resist)
    return grads


def read_flags(flags, shape):
    return tuple(jnp.broadcast_to(flags[i : i + 1], shape) > 0.5 for i in range(6))


def in_order(even, first, second):
    return jnp.where(even, first, second), jnp.where(even, second, first)


def domain_of(flags, prev, own0, own1, nxt):
    both, l0, l1, r0, r1, _ = flags
    zero = jnp.zeros_like(own0)
    first = [jnp.where(l0, prev, zero), own0, jnp.where(r0, jnp.where(both, own1, nxt), zero)]
    second = [jnp.where(l1, own0, zero), own1, jnp.where(r1, nxt, zero)]
    return jnp.concatenate([jnp.concatenate(first, 1), jnp.concatenate(second, 1)], 0)


def thirds(flags, dg):
    both, l0, l1, r0, r1, _ = flags
    cols = dg[0].shape[1] // 3
    left0, mid0, right0 = (dg[0][:, j * cols : (j + 1) * cols] for j in range(3))
    left1, mid1, right1 = (dg[1][:, j * cols : (j + 1) * cols] for j in range(3))
    part0 = mid0 + jnp.where(jnp.logical_and(r0, both), left1, 0.0)
    part1 = mid1 + jnp.where(l1, right0, 0.0)
    return part0, part1, jnp.where(both, right1, right0), left0


def own_gradient(flags, part0, part1, from_prev, from_next):
    both, l0, l1, r0, r1, _ = flags
    g0 = part0 + jnp.where(l0, from_prev, 0.0)
    g0 = g0 + jnp.where(jnp.logical_and(r0, jnp.logical_not(both)), from_next, 0.0)
    return g0, part1 + jnp.where(jnp.logical_and(r1, both), from_next, 0.0)


def stepped(step, params, gradient):
    transmit = jnp.tanh(params)
    return params - step * gradient * (1.0 - transmit * transmit)


def kernel_first(tb, names, marks, mp, got_a, got_b, target, weight, *rest):
    spectra, rest = Spectra(*rest[:3]), rest[3:]
    t = dict(zip(names, rest))
    part, send_a, send_b, e_ref = rest[len(names) :]
    flags = read_flags(marks, got_a.shape)
    prev, nxt = in_order(flags[5], got_b[...], got_a[...])
    tile = [jnp.tanh(v) for v in (prev, mp[0], mp[1], nxt)]
    dg = core(tb, domain_of(flags, *tile), target, weight, spectra, t, e_ref)
    part[0], part[1], to_next, to_prev = thirds(flags, dg)
    send_a[...], send_b[...] = in_order(flags[5], to_next, to_prev)


def side_gradient(flags, part, got, inward):
    even = flags[5]
    zero = jnp.zeros_like(got)
    ahead, behind = (got, zero) if inward else (zero, got)
    from_next, from_prev = jnp.where(even, ahead, behind), jnp.where(even, behind, ahead)
    return own_gradient(flags, part[0], part[1], from_prev, from_next)


def kernel_join(marks, part, third, got, out, send):
    flags = read_flags(marks, got.shape)
    both, even = flags[0], flags[5]
    rows = got.shape[0]
    g0, g1 = side_gradient(flags, part, got[...], True)
    out[0], out[1] = g0, g1
    send[:rows] = third[...]
    send[rows:] = jnp.where(jnp.logical_or(even, jnp.logical_not(both)), g0, g1)


def kernel_update(step, marks, part, params, outer, third, got, out, outer_out, send):
    flags = read_flags(marks, outer.shape)
    both, l0, l1, r0, r1, even = flags
    odd, single = jnp.logical_not(even), jnp.logical_not(both)
    rows = outer.shape[0]
    g0, g1 = side_gradient(flags, part, got[:rows], False)
    new0 = stepped(step, params[0], g0)
    new1 = jnp.where(both, stepped(step, params[1], g1), params[1])
    out[0], out[1] = new0, new1
    send[...] = jnp.where(jnp.logical_and(even, both), new1, new0)
    after = jnp.logical_or(jnp.logical_and(both, r1), jnp.logical_and(single, r0))
    linked = jnp.logical_or(jnp.logical_and(even, l0), jnp.logical_and(odd, after))
    beside = got[rows:] + jnp.where(linked, third[...], 0.0)
    outer_out[...] = stepped(step, outer[...], beside)


def kernel_second(tb, names, marks, mp, got_a, got_b, target, weight, *rest):
    spectra, rest = Spectra(*rest[:3]), rest[3:]
    t = dict(zip(names, rest))
    part, resist_out, send_a, send_b, e_ref = rest[len(names) :]
    flags = read_flags(marks, got_a.shape)
    prev, nxt = in_order(flags[5], got_b[...], got_a[...])
    tile = [jnp.tanh(v) for v in (prev, mp[0], mp[1], nxt)]
    def keep(s, resist):
        resist_out[s] = resist if s == 0 else jnp.where(flags[0], resist, 0.0)

    dg = core(tb, domain_of(flags, *tile), target, weight, spectra, t, e_ref, keep)
    part[0], part[1], to_next, to_prev = thirds(flags, dg)
    send_a[...], send_b[...] = in_order(flags[5], to_next, to_prev)


def kernel_store(image, out, sem):
    move = pltpu.make_async_copy(image, out, sem)
    move.start()
    move.wait()


def kernel_last(step, marks, part, params, got_a, got_b, out):
    flags = read_flags(marks, got_a.shape)
    prev, nxt = in_order(flags[5], got_b[...], got_a[...])
    g0, g1 = own_gradient(flags, part[0], part[1], prev, nxt)
    out[0] = stepped(step, params[0], g0)
    out[1] = jnp.where(flags[0], stepped(step, params[1], g1), params[1])


def kernel_arrange(tb, slots, kernels, weights, order, lanes, out_a, out_b, out_0, padded):
    half, nf = tb.half, tb.nf
    frows, wl = 2 * half + 8, 2 * nf
    bands = kernels.shape[1]
    kcount = out_a.shape[0]
    zb = wl // (2 * slots)
    chunk = RUN * 2 * bands
    padded[...] = jnp.zeros(padded.shape, F32)
    inner = lax.rem(lane_of((frows, wl)), zb)
    sign = jnp.where(lane_of((1, wl)) < nf, -1.0, 1.0)
    zeros = [jnp.zeros((frows, wl), F32) for _ in range(2)]
    roots = jnp.sqrt(weights[...])

    def order_rows(i):
        found = {}
        for j in range(RUN):
            ks = (i * RUN + j, (i + 1) * RUN + j)
            for n, k in enumerate(ks):
                window = pl.ds((i + n) * chunk + tb.starts[j], tb.window)
                padded[k, :, :bands] = kernels[window, :]
            high, low = split(jnp.concatenate([padded[k] for k in ks], 1))
            v = dot(order[j], jnp.concatenate([high, low], 0))
            for n, k in enumerate(ks):
                root = jnp.broadcast_to(roots[:, k : k + 1], (1, wl))
                found[k] = v[:, n * wl : (n + 1) * wl] * root
        return found

    def order_lanes(found):
        ks = sorted(found)
        high, low = split(jnp.concatenate([found[k] for k in ks], 0))
        v = dot(jnp.concatenate([high, low], 1), lanes[...])
        for n, k in enumerate(ks):
            real = v[2 * n * frows : (2 * n + 1) * frows]
            imag = v[(2 * n + 1) * frows : (2 * n + 2) * frows]
            out_a[k] = real[:, :wl]
            out_b[k] = imag[:, :wl] * sign
            zeros[0] = jnp.where(inner == k, real[:, wl:], zeros[0])
            zeros[1] = jnp.where(inner == k, imag[:, wl:], zeros[1])

    waiting = None
    for i in range(0, kcount // RUN, 2):
        found = order_rows(i)
        if waiting is not None:
            order_lanes(waiting)
        waiting = found
    order_lanes(waiting)
    out_0[0] = zeros[0]
    out_0[1] = -conj(zeros[1], zb)


def arrange(tb, slots, parts, ins):
    bands, kcount = ins[0].shape[1], ins[1].shape[1]
    frows, wl = 2 * tb.half + 8, 2 * tb.nf
    return call(
        functools.partial(kernel_arrange, tb, slots),
        list(ins),
        [(kcount, frows, wl)] * 2 + [(2, frows, wl)],
        [pltpu.VMEM((kcount, parts * frows, wl), F32)],
    )


def kernel_choose(ids, links, params, *refs):
    count = (len(refs) - 7) // 2
    far, (marks, send_a, send_b) = refs[:count], refs[count : count + 3]
    near, (ids_s, links_s, params_v, sems) = refs[count + 3 : 2 * count + 3], refs[2 * count + 3 :]
    pairs = [(ids, ids_s), (links, links_s), (params, params_v), *zip(far, near)]
    moves = [pltpu.make_async_copy(*pair, sems.at[i]) for i, pair in enumerate(pairs)]
    for move in moves:
        move.start()
    for move in moves[:3]:
        move.wait()
    both = ids_s[1] >= 0
    even = lax.rem(lax.axis_index("tile"), 2) == 0
    last = jnp.where(both, params_v[1], params_v[0])
    send_a[...], send_b[...] = in_order(even, last, params_v[0])
    flags = [both] + [links_s[s, side] == 1 for side in range(2) for s in range(2)] + [even]
    row = lax.broadcasted_iota(jnp.int32, marks.shape, 0)
    out = jnp.zeros(marks.shape, F32)
    for i, flag in enumerate(flags):
        out = jnp.where(row == i, jnp.where(flag, 1.0, 0.0), out)
    marks[...] = out
    for move in moves[3:]:
        move.wait()


def choose(tile_ids, tile_links, mask_params, far):
    tile = mask_params.shape[1:]
    ins = (tile_ids, tile_links, mask_params, *far)
    shapes = [jax.ShapeDtypeStruct(s, F32) for s in ((8, tile[1]), tile, tile)]
    shapes += [jax.ShapeDtypeStruct(v.shape, v.dtype) for v in far]
    return pl.pallas_call(
        kernel_choose,
        in_specs=[pl.BlockSpec(memory_space=pltpu.HBM)] * len(ins),
        out_specs=[pl.BlockSpec(memory_space=pltpu.VMEM)] * len(shapes),
        out_shape=shapes,
        scratch_shapes=[
            pltpu.SMEM(tile_ids.shape, jnp.int32),
            pltpu.SMEM(tile_links.shape, jnp.int32),
            pltpu.VMEM(mask_params.shape, F32),
            pltpu.SemaphoreType.DMA((len(ins),)),
        ],
        compiler_params=pltpu.CompilerParams(vmem_limit_bytes=8 << 20),
    )(*(pltpu.with_memory_space_constraint(v, pltpu.HBM) for v in ins))


def call(body, ins, outs, scratch=(), limit=32 << 20, moved=()):
    vmem = pl.BlockSpec(memory_space=pltpu.VMEM)
    return pl.pallas_call(
        body,
        in_specs=[vmem] * len(ins),
        out_specs=[
            pl.BlockSpec(memory_space=pltpu.HBM) if i in moved else vmem for i in range(len(outs))
        ],
        out_shape=[jax.ShapeDtypeStruct(s, F32) for s in outs],
        scratch_shapes=list(scratch),
        compiler_params=pltpu.CompilerParams(vmem_limit_bytes=limit),
    )(*ins)


def local(mesh_shape, mask_params, target, weight, kernels, kernel_weight, tile_ids, tile_links):
    slots, rows, cols = mask_params.shape
    bands = kernels.shape[2]
    kcount = kernels.shape[0]
    groups, count = mesh_shape
    step = STEP_SCALE * math.sqrt(rows * cols)
    tb = Tables(rows, cols, bands)
    names = tuple(tb.arrays)
    tables = [jnp.asarray(tb.arrays[n]) for n in names]
    axes = ("grp", "tile")

    inner = swap_pairs(groups, count, 0)
    outer = swap_pairs(groups, count, 1)

    def swap_inner(v):
        return lax.ppermute(v, axes, inner)

    def swap_outer(v):
        return lax.ppermute(v, axes, outer)

    def exchange(a, b):
        return swap_inner(a), swap_outer(b)

    whole, tile = mask_params.shape, (rows, cols)

    flat = jnp.swapaxes(kernels, 1, 2).reshape(-1, bands)
    far = (flat, kernel_weight[None], jnp.asarray(tb.order), jnp.asarray(tb.lanes))
    marks, sa, sb, *near = choose(tile_ids, tile_links, mask_params, far)
    got = exchange(sa, sb)
    arranged = arrange(tb, slots, kernels.shape[1], near)
    field = pltpu.VMEM((slots, kcount, rows, 2 * cols), F32)
    part, sa, sb = call(
        functools.partial(kernel_first, tb, names),
        [marks, mask_params, *got, target, weight, *arranged, *tables],
        [whole, tile, tile],
        [field],
    )
    part, both_sent = call(
        kernel_join, [marks, part, sb, swap_inner(sa)], [whole, (2 * rows, cols)]
    )
    params, outer_tile, sa = call(
        functools.partial(kernel_update, step),
        [marks, part, mask_params, got[1], sb, swap_outer(both_sent)],
        [whole, tile, tile],
    )
    part, resist, sa, sb = call(
        functools.partial(kernel_second, tb, names),
        [marks, params, swap_inner(sa), outer_tile, target, weight, *arranged, *tables],
        [whole, whole, tile, tile],
        [field],
    )
    got = exchange(sa, sb)
    (resist,) = call(kernel_store, [resist], [whole], [pltpu.SemaphoreType.DMA], moved=(0,))
    (out,) = call(
        functools.partial(kernel_last, step),
        [marks, part, params, *got],
        [whole],
    )
    return (out, resist)


def solution(mesh):
    tiles = P(("grp", "tile"), None, None)
    return jax.shard_map(
        functools.partial(local, (mesh.shape["grp"], mesh.shape["tile"])),
        mesh=mesh,
        in_specs=(tiles, tiles, tiles, P(), P(), P(("grp", "tile")), P(("grp", "tile"), None)),
        out_specs=(tiles, tiles),
        check_vma=False,
    )
```

```python
import functools
import math

import jax
import jax.numpy as jnp
import numpy as np
from jax import lax
from jax.experimental import pallas as pl
from jax.experimental.pallas import tpu as pltpu
from jax.sharding import PartitionSpec as P

ITERS = 2
RESIST_SLOPE = 4.0
THRESHOLD = 0.9
STEP_SCALE = 0.04
GROUP = 8
RUN = 4
MID = 16
F32 = jnp.float32
BF16 = jnp.bfloat16


def swap_pairs(groups, count, first):
    pairs = []
    for g in range(groups):
        for i in range(count):
            j = i + 1 if (i - first) % 2 == 0 else i - 1
            other = g
            if not 0 <= j < count:
                j, other = i, g ^ 1 if groups % 2 == 0 else g
            pairs.append((g * count + i, other * count + j))
    return pairs


def split_np(table):
    table = np.asarray(table, np.float32)
    high = table.astype(jnp.bfloat16)
    low = (table - high.astype(np.float32)).astype(jnp.bfloat16)
    return high, low


class Tables:
    def __init__(self, rows, cols, bands):
        half = (bands - 1) // 2
        self.half = half
        area = 1.0 / (rows * cols)
        self.area = area
        pos = np.arange(1, half + 1)
        angle = (np.arange(rows)[:, None] * pos[None, :] % (2 * rows)) * (np.pi / rows)
        ty = np.zeros((rows, 2 * half + MID))
        ty[:, :half] = np.cos(angle)
        ty[:, half] = 1.0
        ty[:, half + MID :] = np.sin(angle)
        freq = np.concatenate([np.arange(-half, 0), np.arange(1, half + 1)])
        self.nf = len(freq)
        period = 3 * cols
        theta = (np.arange(period)[:, None] * freq[None, :] % period) * (2.0 * np.pi / period)
        c, s = np.cos(theta), np.sin(theta)
        co, so = c[cols : 2 * cols].T, s[cols : 2 * cols].T
        forward = np.block([[co, so], [-so, co]])
        adjoint = np.block([[co.T, so.T], [so.T, -co.T]])
        gradient = np.concatenate([c.T, s.T], 0) * (2.0 * area)
        spectrum = np.concatenate([c, -s], 1) * area

        def left(table):
            h, l = split_np(table)
            return np.concatenate([h, h, l], 1)

        def right(table):
            h, l = split_np(table)
            return np.concatenate([h, h, l], 0)

        part = np.arange(2 * self.nf) // (self.nf // 2) % 2
        ones = np.zeros((2 * self.nf, 2 * cols))
        ones[part == 0, :cols] = 1.0
        ones[part == 1, cols:] = 1.0
        sums = np.concatenate([ones.T, ones.T, np.zeros_like(ones.T)], 0).astype(jnp.bfloat16)
        sums[cols : 2 * cols] *= -1
        sums[3 * cols : 4 * cols] *= -1
        picks = np.zeros((self.nf // 2, MID, 2 * self.nf), jnp.bfloat16)
        for k in range(self.nf // 2):
            picks[k, :, k :: self.nf // 2] = 1.0

        def wide(table):
            h, l = split_np(table)
            top = np.concatenate([h, l], 1)
            return np.concatenate([top, np.concatenate([h, np.zeros_like(l)], 1)], 0)

        self.arrays = dict(
            ty=left(ty),
            tyt=left(ty.T),
            fwd=np.concatenate([right(forward), ones.astype(jnp.bfloat16)], 0),
            picks=picks,
            adj=wide(adjoint),
            grad=right(gradient),
            spec=np.stack([wide(spectrum[j * cols : (j + 1) * cols]) for j in range(3)]),
        )
        chunk = RUN * 2 * bands
        frows = 2 * half + 8
        self.window = 2 * frows
        order = np.zeros((RUN, 2 * frows, self.window), jnp.bfloat16)
        self.starts = []
        for j in range(RUN):
            start = min(2 * bands * j // 8 * 8, chunk - self.window)
            self.starts.append(start)
            for part in range(2):
                first = 2 * bands * j - start + part
                base = part * frows
                for f in range(half):
                    order[j, base + f, first + 2 * (half + 1 + f)] = 1.0
                    order[j, base + half + 8 + f, first + 2 * (half - 1 - f)] = 1.0
                order[j, base + half, first + 2 * half] = 1.0
        self.order = np.concatenate([order, order], 2)
        lanes = np.zeros((2 * self.nf, 4 * self.nf), jnp.bfloat16)
        for j, g in enumerate([*range(half), *range(half + 1, bands)]):
            lanes[g, j] = lanes[g, self.nf + j] = 1.0
        lanes[half, 2 * self.nf :] = 1.0
        self.lanes = np.concatenate([lanes, lanes], 0)


def split(v):
    high = v.astype(BF16)
    return high, (v - high.astype(F32)).astype(BF16)


def dot(a, b):
    return jnp.dot(a, b, preferred_element_type=F32)


def lanes3(v):
    high, low = split(v)
    return jnp.concatenate([high, low, high], 1)


def rows3(v):
    high, low = split(v)
    return jnp.concatenate([high, low, high], 0)


def wide_dot(v, table):
    high, low = split(v)
    o = dot(jnp.concatenate([high, low], 1), table)
    n = o.shape[1] // 2
    return o[:, :n] + o[:, n:]


def lane_of(shape):
    return lax.broadcasted_iota(jnp.int32, shape, 1)


def swap(v, block):
    n = v.shape[1]
    if 2 * block == n:
        return pltpu.roll(v, block, 1)
    even = lax.rem(lax.div(lane_of(v.shape), block), 2) == 0
    return jnp.where(even, pltpu.roll(v, n - block, 1), pltpu.roll(v, block, 1))


def conj(v, block):
    even = lax.rem(lax.div(lane_of((1, v.shape[1])), block), 2) == 0
    return v * jnp.where(even, 1.0, -1.0)


def minus_i(v, block):
    return conj(swap(v, block), block)


def fold(half, plus, zero, minus):
    gap = jnp.zeros((MID - 8, plus.shape[1]), F32)
    return jnp.concatenate([plus, zero, gap, minus], 0)


def drive(half, a, b, u):
    p, m = slice(0, half), slice(half + 8, 2 * half + 8)
    d = a * u[0] + b * u[1]
    turned_p = a[p] * u[2][p] + b[p] * u[3][p]
    turned_m = a[m] * u[2][m] + b[m] * u[3][m]
    return fold(half, d[p] + d[m], d[half : half + 8], turned_p - turned_m)


def phases(half, o, block):
    cosine, zero, sine = o[:half], o[half : half + 8], o[half + MID :]
    turned = conj(swap(sine, block), block)
    u = jnp.concatenate([cosine + turned, zero, cosine - turned], 0)
    other, back = swap(o[: half + 8], block), conj(sine, block)
    v = jnp.concatenate([other[:half] - back, other[half:], other[:half] + back], 0)
    return u, v, -conj(v, block), conj(u, block)


def gather(half, q, a, b, o, block):
    p, z, m = slice(0, half), slice(half, half + 8), slice(half + 8, 2 * half + 8)
    c, zero, s = o[:half], o[half : half + 8], conj(o[half + MID :], block)
    parts = [
        a[p] * c + b[p] * s,
        a[z] * zero,
        a[m] * c - b[m] * s,
        b[p] * c - a[p] * s,
        b[z] * zero,
        b[m] * c + a[m] * s,
    ]
    return parts if q is None else [x + y for x, y in zip(q, parts)]


def back_rows(half, q, block):
    plus = q[0] + q[2] - swap(q[3] + q[5], block)
    zero = q[1] - swap(q[4], block)
    turned = conj(swap(q[0] - q[2], block) - (q[3] - q[5]), block)
    return fold(half, plus, zero, turned)


def lane_sum(v):
    return jnp.sum(v, axis=1, keepdims=True)


class Spectra:
    def __init__(self, real, imag, at_zero):
        self.real, self.imag, self.zero = real, imag, at_zero
        self.count = real.shape[0]

    def __getitem__(self, k):
        return self.real[k], self.imag[k]

    def at_zero(self):
        return self.zero[0], self.zero[1]


def core(tb, dom, target, weight, spectra, t, e_ref, keep=None):
    half, nf = tb.half, tb.nf
    slots, rows, cols = target.shape
    kcount = spectra.count
    wl = 2 * nf
    zb = wl // (2 * slots)
    ty, tyt = t["ty"], t["tyt"]
    thirds_of = [dom[:, j * cols : (j + 1) * cols] for j in range(3)]
    g = sum(wide_dot(v, t["spec"][j]) for j, v in enumerate(thirds_of))
    gw = jnp.concatenate([g[s * rows : (s + 1) * rows] for s in range(slots)], 1)
    spec = dot(tyt[...], rows3(gw))
    us = [phases(half, spec[:, s * wl : (s + 1) * wl], nf) for s in range(slots)]
    g0 = lane_sum(thirds_of[0] + thirds_of[1] + thirds_of[2]) * tb.area
    block = lax.div(lane_of((rows, wl)), zb)
    g0w = jnp.zeros((rows, wl), F32)
    for s in range(slots):
        g0w = jnp.where(block == 2 * s, g0[s * rows : (s + 1) * rows], g0w)
    u0 = phases(half, dot(tyt[...], rows3(g0w)), zb)
    a0, b0 = spectra.at_zero()
    r0 = dot(ty[...], rows3(drive(half, a0, b0, u0)))
    r0h, r0l = split(r0)
    r0l = pltpu.roll(r0l.astype(F32), wl // 2, 1)
    r0s = [
        jnp.where(lax.div(block, 2) == s, r0h.astype(F32), r0l).astype(BF16) for s in range(slots)
    ]
    inner = lax.rem(lane_of((rows, wl)), zb)
    groups = [range(k0, min(k0 + GROUP, kcount)) for k0 in range(0, kcount, GROUP)]

    def in_pairs(ks):
        return [ks[i : i + 2] for i in range(0, len(ks), 2)]

    def row_stage(s, ks):
        out, extra = [], []
        for pair in in_pairs(ks):
            w = jnp.concatenate([drive(half, *spectra[k], us[s]) for k in pair], 1)
            r = dot(ty[...], rows3(w))
            for n, k in enumerate(pair):
                out.append(r[:, n * wl : (n + 1) * wl])
                extra += [r0s[s][i : i + MID] * t["picks"][k] for i in range(0, rows, MID)]
        return jnp.concatenate([lanes3(jnp.concatenate(out, 0)), jnp.concatenate(extra, 0)], 1)

    def field_stage(s, ks, ready, inten):
        field = dot(ready, t["fwd"][...])
        for n, k in enumerate(ks):
            e = field[n * rows : (n + 1) * rows]
            e_ref[s, k] = e
            inten = inten + (e[:, :cols] * e[:, :cols] + e[:, cols:] * e[:, cols:])
        return inten

    def slope_of(s, inten):
        resist = jax.nn.sigmoid(RESIST_SLOPE * (inten - THRESHOLD))
        slope = 2.0 * weight[s] * (resist - target[s]) * RESIST_SLOPE * resist * (1.0 - resist)
        return resist, jnp.concatenate([slope, slope], 1)

    def column_stage(s, ks, slope2):
        back = [e_ref[s, k] * slope2 for k in ks]
        flat = [(lane_sum(v[:, :cols]), -lane_sum(v[:, cols:])) for v in back]
        return wide_dot(jnp.concatenate(back, 0), t["adj"][...]), flat

    def sum_stage(s, ks, ready, c0, q):
        for m, pair in enumerate(in_pairs(ks)):
            parts = [
                ready[0][(2 * m + n) * rows : (2 * m + n + 1) * rows] for n in range(len(pair))
            ]
            o = dot(tyt[...], rows3(jnp.concatenate([v[:, :wl] for v in parts], 1)))
            for n, k in enumerate(pair):
                zr, zi = ready[1][2 * m + n]
                c0 = jnp.where(inner == k, jnp.where(lax.rem(block, 2) == 0, zr, zi), c0)
                q = gather(half, q, *spectra[k], o[:, n * wl : (n + 1) * wl], nf)
        return c0, q

    def finish(s, c0, q):
        own = lax.div(block, 2) == s
        q0 = gather(half, None, a0, b0, dot(tyt[...], rows3(jnp.where(own, c0, 0.0))), zb)
        ug = dot(ty[...], rows3(back_rows(half, q, nf)))
        ug0 = dot(ty[...], rows3(back_rows(half, q0, zb)))
        flat = lane_sum(jnp.where(block == 2 * s, ug0, 0.0))
        return dot(lanes3(ug), t["grad"][...]) + (2.0 * tb.area) * flat

    grads = []
    slope2 = None
    for s in range(slots + 1):
        forward, backward = s < slots, s > 0
        inten = jnp.zeros((rows, cols), F32)
        c0, q = jnp.zeros((rows, wl), F32), None
        ahead_f = row_stage(s, groups[0]) if forward else None
        ahead_b = column_stage(s - 1, groups[0], slope2) if backward else None
        for j, ks in enumerate(groups):
            now_f, now_b = ahead_f, ahead_b
            more = j + 1 < len(groups)
            if forward and more:
                ahead_f = row_stage(s, groups[j + 1])
            if backward and more:
                ahead_b = column_stage(s - 1, groups[j + 1], slope2)
            if forward:
                inten = field_stage(s, ks, now_f, inten)
            if backward:
                c0, q = sum_stage(s - 1, ks, now_b, c0, q)
        if backward:
            grads.append(finish(s - 1, c0, q))
        if forward:
            resist, slope2 = slope_of(s, inten)
            if keep is not None:
                keep(s, resist)
    return grads


def read_flags(flags, shape):
    return tuple(jnp.broadcast_to(flags[i : i + 1], shape) > 0.5 for i in range(6))


def in_order(even, first, second):
    return jnp.where(even, first, second), jnp.where(even, second, first)


def domain_of(flags, prev, own0, own1, nxt):
    both, l0, l1, r0, r1, _ = flags
    zero = jnp.zeros_like(own0)
    first = [jnp.where(l0, prev, zero), own0, jnp.where(r0, jnp.where(both, own1, nxt), zero)]
    second = [jnp.where(l1, own0, zero), own1, jnp.where(r1, nxt, zero)]
    return jnp.concatenate([jnp.concatenate(first, 1), jnp.concatenate(second, 1)], 0)


def thirds(flags, dg):
    both, l0, l1, r0, r1, _ = flags
    cols = dg[0].shape[1] // 3
    left0, mid0, right0 = (dg[0][:, j * cols : (j + 1) * cols] for j in range(3))
    left1, mid1, right1 = (dg[1][:, j * cols : (j + 1) * cols] for j in range(3))
    part0 = mid0 + jnp.where(jnp.logical_and(r0, both), left1, 0.0)
    part1 = mid1 + jnp.where(l1, right0, 0.0)
    return part0, part1, jnp.where(both, right1, right0), left0


def own_gradient(flags, part0, part1, from_prev, from_next):
    both, l0, l1, r0, r1, _ = flags
    g0 = part0 + jnp.where(l0, from_prev, 0.0)
    g0 = g0 + jnp.where(jnp.logical_and(r0, jnp.logical_not(both)), from_next, 0.0)
    return g0, part1 + jnp.where(jnp.logical_and(r1, both), from_next, 0.0)


def stepped(step, params, gradient):
    transmit = jnp.tanh(params)
    return params - step * gradient * (1.0 - transmit * transmit)


def kernel_first(tb, names, marks, mp, got_a, got_b, target, weight, *rest):
    spectra, rest = Spectra(*rest[:3]), rest[3:]
    t = dict(zip(names, rest))
    part, send_a, send_b, e_ref = rest[len(names) :]
    flags = read_flags(marks, got_a.shape)
    prev, nxt = in_order(flags[5], got_b[...], got_a[...])
    tile = [jnp.tanh(v) for v in (prev, mp[0], mp[1], nxt)]
    dg = core(tb, domain_of(flags, *tile), target, weight, spectra, t, e_ref)
    part[0], part[1], to_next, to_prev = thirds(flags, dg)
    send_a[...], send_b[...] = in_order(flags[5], to_next, to_prev)


def side_gradient(flags, part, got, inward):
    even = flags[5]
    zero = jnp.zeros_like(got)
    ahead, behind = (got, zero) if inward else (zero, got)
    from_next, from_prev = jnp.where(even, ahead, behind), jnp.where(even, behind, ahead)
    return own_gradient(flags, part[0], part[1], from_prev, from_next)


def kernel_join(marks, part, third, got, out, send):
    flags = read_flags(marks, got.shape)
    both, even = flags[0], flags[5]
    rows = got.shape[0]
    g0, g1 = side_gradient(flags, part, got[...], True)
    out[0], out[1] = g0, g1
    send[:rows] = third[...]
    send[rows:] = jnp.where(jnp.logical_or(even, jnp.logical_not(both)), g0, g1)


def kernel_update(step, marks, part, params, outer, third, got, out, outer_out, send):
    flags = read_flags(marks, outer.shape)
    both, l0, l1, r0, r1, even = flags
    odd, single = jnp.logical_not(even), jnp.logical_not(both)
    rows = outer.shape[0]
    g0, g1 = side_gradient(flags, part, got[:rows], False)
    new0 = stepped(step, params[0], g0)
    new1 = jnp.where(both, stepped(step, params[1], g1), params[1])
    out[0], out[1] = new0, new1
    send[...] = jnp.where(jnp.logical_and(even, both), new1, new0)
    after = jnp.logical_or(jnp.logical_and(both, r1), jnp.logical_and(single, r0))
    linked = jnp.logical_or(jnp.logical_and(even, l0), jnp.logical_and(odd, after))
    beside = got[rows:] + jnp.where(linked, third[...], 0.0)
    outer_out[...] = stepped(step, outer[...], beside)


def kernel_second(tb, names, marks, mp, got_a, got_b, target, weight, *rest):
    spectra, rest = Spectra(*rest[:3]), rest[3:]
    t = dict(zip(names, rest))
    part, resist_out, send_a, send_b, e_ref = rest[len(names) :]
    flags = read_flags(marks, got_a.shape)
    prev, nxt = in_order(flags[5], got_b[...], got_a[...])
    tile = [jnp.tanh(v) for v in (prev, mp[0], mp[1], nxt)]
    def keep(s, resist):
        resist_out[s] = resist if s == 0 else jnp.where(flags[0], resist, 0.0)

    dg = core(tb, domain_of(flags, *tile), target, weight, spectra, t, e_ref, keep)
    part[0], part[1], to_next, to_prev = thirds(flags, dg)
    send_a[...], send_b[...] = in_order(flags[5], to_next, to_prev)


def kernel_store(image, out, sem):
    move = pltpu.make_async_copy(image, out, sem)
    move.start()
    move.wait()


def kernel_last(step, marks, part, params, got_a, got_b, out):
    flags = read_flags(marks, got_a.shape)
    prev, nxt = in_order(flags[5], got_b[...], got_a[...])
    g0, g1 = own_gradient(flags, part[0], part[1], prev, nxt)
    out[0] = stepped(step, params[0], g0)
    out[1] = jnp.where(flags[0], stepped(step, params[1], g1), params[1])


def kernel_arrange(tb, slots, kernels, *refs):
    small_far, (out_a, out_b, out_0), small = refs[:3], refs[3:6], refs[6:9]
    raw, padded, sems, small_sems = refs[9:]
    half, nf = tb.half, tb.nf
    frows, wl = 2 * half + 8, 2 * nf
    bands = kernels.shape[1]
    kcount = out_a.shape[0]
    zb = wl // (2 * slots)
    chunk = RUN * 2 * bands
    first_moves = [
        pltpu.make_async_copy(small_far[i], small[i], small_sems.at[i]) for i in range(3)
    ]
    moves = []
    for i in range(kcount // RUN):
        part = pl.ds(i * chunk, chunk)
        moves.append(pltpu.make_async_copy(kernels.at[part], raw.at[part], sems.at[i]))
    for move in moves[:2] + first_moves + moves[2:]:
        move.start()
    padded[...] = jnp.zeros(padded.shape, F32)
    weights, order, lanes = small
    inner = lax.rem(lane_of((frows, wl)), zb)
    sign = jnp.where(lane_of((1, wl)) < nf, -1.0, 1.0)
    zeros = [jnp.zeros((frows, wl), F32) for _ in range(2)]
    for move in first_moves:
        move.wait()
    roots = jnp.sqrt(weights[...])

    def order_rows(i):
        found = {}
        for j in range(RUN):
            ks = (i * RUN + j, (i + 1) * RUN + j)
            for n, k in enumerate(ks):
                window = pl.ds((i + n) * chunk + tb.starts[j], tb.window)
                padded[k, :, :bands] = raw[window, :]
            high, low = split(jnp.concatenate([padded[k] for k in ks], 1))
            v = dot(order[j], jnp.concatenate([high, low], 0))
            for n, k in enumerate(ks):
                root = jnp.broadcast_to(roots[:, k : k + 1], (1, wl))
                found[k] = v[:, n * wl : (n + 1) * wl] * root
        return found

    def order_lanes(found):
        ks = sorted(found)
        high, low = split(jnp.concatenate([found[k] for k in ks], 0))
        v = dot(jnp.concatenate([high, low], 1), lanes[...])
        for n, k in enumerate(ks):
            real = v[2 * n * frows : (2 * n + 1) * frows]
            imag = v[(2 * n + 1) * frows : (2 * n + 2) * frows]
            out_a[k] = real[:, :wl]
            out_b[k] = imag[:, :wl] * sign
            zeros[0] = jnp.where(inner == k, real[:, wl:], zeros[0])
            zeros[1] = jnp.where(inner == k, imag[:, wl:], zeros[1])

    waiting = None
    for i in range(0, kcount // RUN, 2):
        moves[i].wait()
        moves[i + 1].wait()
        found = order_rows(i)
        if waiting is not None:
            order_lanes(waiting)
        waiting = found
    order_lanes(waiting)
    out_0[0] = zeros[0]
    out_0[1] = -conj(zeros[1], zb)


def arrange(tb, slots, kernels, kernel_weight):
    kcount, parts, bands = kernels.shape[:3]
    frows, wl = 2 * tb.half + 8, 2 * tb.nf
    flat = jnp.swapaxes(kernels, 1, 2).reshape(kcount * bands * parts, bands)
    shapes = [(kcount, frows, wl)] * 2 + [(2, frows, wl)]
    ins = [flat, kernel_weight[None], jnp.asarray(tb.order), jnp.asarray(tb.lanes)]
    return pl.pallas_call(
        functools.partial(kernel_arrange, tb, slots),
        in_specs=[pl.BlockSpec(memory_space=pltpu.HBM)] * 4,
        out_specs=[pl.BlockSpec(memory_space=pltpu.VMEM)] * 3,
        out_shape=[jax.ShapeDtypeStruct(shape, F32) for shape in shapes],
        scratch_shapes=[pltpu.VMEM(v.shape, v.dtype) for v in ins[1:]]
        + [
            pltpu.VMEM(flat.shape, F32),
            pltpu.VMEM((kcount, parts * frows, wl), F32),
            pltpu.SemaphoreType.DMA((kcount // RUN,)),
            pltpu.SemaphoreType.DMA((3,)),
        ],
        compiler_params=pltpu.CompilerParams(vmem_limit_bytes=24 << 20),
    )(*(pltpu.with_memory_space_constraint(v, pltpu.HBM) for v in ins))


def kernel_choose(ids, links, params, marks, send_a, send_b, ids_s, links_s, params_v, sems):
    moves = [
        pltpu.make_async_copy(source, target, sems.at[i])
        for i, (source, target) in enumerate(((ids, ids_s), (links, links_s), (params, params_v)))
    ]
    for move in moves:
        move.start()
    for move in moves:
        move.wait()
    both = ids_s[1] >= 0
    even = lax.rem(lax.axis_index("tile"), 2) == 0
    last = jnp.where(both, params_v[1], params_v[0])
    send_a[...], send_b[...] = in_order(even, last, params_v[0])
    flags = [both] + [links_s[s, side] == 1 for side in range(2) for s in range(2)] + [even]
    row = lax.broadcasted_iota(jnp.int32, marks.shape, 0)
    out = jnp.zeros(marks.shape, F32)
    for i, flag in enumerate(flags):
        out = jnp.where(row == i, jnp.where(flag, 1.0, 0.0), out)
    marks[...] = out


def choose(*ins):
    tile_ids, tile_links, mask_params = ins
    tile = mask_params.shape[1:]
    far = pl.BlockSpec(memory_space=pltpu.HBM)
    return pl.pallas_call(
        kernel_choose,
        in_specs=[far] * 3,
        out_specs=[pl.BlockSpec(memory_space=pltpu.VMEM)] * 3,
        out_shape=[jax.ShapeDtypeStruct(s, F32) for s in ((8, tile[1]), tile, tile)],
        scratch_shapes=[
            pltpu.SMEM(tile_ids.shape, jnp.int32),
            pltpu.SMEM(tile_links.shape, jnp.int32),
            pltpu.VMEM(mask_params.shape, F32),
            pltpu.SemaphoreType.DMA((3,)),
        ],
        compiler_params=pltpu.CompilerParams(vmem_limit_bytes=4 << 20),
    )(*(pltpu.with_memory_space_constraint(v, pltpu.HBM) for v in ins))


def call(body, ins, outs, scratch=(), limit=32 << 20, moved=()):
    vmem = pl.BlockSpec(memory_space=pltpu.VMEM)
    return pl.pallas_call(
        body,
        in_specs=[vmem] * len(ins),
        out_specs=[
            pl.BlockSpec(memory_space=pltpu.HBM) if i in moved else vmem for i in range(len(outs))
        ],
        out_shape=[jax.ShapeDtypeStruct(s, F32) for s in outs],
        scratch_shapes=list(scratch),
        compiler_params=pltpu.CompilerParams(vmem_limit_bytes=limit),
    )(*ins)


def local(mesh_shape, mask_params, target, weight, kernels, kernel_weight, tile_ids, tile_links):
    slots, rows, cols = mask_params.shape
    bands = kernels.shape[2]
    kcount = kernels.shape[0]
    groups, count = mesh_shape
    step = STEP_SCALE * math.sqrt(rows * cols)
    tb = Tables(rows, cols, bands)
    names = tuple(tb.arrays)
    tables = [jnp.asarray(tb.arrays[n]) for n in names]
    axes = ("grp", "tile")

    inner = swap_pairs(groups, count, 0)
    outer = swap_pairs(groups, count, 1)

    def swap_inner(v):
        return lax.ppermute(v, axes, inner)

    def swap_outer(v):
        return lax.ppermute(v, axes, outer)

    def exchange(a, b):
        return swap_inner(a), swap_outer(b)

    whole, tile = mask_params.shape, (rows, cols)

    marks, sa, sb = choose(tile_ids, tile_links, mask_params)
    got = exchange(sa, sb)
    arranged = arrange(tb, slots, kernels, kernel_weight)
    field = pltpu.VMEM((slots, kcount, rows, 2 * cols), F32)
    part, sa, sb = call(
        functools.partial(kernel_first, tb, names),
        [marks, mask_params, *got, target, weight, *arranged, *tables],
        [whole, tile, tile],
        [field],
    )
    part, both_sent = call(
        kernel_join, [marks, part, sb, swap_inner(sa)], [whole, (2 * rows, cols)]
    )
    params, outer_tile, sa = call(
        functools.partial(kernel_update, step),
        [marks, part, mask_params, got[1], sb, swap_outer(both_sent)],
        [whole, tile, tile],
    )
    part, resist, sa, sb = call(
        functools.partial(kernel_second, tb, names),
        [marks, params, swap_inner(sa), outer_tile, target, weight, *arranged, *tables],
        [whole, whole, tile, tile],
        [field],
    )
    got = exchange(sa, sb)
    (resist,) = call(kernel_store, [resist], [whole], [pltpu.SemaphoreType.DMA], moved=(0,))
    (out,) = call(
        functools.partial(kernel_last, step),
        [marks, part, params, *got],
        [whole],
    )
    return (out, resist)


def solution(mesh):
    tiles = P(("grp", "tile"), None, None)
    return jax.shard_map(
        functools.partial(local, (mesh.shape["grp"], mesh.shape["tile"])),
        mesh=mesh,
        in_specs=(tiles, tiles, tiles, P(), P(), P(("grp", "tile")), P(("grp", "tile"), None)),
        out_specs=(tiles, tiles),
        check_vma=False,
    )
```
